128 devices in a mesh: dp: 32 (over x, y, core), tensor: 4 (over z).
Axes of the slice: x: 4, y: 4, z: 4, core: 2. Of those that a mesh axis runs over, the one named last changes fastest.
Arguments:
- memory: bfloat16 [49152, 1280], P('dp'), may hold values from -6 to 6
- hidden: bfloat16 [49152, 2560], P('dp', 'tensor'), may hold values from -6 to 6
- grad_out: bfloat16 [49152, 2560], P('dp', 'tensor'), may hold values from -6 to 6
- key_weight: bfloat16 [1280, 2560], P('dp', 'tensor'), may hold values from -0.15625 to 0.15625
- value_weight: bfloat16 [1280, 2560], P('dp', 'tensor'), may hold values from -0.15625 to 0.15625
- row_ids: int32 [49152, 5], P('dp'), may hold values from 0 to 262143, as said below
- embed_table: float32 [262144, 256], P(('dp', 'tensor')), may hold values from -6 to 6
- first_moment: float32 [262144, 256], P(('dp', 'tensor')), may hold values from -0.6 to 0.6
- second_moment: float32 [262144, 256], P(('dp', 'tensor')), may hold values from 0.001 to 0.1
Outputs:
- key_weight_grad: float32 [1280, 2560], P('dp', 'tensor')
- value_weight_grad: float32 [1280, 2560], P('dp', 'tensor')
- new_table: float32 [262144, 256], P(('dp', 'tensor'))
- new_first: float32 [262144, 256], P(('dp', 'tensor'))
- new_second: float32 [262144, 256], P(('dp', 'tensor'))
The draws below stay inside these ranges and needn't reach their ends.
Inputs may be any that keep to these rules, and one draw needn't show every extreme that they name: `row_ids`: the table's rows fall into 128 owners of 2048 consecutive rows each. Taking the tokens in aligned blocks of 384 consecutive tokens with all their 5 ids, at most 45 ids of one block fall in one owner's rows, and in every block some owner gets exactly 45 of them.
All inputs are finite; a program needn't handle non-finite values.
Results may differ from the reference program's by a relative error of at most 0.0043.
Values may be sent and summed in bfloat16 or wider, within the bound.
No kernel may reach another device: no remote copies, remote signals or barrier semaphores. Data moves between devices by JAX's collectives and lax.ppermute only.
A program may use at most 128 MiB of HBM per device.

```python
import math
import jax
import jax.numpy as jnp
from jax import lax

D = 2560
ROW_W = 256
LOOKUPS = 5
MEM = 1280
ROWS_DEV = 2048
BLOCK = 384
CAP = 45
TOKENS = 49152
ROWS = 262144
DEVICES = 128


def block_ids(block_key):
    entries = BLOCK * LOOKUPS
    owners = DEVICES
    slots = owners * CAP
    keys = jax.random.split(block_key, 5)
    loads = jax.random.randint(keys[0], (owners,), 1, CAP + 1)
    hottest = jax.random.randint(keys[1], (), 0, owners)
    slot_index = jnp.arange(slots, dtype=jnp.int32)
    slot_owner = slot_index // CAP
    slot_copy = slot_index % CAP
    tier = jnp.where(slot_owner == hottest, 2, jnp.where(slot_copy < loads[slot_owner], 1, 0))
    noise = jax.random.randint(keys[2], (slots,), 0, 2048)
    score = tier * 16777216 + noise * 8192 + slot_index
    chosen = lax.top_k(score, entries)[1]
    owner_of = jax.random.permutation(keys[3], chosen // CAP)
    local_row = jax.random.randint(keys[4], (entries,), 0, ROWS_DEV)
    return (owner_of * ROWS_DEV + local_row).astype(jnp.int32)


def draw_row_ids(key, part):
    count = TOKENS // BLOCK
    keys = jax.random.split(jax.random.fold_in(key, 7), count)
    table_ids = jax.vmap(block_ids)(keys)
    return table_ids.reshape(TOKENS, LOOKUPS).astype(jnp.int32)


def block_levels(own_key, extent, cuts, low, top_value):
    factor_of = 1.0
    for position, blocks in cuts:
        steps = jax.random.uniform(jax.random.fold_in(jax.random.fold_in(own_key, 6), position), (blocks,), jnp.float32, low / len(cuts), top_value / len(cuts))
        factor_of = factor_of * jnp.repeat(jnp.exp(steps), extent[position] // blocks).reshape((-1,) + (1,) * (len(extent) - 1 - position))
    return factor_of


def normal_values(rng, dims, spread, reach, shards=(), kind=jnp.bfloat16):
    values = spread * jax.random.normal(rng, dims, jnp.float32)
    if shards:
        values = values * block_levels(rng, dims, shards, -0.22, 0.18)
    return jnp.clip(values, -reach, reach).astype(kind)


def setup_inputs(seed: int = 0) -> dict:
    streams_of = jax.random.split(jax.random.key(seed), 10)
    return {
        "memory": normal_values(streams_of[0], (TOKENS, MEM), 1.0, 6.0, ((0, 32),)),
        "hidden": normal_values(streams_of[1], (TOKENS, D), 1.0, 6.0, ((0, 32), (1, 4))),
        "grad_out": normal_values(streams_of[2], (TOKENS, D), 1.0, 6.0, ((0, 32), (1, 4))),
        "key_weight": normal_values(streams_of[3], (MEM, D), MEM ** -0.5, 0.15625, ((0, 32), (1, 4))),
        "value_weight": normal_values(streams_of[4], (MEM, D), MEM ** -0.5, 0.15625, ((0, 32), (1, 4))),
        "row_ids": draw_row_ids(jax.random.fold_in(streams_of[9], 71), 0),
        "embed_table": normal_values(streams_of[6], (ROWS, ROW_W), 1.0, 6.0, ((0, 128),), jnp.float32),
        "first_moment": normal_values(streams_of[7], (ROWS, ROW_W), 0.1, 0.6, ((0, 128),), jnp.float32),
        "second_moment": jnp.clip(jnp.exp(math.log(0.1) - 4.6051702 * jax.random.uniform(streams_of[8], (ROWS, ROW_W), jnp.float32) ** block_levels(streams_of[8], (ROWS, ROW_W), ((0, 128),), -0.2, 0.2)), 0.001, 0.1),
    }


beta_one = 0.9
beta_two = 0.999
learn_rate = 0.01
adam_eps = 1e-08
norm_eps = 1e-06
correct_one = 0.9999734386011124
correct_two = 0.0952078528863

def adam_update(table_grad, embed_table, first_moment, second_moment):
    new_first = beta_one * first_moment + (1.0 - beta_one) * table_grad
    new_second = beta_two * second_moment + (1.0 - beta_two) * table_grad * table_grad
    stepped = new_first / correct_one / (jnp.sqrt(new_second / correct_two) + adam_eps)
    return (embed_table - learn_rate * stepped, new_first, new_second)

def reference(memory, hidden, grad_out, key_weight, value_weight, row_ids, embed_table, first_moment, second_moment):
    key_proj = jnp.dot(memory, key_weight, preferred_element_type=jnp.float32)
    value_proj = jnp.dot(memory, value_weight, preferred_element_type=jnp.float32)
    hidden_float = hidden.astype(jnp.float32)
    grad_float = grad_out.astype(jnp.float32)
    root_width = math.sqrt(D)
    key_scale = jnp.sqrt(lax.optimization_barrier(jnp.mean(key_proj * key_proj, axis=1, keepdims=True)) + norm_eps)
    gate_score = lax.optimization_barrier(jnp.sum(hidden_float * key_proj, axis=1, keepdims=True)) / (key_scale * root_width)
    gate_value = jax.nn.sigmoid(gate_score)
    gate_grad = gate_value * (1.0 - gate_value) * lax.optimization_barrier(jnp.sum(grad_float * value_proj, axis=1, keepdims=True))
    value_grad = (gate_value * grad_float).astype(jnp.bfloat16)
    key_grad = (gate_grad * (hidden_float / (key_scale * root_width) - gate_score * key_proj / (D * key_scale * key_scale))).astype(jnp.bfloat16)
    contract = (((0,), (0,)), ((), ()))
    key_weight_grad = lax.dot_general(memory, key_grad, contract, preferred_element_type=jnp.float32)
    value_weight_grad = lax.dot_general(memory, value_grad, contract, preferred_element_type=jnp.float32)
    memory_grad = jnp.dot(key_grad, key_weight.T, preferred_element_type=jnp.float32) + jnp.dot(value_grad, value_weight.T, preferred_element_type=jnp.float32)
    memory_grad = memory_grad.astype(jnp.bfloat16)
    pieces = memory_grad.reshape(-1, ROW_W).astype(jnp.float32)
    table_grad = jnp.zeros(embed_table.shape, jnp.float32).at[row_ids.reshape(-1).astype(jnp.int32)].add(pieces)
    new_table, new_first, new_second = adam_update(table_grad, embed_table, first_moment, second_moment)
    return (key_weight_grad, value_weight_grad, new_table, new_first, new_second)
```

```python
import math

import jax
import jax.numpy as jnp
from jax import lax
from jax.experimental import pallas as pl
from jax.experimental.pallas import tpu as pltpu
from jax.sharding import PartitionSpec as P

D = 2560


beta_one = 0.9
beta_two = 0.999
learn_rate = 0.01
adam_eps = 1e-08
norm_eps = 1e-06
correct_one = 0.9999734386011124
correct_two = 0.0952078528863


def in_one_piece(arrays, axis, dim, along):
    widths = [a.shape[along] for a in arrays]
    both = jnp.concatenate(arrays, axis=along)
    whole = lax.all_gather(both, axis, axis=dim, tiled=True)
    return tuple(jnp.split(whole, [sum(widths[:k]) for k in range(1, len(widths))], axis=along))


def sent_to_all(shard, axis):
    length = lax.axis_size(axis)
    return lax.all_to_all(
        jnp.broadcast_to(shard[None], (length, *shard.shape)), axis, 0, 0, tiled=True
    )


def over_copies(shard, axis):
    return sent_to_all(shard, axis).sum(axis=0)


def packed_total(arrays, axis):
    vector, at, done = (jnp.concatenate([a.reshape(-1) for a in arrays]), 0, [])
    subtotal = over_copies(vector, axis)
    for a in arrays:
        done.append(subtotal[at : at + a.size].reshape(a.shape))
        at += a.size
    return tuple(done)


def split_up(shard, dim, length):
    lengths = shard.shape
    tiles = shard.reshape(*lengths[:dim], length, lengths[dim] // length, *lengths[dim + 1 :])
    return jnp.moveaxis(tiles, dim, 0)


def sum_at_owner(shard, axis, dim):
    length = lax.axis_size(axis)
    tiles = lax.all_to_all(split_up(shard, dim, length), axis, 0, 0, tiled=True)
    return jnp.sum(tiles.astype(jnp.float32), axis=0)


SLOTS = 48
TILE = 256


def pack_kernel(tile_ref, spot_ref, parts_ref, out_ref, rows_ref):
    lookups, width = tile_ref.shape[0], out_ref.shape[1]
    tokens = parts_ref.shape[1]

    @pl.when(pl.program_id(0) == 0)
    def _():
        for l in range(lookups):
            total = parts_ref[0, :, l * width : (l + 1) * width].astype(jnp.float32)
            for k in range(1, parts_ref.shape[0]):
                total += parts_ref[k, :, l * width : (l + 1) * width].astype(jnp.float32)
            rows_ref[l * tokens : (l + 1) * tokens, :] = total.astype(jnp.bfloat16)

    steps = out_ref.shape[0] // TILE
    place = lax.broadcasted_iota(jnp.int32, (TILE, tokens), 0).astype(jnp.bfloat16)
    one, zero = jnp.ones((), jnp.bfloat16), jnp.zeros((), jnp.bfloat16)
    for s in range(steps):
        here = pl.program_id(0) * steps + s
        total = jnp.zeros((TILE, width), jnp.float32)
        for l in range(lookups):
            spot = jnp.where(tile_ref[l : l + 1, :] == here, spot_ref[l : l + 1, :], -1)
            spot = jnp.broadcast_to(spot.astype(jnp.bfloat16), (TILE, tokens))
            hits = jnp.where(place == spot, one, zero)
            total += jnp.dot(
                hits,
                rows_ref[l * tokens : (l + 1) * tokens, :],
                preferred_element_type=jnp.float32,
            )
        out_ref[s * TILE : (s + 1) * TILE, :] = total.astype(jnp.bfloat16)


def pack_rows(slot, parts, total_slots, width):
    per_step = 3 * TILE
    tokens = parts.shape[1]
    lookups = slot.shape[0]
    return pl.pallas_call(
        pack_kernel,
        out_shape=jax.ShapeDtypeStruct((total_slots, width), jnp.bfloat16),
        grid=(total_slots // per_step,),
        in_specs=[
            pl.BlockSpec(slot.shape, lambda i: (0, 0)),
            pl.BlockSpec(slot.shape, lambda i: (0, 0)),
            pl.BlockSpec(parts.shape, lambda i: (0, 0, 0)),
        ],
        out_specs=pl.BlockSpec((per_step, width), lambda i: (i, 0)),
        scratch_shapes=[pltpu.VMEM((lookups * tokens, width), jnp.bfloat16)],
        compiler_params=pltpu.CompilerParams(vmem_limit_bytes=40 * 1024 * 1024),
        name="pack_rows",
    )(slot // TILE, slot % TILE, parts)


def adam_kernel(
    tile_ref, spot_ref, rows_ref, table_ref, first_ref, second_ref, new_table_ref, new_first_ref, new_second_ref
):
    steps = table_ref.shape[0] // TILE
    width = table_ref.shape[1]
    entries = rows_ref.shape[0]
    chunk = 1024
    place = lax.broadcasted_iota(jnp.int32, (TILE, chunk), 0).astype(jnp.bfloat16)
    one, zero = jnp.ones((), jnp.bfloat16), jnp.zeros((), jnp.bfloat16)
    for s in range(steps):
        here = pl.program_id(0) * steps + s
        grad = jnp.zeros((TILE, width), jnp.float32)
        for k in range(0, entries, chunk):
            spot = jnp.where(tile_ref[:, k : k + chunk] == here, spot_ref[:, k : k + chunk], -1)
            spot = jnp.broadcast_to(spot.astype(jnp.bfloat16), (TILE, chunk))
            hits = jnp.where(place == spot, one, zero)
            grad += jnp.dot(hits, rows_ref[k : k + chunk, :], preferred_element_type=jnp.float32)
        at = slice(s * TILE, (s + 1) * TILE)
        new_first = beta_one * first_ref[at, :] + (1.0 - beta_one) * grad
        new_second = beta_two * second_ref[at, :] + (1.0 - beta_two) * grad * grad
        stepped = new_first / correct_one / (jnp.sqrt(new_second / correct_two) + adam_eps)
        new_table_ref[at, :] = table_ref[at, :] - learn_rate * stepped
        new_first_ref[at, :] = new_first
        new_second_ref[at, :] = new_second


def adam_rows(got_ids, got_rows, embed_table, first_moment, second_moment):
    rows_dev, width = embed_table.shape
    per_step = 2 * TILE
    block = pl.BlockSpec((per_step, width), lambda i: (i, 0))
    ids = got_ids.reshape(1, -1)
    whole = pl.BlockSpec(ids.shape, lambda i: (0, 0))
    return pl.pallas_call(
        adam_kernel,
        out_shape=(jax.ShapeDtypeStruct((rows_dev, width), jnp.float32),) * 3,
        grid=(rows_dev // per_step,),
        in_specs=[
            whole,
            whole,
            pl.BlockSpec(got_rows.shape, lambda i: (0, 0)),
            block,
            block,
            block,
        ],
        out_specs=(block,) * 3,
        compiler_params=pltpu.CompilerParams(vmem_limit_bytes=40 * 1024 * 1024),
        name="adam_rows",
    )(ids // TILE, ids % TILE, got_rows, embed_table, first_moment, second_moment)


def route(my_ids, owners, rows_dev):
    ids = my_ids.T
    lookups, tokens = ids.shape
    flat = ids.reshape(-1)
    entries = flat.shape[0]
    owner_of = flat // rows_dev
    local_row = flat % rows_dev
    owner_hits = (owner_of[:, None] == jnp.arange(owners, dtype=jnp.int32)[None, :]).astype(
        jnp.bfloat16
    )
    earlier = (jnp.arange(entries)[None, :] < jnp.arange(entries)[:, None]).astype(jnp.bfloat16)
    before_counts = jnp.dot(earlier, owner_hits, preferred_element_type=jnp.float32)
    slot_rank = jnp.sum(before_counts * owner_hits.astype(jnp.float32), axis=1).astype(jnp.int32)
    slot = (owner_of * SLOTS + slot_rank).reshape(lookups, tokens)
    rank_hits = slot_rank[:, None] == jnp.arange(SLOTS, dtype=jnp.int32)[None, :]
    low = local_row % 64
    high = local_row // 64
    values = jnp.concatenate(
        [
            jnp.where(rank_hits, v[:, None], 0).astype(jnp.bfloat16)
            for v in (high, low, jnp.ones_like(low))
        ],
        axis=1,
    )
    found = lax.dot_general(
        owner_hits, values, (((0,), (0,)), ((), ())), preferred_element_type=jnp.float32
    ).astype(jnp.int32)
    got_high, got_low, filled = jnp.split(found, 3, axis=1)
    send_ids = jnp.where(filled > 0, got_high * 64 + got_low, rows_dev)
    return slot, send_ids


def body(
    memory,
    hidden,
    grad_out,
    key_weight,
    value_weight,
    row_ids,
    embed_table,
    first_moment,
    second_moment,
):
    dp_count = lax.axis_size("dp")
    tensor_count = lax.axis_size("tensor")
    owners = dp_count * tensor_count
    rows_dev, row_width = embed_table.shape
    block_rows = memory.shape[0] // tensor_count
    my_ids = lax.dynamic_slice_in_dim(
        row_ids, lax.axis_index("tensor") * block_rows, block_rows, 0
    )
    slot, send_ids = route(my_ids, owners, rows_dev)
    got_ids = lax.all_to_all(
        send_ids, ("dp", "tensor"), split_axis=0, concat_axis=0, tiled=True
    )
    key_full, value_full = in_one_piece((key_weight, value_weight), "dp", 0, 1)
    key_proj = jnp.dot(memory, key_full, preferred_element_type=jnp.float32)
    value_proj = jnp.dot(memory, value_full, preferred_element_type=jnp.float32)
    hidden_float = hidden.astype(jnp.float32)
    grad_float = grad_out.astype(jnp.float32)
    root_width = math.sqrt(D)
    square_sum, cross_sum, output_sum = packed_total(
        (
            jnp.sum(key_proj * key_proj, axis=1, keepdims=True),
            jnp.sum(hidden_float * key_proj, axis=1, keepdims=True),
            jnp.sum(grad_float * value_proj, axis=1, keepdims=True),
        ),
        "tensor",
    )
    key_scale = jnp.sqrt(square_sum / D + norm_eps)
    gate_score = cross_sum / (key_scale * root_width)
    gate_value = jax.nn.sigmoid(gate_score)
    gate_grad = gate_value * (1.0 - gate_value) * output_sum
    key_grad = gate_grad * (
        hidden_float / (key_scale * root_width)
        - gate_score * key_proj / (D * key_scale * key_scale)
    )
    value_grad = gate_value * grad_float
    both_grads = jnp.concatenate(
        [key_grad.astype(jnp.bfloat16), value_grad.astype(jnp.bfloat16)], axis=1
    )
    width_local = key_full.shape[1]
    weight_grads = sum_at_owner(
        lax.dot_general(
            memory, both_grads, (((0,), (0,)), ((), ())), preferred_element_type=jnp.float32
        ).astype(jnp.bfloat16),
        "dp",
        0,
    )
    key_weight_grad = weight_grads[:, :width_local]
    value_weight_grad = weight_grads[:, width_local:]
    both_full = jnp.concatenate([key_full, value_full], axis=1)
    memory_parts = lax.all_to_all(
        lax.dot_general(
            both_grads, both_full, (((1,), (1,)), ((), ())), preferred_element_type=jnp.float32
        )
        .astype(jnp.bfloat16)
        .reshape(tensor_count, block_rows, -1),
        "tensor",
        0,
        0,
        tiled=True,
    )
    send_rows = pack_rows(slot, memory_parts, owners * SLOTS, row_width)
    got_rows = lax.all_to_all(
        send_rows.reshape(owners, SLOTS, row_width),
        ("dp", "tensor"),
        split_axis=0,
        concat_axis=0,
        tiled=True,
    )
    new_table, new_first, new_second = adam_rows(
        got_ids, got_rows.reshape(-1, row_width), embed_table, first_moment, second_moment
    )
    return (key_weight_grad, value_weight_grad, new_table, new_first, new_second)


def solution(mesh):
    return jax.shard_map(
        body,
        mesh=mesh,
        in_specs=(
            P("dp", None),
            P("dp", "tensor"),
            P("dp", "tensor"),
            P("dp", "tensor"),
            P("dp", "tensor"),
            P("dp", None),
            P(("dp", "tensor"), None),
            P(("dp", "tensor"), None),
            P(("dp", "tensor"), None),
        ),
        out_specs=(
            P("dp", "tensor"),
            P("dp", "tensor"),
            P(("dp", "tensor"), None),
            P(("dp", "tensor"), None),
            P(("dp", "tensor"), None),
        ),
        check_vma=False,
    )
```

```python
import math

import jax
import jax.numpy as jnp
from jax import lax
from jax.experimental import pallas as pl
from jax.experimental.pallas import tpu as pltpu
from jax.sharding import PartitionSpec as P

D = 2560


beta_one = 0.9
beta_two = 0.999
learn_rate = 0.01
adam_eps = 1e-08
norm_eps = 1e-06
correct_one = 0.9999734386011124
correct_two = 0.0952078528863


def dp_index(x, y, c):
    return (x % 4) * 8 + (y % 4) * 2 + c


def along_x(d):
    return [
        (dp_index(x, y, c), dp_index(x + d, y, c))
        for x in range(4)
        for y in range(4)
        for c in range(2)
    ]


def along_y(d):
    return [
        (dp_index(x, y, c), dp_index(x, y + d, c))
        for x in range(4)
        for y in range(4)
        for c in range(2)
    ]


def other_core():
    return [
        (dp_index(x, y, c), dp_index(x, y, 1 - c))
        for x in range(4)
        for y in range(4)
        for c in range(2)
    ]


def along_z(d):
    return [(z, (z + d) % 4) for z in range(4)]


STEPS = (1, 2, 3)


def ring_gather(shard, perm_of):
    return [shard] + [lax.ppermute(shard, "dp", perm_of(d)) for d in STEPS]


def ring_sum(tiles, here, perm_of):
    own = lax.dynamic_index_in_dim(tiles, here, 0, keepdims=False).astype(jnp.float32)
    got = [
        lax.ppermute(
            lax.dynamic_index_in_dim(tiles, (here + d) % 4, 0, keepdims=False), "dp", perm_of(d)
        )
        for d in STEPS
    ]
    for g in got:
        own += g.astype(jnp.float32)
    return own


def gather_weights(key_weight, value_weight):
    key_x = ring_gather(key_weight, along_x)
    value_y = ring_gather(value_weight, along_y)
    key_x = jnp.stack(key_x)
    value_y = jnp.stack(value_y)
    key_x, value_y = lax.optimization_barrier((key_x, value_y))
    key_all = jnp.stack(ring_gather(key_x, along_y))
    value_all = jnp.stack(ring_gather(value_y, along_x))
    return jnp.stack([key_all, value_all])


def sum_weight_grads(weight_grads, x, y, c):
    width = weight_grads.shape[1]
    tiles = weight_grads.reshape(16, 2, -1, width)
    sent = lax.dynamic_index_in_dim(tiles, 1 - c, 1, keepdims=False)
    kept = lax.dynamic_index_in_dim(tiles, c, 1, keepdims=False)
    got = lax.ppermute(sent, "dp", other_core())
    both = (kept.astype(jnp.float32) + got.astype(jnp.float32)).astype(jnp.bfloat16)
    both = both.reshape(4, 4, -1, width)
    half = width // 2
    key_part = ring_sum(both[:, :, :, :half], x, along_x).astype(jnp.bfloat16)
    value_part = ring_sum(jnp.swapaxes(both[:, :, :, half:], 0, 1), y, along_y).astype(jnp.bfloat16)
    return (ring_sum(key_part, y, along_y), ring_sum(value_part, x, along_x))


def project_kernel(
    spot_ref, mine_ref, got_ref, memory_ref, hidden_ref, grad_ref, weight_ref, key_proj_ref, sums_ref
):
    half = hidden_ref.shape[1]

    @pl.when(pl.program_id(0) == 0)
    def _():
        x, y, c = spot_ref[0], spot_ref[1], spot_ref[2]
        rows = mine_ref.shape[2]
        for one in range(4):
            for two in range(4):
                for half_index in range(2):
                    a = mine_ref[half_index, one * 4 + two].astype(jnp.float32)
                    b = got_ref[half_index, one * 4 + two].astype(jnp.float32)
                    low = jnp.where(c == 0, a, b)
                    high = jnp.where(c == 0, b, a)
                    dx, dy = (two, one) if half_index == 0 else (one, two)
                    at = ((x + 4 - dx) % 4) * 4 + (y + 4 - dy) % 4
                    both = jnp.concatenate([low, high], axis=0).astype(jnp.bfloat16)
                    weight_ref[
                        pl.ds(pl.multiple_of(at * (2 * rows), 16), 2 * rows),
                        half_index * half : (half_index + 1) * half,
                    ] = both

    memory = memory_ref[...]
    key_proj = jnp.dot(memory, weight_ref[:, :half], preferred_element_type=jnp.float32)
    value_proj = jnp.dot(memory, weight_ref[:, half:], preferred_element_type=jnp.float32)
    key_proj_ref[...] = key_proj
    hidden = hidden_ref[...].astype(jnp.float32)
    grad = grad_ref[...].astype(jnp.float32)
    square_sum = jnp.sum(key_proj * key_proj, axis=1, keepdims=True)
    cross_sum = jnp.sum(hidden * key_proj, axis=1, keepdims=True)
    output_sum = jnp.sum(grad * value_proj, axis=1, keepdims=True)
    lane = lax.broadcasted_iota(jnp.int32, (memory.shape[0], 128), 1)
    sums = jnp.where(lane == 0, square_sum, jnp.where(lane == 1, cross_sum, output_sum))
    sums_ref[...] = sums.T[:8, :]


def project(spot, mine, got, memory, hidden, grad_out):
    tokens, mem = memory.shape
    half = hidden.shape[1]
    tile = tokens // 4
    fixed = lambda i, s: (0, 0)
    return pl.pallas_call(
        project_kernel,
        out_shape=(
            jax.ShapeDtypeStruct((mem, 2 * half), jnp.bfloat16),
            jax.ShapeDtypeStruct((tokens, half), jnp.float32),
            jax.ShapeDtypeStruct((8, tokens), jnp.float32),
        ),
        grid_spec=pltpu.PrefetchScalarGridSpec(
            num_scalar_prefetch=1,
            grid=(4,),
            in_specs=[
                pl.BlockSpec(mine.shape, lambda i, s: (0, 0, 0, 0)),
                pl.BlockSpec(got.shape, lambda i, s: (0, 0, 0, 0)),
                pl.BlockSpec((tile, mem), lambda i, s: (i, 0)),
                pl.BlockSpec((tile, half), lambda i, s: (i, 0)),
                pl.BlockSpec((tile, half), lambda i, s: (i, 0)),
            ],
            out_specs=(
                pl.BlockSpec((mem, 2 * half), fixed),
                pl.BlockSpec((tile, half), lambda i, s: (i, 0)),
                pl.BlockSpec((8, tile), lambda i, s: (0, i)),
            ),
        ),
        compiler_params=pltpu.CompilerParams(vmem_limit_bytes=44 * 1024 * 1024),
        name="project",
    )(spot, mine, got, memory, hidden, grad_out)


def grads_of(sums_refs, hidden_ref, grad_ref, key_proj_ref, weight_ref, both_ref):
    half = hidden_ref.shape[1]
    sums = sums_refs[0][...] + sums_refs[1][...] + sums_refs[2][...] + sums_refs[3][...]
    root_width = math.sqrt(D)
    key_scale = jnp.sqrt(sums[0:1, :] / D + norm_eps)
    gate_score = sums[1:2, :] / (key_scale * root_width)
    gate_value = 1.0 / (1.0 + jnp.exp(-gate_score))
    gate_grad = gate_value * (1.0 - gate_value) * sums[2:3, :]
    by_hidden = 1.0 / (key_scale * root_width)
    by_key = gate_score / (D * key_scale * key_scale)
    row = lax.broadcasted_iota(jnp.int32, (128, sums.shape[1]), 0)
    coded = jnp.where(
        row == 0,
        gate_value,
        jnp.where(row == 1, gate_grad, jnp.where(row == 2, by_hidden, by_key)),
    ).T
    hidden = hidden_ref[...].astype(jnp.float32)
    key_grad = coded[:, 1:2] * (hidden * coded[:, 2:3] - key_proj_ref[...] * coded[:, 3:4])
    value_grad = coded[:, 0:1] * grad_ref[...].astype(jnp.float32)
    both_ref[:, :half] = key_grad.astype(jnp.bfloat16)
    both_ref[:, half:] = value_grad.astype(jnp.bfloat16)
    return lax.dot_general(
        both_ref[...],
        weight_ref[...],
        (((1,), (1,)), ((), ())),
        preferred_element_type=jnp.float32,
    ).astype(jnp.bfloat16)


def grads_kernel(order_ref, *refs):
    sums_refs, (hidden_ref, grad_ref, key_proj_ref, weight_ref), rest = refs[:4], refs[4:8], refs[8:]
    if len(rest) % 2 == 0:
        rest = rest[1:]
    both_ref, outs = rest[0], rest[1:]
    memory_grad = grads_of(sums_refs, hidden_ref, grad_ref, key_proj_ref, weight_ref, both_ref)
    half = outs[0].shape[1]
    for k in range(len(outs) // 2):

        @pl.when(pl.program_id(0) == k)
        def _():
            outs[2 * k][...] = memory_grad[:, :half]
            outs[2 * k + 1][...] = memory_grad[:, half:]


def grads(order, sums, hidden, grad_out, key_proj, weights, both):
    steps = order.shape[0]
    tokens, half = hidden.shape
    tile = tokens // 4
    mem = weights.shape[0]
    at = lambda i, o: (o[i], 0)
    out_half = pl.BlockSpec((tile, mem // 2), lambda i, o: (0, 0))
    whole = pl.BlockSpec((tile, 2 * half), at)
    given = () if both is None else (both,)
    return pl.pallas_call(
        grads_kernel,
        out_shape=(
            jax.ShapeDtypeStruct((tokens, 2 * half), jnp.bfloat16),
            *([jax.ShapeDtypeStruct((tile, mem // 2), jnp.bfloat16)] * (2 * steps)),
        ),
        grid_spec=pltpu.PrefetchScalarGridSpec(
            num_scalar_prefetch=1,
            grid=(steps,),
            in_specs=[pl.BlockSpec((8, tile), lambda i, o: (0, o[i]))] * 4
            + [pl.BlockSpec((tile, half), at)] * 3
            + [pl.BlockSpec(weights.shape, lambda i, o: (0, 0))]
            + [pl.BlockSpec(memory_space=pl.ANY)] * len(given),
            out_specs=(whole, *([out_half] * (2 * steps))),
        ),
        input_output_aliases={9: 0} if given else {},
        compiler_params=pltpu.CompilerParams(vmem_limit_bytes=44 * 1024 * 1024),
        name="grads_far" if both is None else "grads_near",
    )(order, *sums, hidden, grad_out, key_proj, weights, *given)


SLOTS = 48
TILE = 256


def pack_kernel(tile_ref, spot_ref, l1, l2, l3, r1, r2, r3, out_ref, sum_ref, rows_ref):
    lookups, width = tile_ref.shape[0], out_ref.shape[1]
    tokens, half = l1.shape

    @pl.when(pl.program_id(0) == 0)
    def _():
        f32 = jnp.float32
        left = l1[...].astype(f32) + l2[...].astype(f32) + l3[...].astype(f32)
        right = r1[...].astype(f32) + r2[...].astype(f32) + r3[...].astype(f32)
        sum_ref[:, :half] = left.astype(jnp.bfloat16)
        sum_ref[:, half:] = right.astype(jnp.bfloat16)
        for l in range(lookups):
            rows_ref[l * tokens : (l + 1) * tokens, :] = sum_ref[:, l * width : (l + 1) * width]

    steps = out_ref.shape[0] // TILE
    place = lax.broadcasted_iota(jnp.int32, (TILE, lookups * tokens), 0).astype(jnp.bfloat16)
    one, zero = jnp.ones((), jnp.bfloat16), jnp.zeros((), jnp.bfloat16)
    hits = []
    for s in range(steps):
        here = pl.program_id(0) * steps + s
        spot = jnp.concatenate(
            [
                jnp.where(tile_ref[l : l + 1, :] == here, spot_ref[l : l + 1, :], -1)
                for l in range(lookups)
            ],
            axis=1,
        )
        spot = jnp.broadcast_to(spot.astype(jnp.bfloat16), place.shape)
        hits.append(jnp.where(place == spot, one, zero))
    out_ref[...] = jnp.dot(
        jnp.concatenate(hits, axis=0), rows_ref[...], preferred_element_type=jnp.float32
    ).astype(jnp.bfloat16)


def pack_rows(slot, parts, total_slots, width):
    per_step = 3 * TILE
    tokens, half = parts[0].shape
    lookups = slot.shape[0]
    return pl.pallas_call(
        pack_kernel,
        out_shape=jax.ShapeDtypeStruct((total_slots, width), jnp.bfloat16),
        grid=(total_slots // per_step,),
        in_specs=[pl.BlockSpec(slot.shape, lambda i: (0, 0))] * 2
        + [pl.BlockSpec((tokens, half), lambda i: (0, 0))] * 6,
        out_specs=pl.BlockSpec((per_step, width), lambda i: (i, 0)),
        scratch_shapes=[
            pltpu.VMEM((tokens, 2 * half), jnp.bfloat16),
            pltpu.VMEM((lookups * tokens, width), jnp.bfloat16),
        ],
        compiler_params=pltpu.CompilerParams(vmem_limit_bytes=40 * 1024 * 1024),
        name="pack_rows",
    )(slot // TILE, slot % TILE, *parts)


def adam_kernel(
    tile_ref, spot_ref, rows_ref, table_ref, first_ref, second_ref, new_table_ref, new_first_ref, new_second_ref
):
    steps = table_ref.shape[0] // TILE
    width = table_ref.shape[1]
    entries = rows_ref.shape[0]
    chunk = 1024
    place = lax.broadcasted_iota(jnp.int32, (TILE, chunk), 0).astype(jnp.bfloat16)
    one, zero = jnp.ones((), jnp.bfloat16), jnp.zeros((), jnp.bfloat16)
    for s in range(steps):
        here = pl.program_id(0) * steps + s
        grad = jnp.zeros((TILE, width), jnp.float32)
        for k in range(0, entries, chunk):
            spot = jnp.where(tile_ref[:, k : k + chunk] == here, spot_ref[:, k : k + chunk], -1)
            spot = jnp.broadcast_to(spot.astype(jnp.bfloat16), (TILE, chunk))
            hits = jnp.where(place == spot, one, zero)
            grad += jnp.dot(hits, rows_ref[k : k + chunk, :], preferred_element_type=jnp.float32)
        at = slice(s * TILE, (s + 1) * TILE)
        new_first = beta_one * first_ref[at, :] + (1.0 - beta_one) * grad
        new_second = beta_two * second_ref[at, :] + (1.0 - beta_two) * grad * grad
        stepped = new_first / correct_one / (jnp.sqrt(new_second / correct_two) + adam_eps)
        new_table_ref[at, :] = table_ref[at, :] - learn_rate * stepped
        new_first_ref[at, :] = new_first
        new_second_ref[at, :] = new_second


def adam_rows(got_ids, got_rows, embed_table, first_moment, second_moment):
    rows_dev, width = embed_table.shape
    per_step = 2 * TILE
    block = pl.BlockSpec((per_step, width), lambda i: (i, 0))
    ids = got_ids.reshape(1, -1)
    whole = pl.BlockSpec(ids.shape, lambda i: (0, 0))
    return pl.pallas_call(
        adam_kernel,
        out_shape=(jax.ShapeDtypeStruct((rows_dev, width), jnp.float32),) * 3,
        grid=(rows_dev // per_step,),
        in_specs=[
            whole,
            whole,
            pl.BlockSpec(got_rows.shape, lambda i: (0, 0)),
            block,
            block,
            block,
        ],
        out_specs=(block,) * 3,
        compiler_params=pltpu.CompilerParams(vmem_limit_bytes=40 * 1024 * 1024),
        name="adam_rows",
    )(ids // TILE, ids % TILE, got_rows, embed_table, first_moment, second_moment)


def route(my_ids, owners, rows_dev):
    ids = my_ids.T
    lookups, tokens = ids.shape
    flat = ids.reshape(-1)
    entries = flat.shape[0]
    owner_of = flat // rows_dev
    local_row = flat % rows_dev
    owner_hits = (owner_of[:, None] == jnp.arange(owners, dtype=jnp.int32)[None, :]).astype(
        jnp.bfloat16
    )
    earlier = (jnp.arange(entries)[None, :] < jnp.arange(entries)[:, None]).astype(jnp.bfloat16)
    before_counts = jnp.dot(earlier, owner_hits, preferred_element_type=jnp.float32)
    slot_rank = jnp.sum(before_counts * owner_hits.astype(jnp.float32), axis=1).astype(jnp.int32)
    slot = (owner_of * SLOTS + slot_rank).reshape(lookups, tokens)
    rank_hits = slot_rank[:, None] == jnp.arange(SLOTS, dtype=jnp.int32)[None, :]
    low = local_row % 64
    high = local_row // 64
    values = jnp.concatenate(
        [
            jnp.where(rank_hits, v[:, None], 0).astype(jnp.bfloat16)
            for v in (high, low, jnp.ones_like(low))
        ],
        axis=1,
    )
    found = lax.dot_general(
        owner_hits, values, (((0,), (0,)), ((), ())), preferred_element_type=jnp.float32
    ).astype(jnp.int32)
    got_high, got_low, filled = jnp.split(found, 3, axis=1)
    send_ids = jnp.where(filled > 0, got_high * 64 + got_low, rows_dev)
    return slot, send_ids


def body(
    memory,
    hidden,
    grad_out,
    key_weight,
    value_weight,
    row_ids,
    embed_table,
    first_moment,
    second_moment,
):
    dp_count = lax.axis_size("dp")
    tensor_count = lax.axis_size("tensor")
    owners = dp_count * tensor_count
    rows_dev, row_width = embed_table.shape
    block_rows = memory.shape[0] // tensor_count
    my_ids = lax.dynamic_slice_in_dim(
        row_ids, lax.axis_index("tensor") * block_rows, block_rows, 0
    )
    at = lax.axis_index("dp")
    z = lax.axis_index("tensor")
    x, y, c = at // 8, (at // 2) % 4, at % 2
    slot, send_ids = route(my_ids, owners, rows_dev)
    got_ids = lax.all_to_all(
        send_ids, ("dp", "tensor"), split_axis=0, concat_axis=0, tiled=True
    )
    mine = gather_weights(key_weight, value_weight)
    mine, got_ids, slot = lax.optimization_barrier((mine, got_ids, slot))
    mine = mine.reshape(2, 16, *key_weight.shape)
    got = lax.ppermute(mine, "dp", other_core())
    spot = jnp.stack([x, y, c]).astype(jnp.int32)
    weights, key_proj, sums = project(spot, mine, got, memory, hidden, grad_out)
    sums = [sums] + [lax.ppermute(sums, "tensor", along_z(d)) for d in STEPS]
    far = ((z + 2) % 4)[None].astype(jnp.int32)
    near = jnp.stack([(z + 1) % 4, (z + 3) % 4, z]).astype(jnp.int32)
    both, far_left, far_right = grads(
        far, sums, hidden, grad_out, key_proj, weights, None
    )
    up = lax.ppermute(far_left, "tensor", along_z(1))
    down = lax.ppermute(far_right, "tensor", along_z(3))
    both, next_left, next_right, last_left, last_right, own_left, own_right = grads(
        near, sums, hidden, grad_out, key_proj, weights, both
    )
    from_last_right = lax.ppermute(next_right, "tensor", along_z(1))
    from_next_left = lax.ppermute(last_left, "tensor", along_z(3))
    from_last_left = lax.ppermute(
        (up.astype(jnp.float32) + next_left.astype(jnp.float32)).astype(jnp.bfloat16),
        "tensor",
        along_z(1),
    )
    from_next_right = lax.ppermute(
        (down.astype(jnp.float32) + last_right.astype(jnp.float32)).astype(jnp.bfloat16),
        "tensor",
        along_z(3),
    )
    key_weight_grad, value_weight_grad = sum_weight_grads(
        lax.dot_general(
            memory, both, (((0,), (0,)), ((), ())), preferred_element_type=jnp.float32
        ).astype(jnp.bfloat16),
        x,
        y,
        c,
    )
    send_rows = pack_rows(
        slot,
        (own_left, from_last_left, from_next_left, own_right, from_last_right, from_next_right),
        owners * SLOTS,
        row_width,
    )
    got_rows = lax.all_to_all(
        send_rows.reshape(owners, SLOTS, row_width),
        ("dp", "tensor"),
        split_axis=0,
        concat_axis=0,
        tiled=True,
    )
    new_table, new_first, new_second = adam_rows(
        got_ids, got_rows.reshape(-1, row_width), embed_table, first_moment, second_moment
    )
    return (key_weight_grad, value_weight_grad, new_table, new_first, new_second)


def solution(mesh):
    return jax.shard_map(
        body,
        mesh=mesh,
        in_specs=(
            P("dp", None),
            P("dp", "tensor"),
            P("dp", "tensor"),
            P("dp", "tensor"),
            P("dp", "tensor"),
            P("dp", None),
            P(("dp", "tensor"), None),
            P(("dp", "tensor"), None),
            P(("dp", "tensor"), None),
        ),
        out_specs=(
            P("dp", "tensor"),
            P("dp", "tensor"),
            P(("dp", "tensor"), None),
            P(("dp", "tensor"), None),
            P(("dp", "tensor"), None),
        ),
        check_vma=False,
    )
```

```python
import math

import jax
import jax.numpy as jnp
from jax import lax
from jax.experimental import pallas as pl
from jax.experimental.pallas import tpu as pltpu
from jax.sharding import PartitionSpec as P

D = 2560


beta_one = 0.9
beta_two = 0.999
learn_rate = 0.01
adam_eps = 1e-08
norm_eps = 1e-06
correct_one = 0.9999734386011124
correct_two = 0.0952078528863


def dp_index(x, y, c):
    return (x % 4) * 8 + (y % 4) * 2 + c


def along_x(d):
    return [
        (dp_index(x, y, c), dp_index(x + d, y, c))
        for x in range(4)
        for y in range(4)
        for c in range(2)
    ]


def along_y(d):
    return [
        (dp_index(x, y, c), dp_index(x, y + d, c))
        for x in range(4)
        for y in range(4)
        for c in range(2)
    ]


def other_core():
    return [
        (dp_index(x, y, c), dp_index(x, y, 1 - c))
        for x in range(4)
        for y in range(4)
        for c in range(2)
    ]


def along_z(d):
    return [(z, (z + d) % 4) for z in range(4)]


STEPS = (1, 2, 3)


def in_hbm(*arrays):
    return tuple(pltpu.with_memory_space_constraint(a, pltpu.HBM) for a in arrays)


def ring_gather(shard, perm_of):
    return [shard] + [lax.ppermute(shard, "dp", perm_of(d)) for d in STEPS]


def ring_sum(tiles, here, perm_of):
    own = lax.dynamic_index_in_dim(tiles, here, 0, keepdims=False).astype(jnp.float32)
    got = [
        lax.ppermute(
            lax.dynamic_index_in_dim(tiles, (here + d) % 4, 0, keepdims=False), "dp", perm_of(d)
        )
        for d in STEPS
    ]
    for g in got:
        own += g.astype(jnp.float32)
    return own


def gather_weights(key_weight, value_weight, send_ids):
    key_x = ring_gather(key_weight, along_x)
    value_y = ring_gather(value_weight, along_y)
    key_x = jnp.stack(key_x)
    value_y = jnp.stack(value_y)
    key_x, value_y = lax.optimization_barrier((key_x, value_y))
    key_all = ring_gather(key_x, along_y)
    value_all = ring_gather(value_y, along_x)
    key_all[1], send_ids = lax.optimization_barrier((key_all[1], send_ids))
    got_ids = lax.all_to_all(
        send_ids, ("dp", "tensor"), split_axis=0, concat_axis=0, tiled=True
    )
    return (jnp.stack([jnp.stack(key_all), jnp.stack(value_all)]), got_ids)


def core_halves(weight_grads, c):
    tiles = weight_grads.reshape(16, 2, -1, weight_grads.shape[1])
    sent = lax.dynamic_index_in_dim(tiles, 1 - c, 1, keepdims=False)
    kept = lax.dynamic_index_in_dim(tiles, c, 1, keepdims=False)
    return (sent, kept)


def sum_on_chip(sent, kept):
    got = lax.ppermute(sent, "dp", other_core())
    both = (kept.astype(jnp.float32) + got.astype(jnp.float32)).astype(jnp.bfloat16)
    return both.reshape(4, 4, *both.shape[1:])


def sum_one_axis(both, x, y):
    half = both.shape[3] // 2
    key_part = ring_sum(both[:, :, :, :half], x, along_x).astype(jnp.bfloat16)
    value_part = ring_sum(jnp.swapaxes(both[:, :, :, half:], 0, 1), y, along_y).astype(jnp.bfloat16)
    return (key_part, value_part)


def project_kernel(
    spot_ref, mine_ref, got_ref, memory_ref, hidden_ref, grad_ref, weight_ref, key_proj_ref, sums_ref
):
    half = hidden_ref.shape[1]

    @pl.when(pl.program_id(0) == 0)
    def _():
        x, y, c = spot_ref[0], spot_ref[1], spot_ref[2]
        rows = mine_ref.shape[2]
        for one in range(4):
            for two in range(4):
                for half_index in range(2):
                    a = mine_ref[half_index, one * 4 + two].astype(jnp.float32)
                    b = got_ref[half_index, one * 4 + two].astype(jnp.float32)
                    low = jnp.where(c == 0, a, b)
                    high = jnp.where(c == 0, b, a)
                    dx, dy = (two, one) if half_index == 0 else (one, two)
                    at = ((x + 4 - dx) % 4) * 4 + (y + 4 - dy) % 4
                    both = jnp.concatenate([low, high], axis=0).astype(jnp.bfloat16)
                    weight_ref[
                        pl.ds(pl.multiple_of(at * (2 * rows), 16), 2 * rows),
                        half_index * half : (half_index + 1) * half,
                    ] = both

    memory = memory_ref[...]
    key_proj = jnp.dot(memory, weight_ref[:, :half], preferred_element_type=jnp.float32)
    value_proj = jnp.dot(memory, weight_ref[:, half:], preferred_element_type=jnp.float32)
    key_proj_ref[...] = key_proj
    hidden = hidden_ref[...].astype(jnp.float32)
    grad = grad_ref[...].astype(jnp.float32)
    square_sum = jnp.sum(key_proj * key_proj, axis=1, keepdims=True)
    cross_sum = jnp.sum(hidden * key_proj, axis=1, keepdims=True)
    output_sum = jnp.sum(grad * value_proj, axis=1, keepdims=True)
    lane = lax.broadcasted_iota(jnp.int32, (memory.shape[0], 128), 1)
    sums = jnp.where(lane == 0, square_sum, jnp.where(lane == 1, cross_sum, output_sum))
    sums_ref[...] = sums.T[:8, :]


def project(spot, mine, got, memory, hidden, grad_out):
    tokens, mem = memory.shape
    half = hidden.shape[1]
    tile = tokens // 4
    fixed = lambda i, s: (0, 0)
    return pl.pallas_call(
        project_kernel,
        out_shape=(
            jax.ShapeDtypeStruct((mem, 2 * half), jnp.bfloat16),
            pltpu.HBM((tokens, half), jnp.float32),
            jax.ShapeDtypeStruct((8, tokens), jnp.float32),
        ),
        grid_spec=pltpu.PrefetchScalarGridSpec(
            num_scalar_prefetch=1,
            grid=(4,),
            in_specs=[
                pl.BlockSpec(mine.shape, lambda i, s: (0, 0, 0, 0), pipeline_mode=pl.Buffered(1)),
                pl.BlockSpec(got.shape, lambda i, s: (0, 0, 0, 0), pipeline_mode=pl.Buffered(1)),
                pl.BlockSpec((tile, mem), lambda i, s: (i, 0)),
                pl.BlockSpec((tile, half), lambda i, s: (i, 0)),
                pl.BlockSpec((tile, half), lambda i, s: (i, 0)),
            ],
            out_specs=(
                pl.BlockSpec((mem, 2 * half), fixed, pipeline_mode=pl.Buffered(1)),
                pl.BlockSpec((tile, half), lambda i, s: (i, 0)),
                pl.BlockSpec((8, tile), lambda i, s: (0, i)),
            ),
        ),
        compiler_params=pltpu.CompilerParams(vmem_limit_bytes=30 * 1024 * 1024),
        name="project",
    )(spot, *in_hbm(mine, got, memory, hidden, grad_out))


def gates_of(sums_refs, hidden_ref, grad_ref, key_proj_ref, both_ref):
    half = hidden_ref.shape[1]
    sums = sums_refs[0][...] + sums_refs[1][...] + sums_refs[2][...] + sums_refs[3][...]
    root_width = math.sqrt(D)
    key_scale = jnp.sqrt(sums[0:1, :] / D + norm_eps)
    gate_score = sums[1:2, :] / (key_scale * root_width)
    gate_value = 1.0 / (1.0 + jnp.exp(-gate_score))
    gate_grad = gate_value * (1.0 - gate_value) * sums[2:3, :]
    by_hidden = 1.0 / (key_scale * root_width)
    by_key = gate_score / (D * key_scale * key_scale)
    row = lax.broadcasted_iota(jnp.int32, (128, sums.shape[1]), 0)
    coded = jnp.where(
        row == 0,
        gate_value,
        jnp.where(row == 1, gate_grad, jnp.where(row == 2, by_hidden, by_key)),
    ).T
    hidden = hidden_ref[...].astype(jnp.float32)
    key_grad = coded[:, 1:2] * (hidden * coded[:, 2:3] - key_proj_ref[...] * coded[:, 3:4])
    value_grad = coded[:, 0:1] * grad_ref[...].astype(jnp.float32)
    both_ref[:, :half] = key_grad.astype(jnp.bfloat16)
    both_ref[:, half:] = value_grad.astype(jnp.bfloat16)


def grads_kernel(order_ref, *refs):
    both_ref, outs = refs[8], refs[9:]
    half = outs[0].shape[1]
    gates_of(refs[:4], *refs[4:7], both_ref)

    @pl.when(pl.program_id(0) < len(outs) // 2)
    def _():
        memory_grad = lax.dot_general(
            both_ref[...],
            refs[7][...],
            (((1,), (1,)), ((), ())),
            preferred_element_type=jnp.float32,
        ).astype(jnp.bfloat16)
        for k in range(len(outs) // 2):

            @pl.when(pl.program_id(0) == k)
            def _():
                outs[2 * k][...] = memory_grad[:, :half]
                outs[2 * k + 1][...] = memory_grad[:, half:]


def grads(order, products, sums, hidden, grad_out, key_proj, weights):
    steps = order.shape[0]
    tokens, half = hidden.shape
    tile = tokens // 4
    mem = weights.shape[0]
    at = lambda i, o: (o[i], 0)
    fixed = lambda i, o: (0, 0)
    one = pl.Buffered(1)
    if steps == 1:
        both_shape, both_spec = (tile, 2 * half), pl.BlockSpec((tile, 2 * half), fixed)
    else:
        both_shape, both_spec = (tokens, 2 * half), pl.BlockSpec((tile, 2 * half), at)
    return pl.pallas_call(
        grads_kernel,
        out_shape=(
            pltpu.HBM(both_shape, jnp.bfloat16),
            *([jax.ShapeDtypeStruct((tile, mem // 2), jnp.bfloat16)] * (2 * products)),
        ),
        grid_spec=pltpu.PrefetchScalarGridSpec(
            num_scalar_prefetch=1,
            grid=(steps,),
            in_specs=[pl.BlockSpec((8, tile), lambda i, o: (0, o[i]))] * 4
            + [pl.BlockSpec((tile, half), at)] * 3
            + [pl.BlockSpec(weights.shape, fixed, pipeline_mode=one)],
            out_specs=(
                both_spec,
                *([pl.BlockSpec((tile, mem // 2), fixed, pipeline_mode=one)] * (2 * products)),
            ),
        ),
        compiler_params=pltpu.CompilerParams(vmem_limit_bytes=26 * 1024 * 1024),
        name="grads_far" if steps == 1 else "grads_near",
    )(order, *sums, *in_hbm(hidden, grad_out, key_proj), weights)


SLOTS = 48
TILE = 256


def pack_kernel(tile_ref, spot_ref, l1, l2, l3, r1, r2, r3, out_ref, sum_ref, rows_ref):
    lookups, width = tile_ref.shape[0], out_ref.shape[1]
    tokens, half = l1.shape

    @pl.when(pl.program_id(0) == 0)
    def _():
        f32 = jnp.float32
        left = l1[...].astype(f32) + l2[...].astype(f32) + l3[...].astype(f32)
        right = r1[...].astype(f32) + r2[...].astype(f32) + r3[...].astype(f32)
        sum_ref[:, :half] = left.astype(jnp.bfloat16)
        sum_ref[:, half:] = right.astype(jnp.bfloat16)
        for l in range(lookups):
            rows_ref[l * tokens : (l + 1) * tokens, :] = sum_ref[:, l * width : (l + 1) * width]

    steps = out_ref.shape[0] // TILE
    place = lax.broadcasted_iota(jnp.int32, (TILE, lookups * tokens), 0).astype(jnp.bfloat16)
    one, zero = jnp.ones((), jnp.bfloat16), jnp.zeros((), jnp.bfloat16)
    hits = []
    for s in range(steps):
        here = pl.program_id(0) * steps + s
        spot = jnp.concatenate(
            [
                jnp.where(tile_ref[l : l + 1, :] == here, spot_ref[l : l + 1, :], -1)
                for l in range(lookups)
            ],
            axis=1,
        )
        spot = jnp.broadcast_to(spot.astype(jnp.bfloat16), place.shape)
        hits.append(jnp.where(place == spot, one, zero))
    out_ref[...] = jnp.dot(
        jnp.concatenate(hits, axis=0), rows_ref[...], preferred_element_type=jnp.float32
    ).astype(jnp.bfloat16)


def pack_rows(slot, parts, total_slots, width):
    per_step = 3 * TILE
    tokens, half = parts[0].shape
    lookups = slot.shape[0]
    return pl.pallas_call(
        pack_kernel,
        out_shape=jax.ShapeDtypeStruct((total_slots, width), jnp.bfloat16),
        grid=(total_slots // per_step,),
        in_specs=[pl.BlockSpec(slot.shape, lambda i: (0, 0))] * 2
        + [pl.BlockSpec((tokens, half), lambda i: (0, 0))] * 6,
        out_specs=pl.BlockSpec((per_step, width), lambda i: (i, 0)),
        scratch_shapes=[
            pltpu.VMEM((tokens, 2 * half), jnp.bfloat16),
            pltpu.VMEM((lookups * tokens, width), jnp.bfloat16),
        ],
        compiler_params=pltpu.CompilerParams(vmem_limit_bytes=26 * 1024 * 1024),
        name="pack_rows",
    )(slot // TILE, slot % TILE, *parts)


def adam_kernel(
    tile_ref, spot_ref, rows_ref, table_ref, first_ref, second_ref, new_table_ref, new_first_ref, new_second_ref
):
    steps = table_ref.shape[0] // TILE
    width = table_ref.shape[1]
    entries = rows_ref.shape[0]
    chunk = 1024
    place = lax.broadcasted_iota(jnp.int32, (TILE, chunk), 0).astype(jnp.bfloat16)
    one, zero = jnp.ones((), jnp.bfloat16), jnp.zeros((), jnp.bfloat16)
    for s in range(steps):
        here = pl.program_id(0) * steps + s
        grad = jnp.zeros((TILE, width), jnp.float32)
        for k in range(0, entries, chunk):
            spot = jnp.where(tile_ref[:, k : k + chunk] == here, spot_ref[:, k : k + chunk], -1)
            spot = jnp.broadcast_to(spot.astype(jnp.bfloat16), (TILE, chunk))
            hits = jnp.where(place == spot, one, zero)
            grad += jnp.dot(hits, rows_ref[k : k + chunk, :], preferred_element_type=jnp.float32)
        at = slice(s * TILE, (s + 1) * TILE)
        new_first = beta_one * first_ref[at, :] + (1.0 - beta_one) * grad
        new_second = beta_two * second_ref[at, :] + (1.0 - beta_two) * grad * grad
        stepped = new_first / correct_one / (jnp.sqrt(new_second / correct_two) + adam_eps)
        new_table_ref[at, :] = table_ref[at, :] - learn_rate * stepped
        new_first_ref[at, :] = new_first
        new_second_ref[at, :] = new_second


def adam_rows(got_ids, got_rows, embed_table, first_moment, second_moment):
    rows_dev, width = embed_table.shape
    per_step = 2 * TILE
    block = pl.BlockSpec((per_step, width), lambda i: (i, 0))
    ids = got_ids.reshape(1, -1)
    whole = pl.BlockSpec(ids.shape, lambda i: (0, 0))
    return pl.pallas_call(
        adam_kernel,
        out_shape=(jax.ShapeDtypeStruct((rows_dev, width), jnp.float32),) * 3,
        grid=(rows_dev // per_step,),
        in_specs=[
            whole,
            whole,
            pl.BlockSpec(got_rows.shape, lambda i: (0, 0)),
            block,
            block,
            block,
        ],
        out_specs=(block,) * 3,
        compiler_params=pltpu.CompilerParams(vmem_limit_bytes=26 * 1024 * 1024),
        name="adam_rows",
    )(ids // TILE, ids % TILE, got_rows, *in_hbm(embed_table, first_moment, second_moment))


def route(my_ids, owners, rows_dev):
    ids = my_ids.T
    lookups, tokens = ids.shape
    flat = ids.reshape(-1)
    entries = flat.shape[0]
    owner_of = flat // rows_dev
    local_row = flat % rows_dev
    owner_hits = (owner_of[:, None] == jnp.arange(owners, dtype=jnp.int32)[None, :]).astype(
        jnp.bfloat16
    )
    earlier = (jnp.arange(entries)[None, :] < jnp.arange(entries)[:, None]).astype(jnp.bfloat16)
    before_counts = jnp.dot(earlier, owner_hits, preferred_element_type=jnp.float32)
    slot_rank = jnp.sum(before_counts * owner_hits.astype(jnp.float32), axis=1).astype(jnp.int32)
    slot = (owner_of * SLOTS + slot_rank).reshape(lookups, tokens)
    rank_hits = slot_rank[:, None] == jnp.arange(SLOTS, dtype=jnp.int32)[None, :]
    low = local_row % 64
    high = local_row // 64
    values = jnp.concatenate(
        [
            jnp.where(rank_hits, v[:, None], 0).astype(jnp.bfloat16)
            for v in (high, low, jnp.ones_like(low))
        ],
        axis=1,
    )
    found = lax.dot_general(
        owner_hits, values, (((0,), (0,)), ((), ())), preferred_element_type=jnp.float32
    ).astype(jnp.int32)
    got_high, got_low, filled = jnp.split(found, 3, axis=1)
    send_ids = jnp.where(filled > 0, got_high * 64 + got_low, rows_dev)
    return slot, send_ids


def body(
    memory,
    hidden,
    grad_out,
    key_weight,
    value_weight,
    row_ids,
    embed_table,
    first_moment,
    second_moment,
):
    dp_count = lax.axis_size("dp")
    tensor_count = lax.axis_size("tensor")
    owners = dp_count * tensor_count
    rows_dev, row_width = embed_table.shape
    block_rows = memory.shape[0] // tensor_count
    my_ids = lax.dynamic_slice_in_dim(
        row_ids, lax.axis_index("tensor") * block_rows, block_rows, 0
    )
    at = lax.axis_index("dp")
    z = lax.axis_index("tensor")
    x, y, c = at // 8, (at // 2) % 4, at % 2
    slot, send_ids = route(my_ids, owners, rows_dev)
    mine, got_ids = gather_weights(key_weight, value_weight, send_ids)
    mine, got_ids, slot = lax.optimization_barrier((mine, got_ids, slot))
    mine = mine.reshape(2, 16, *key_weight.shape)
    got = lax.ppermute(mine, "dp", other_core())
    spot = jnp.stack([x, y, c]).astype(jnp.int32)
    weights, key_proj, sums = project(spot, mine, got, memory, hidden, grad_out)
    sums = [sums] + [lax.ppermute(sums, "tensor", along_z(d)) for d in STEPS]
    far = ((z + 2) % 4)[None].astype(jnp.int32)
    near = jnp.stack([(z + 1) % 4, (z + 3) % 4, z, (z + 2) % 4]).astype(jnp.int32)
    _, far_left, far_right = grads(far, 1, sums, hidden, grad_out, key_proj, weights)
    up = lax.ppermute(far_left, "tensor", along_z(1))
    down = lax.ppermute(far_right, "tensor", along_z(3))
    both, next_left, next_right, last_left, last_right, own_left, own_right = grads(
        near, 3, sums, hidden, grad_out, key_proj, weights
    )
    from_last_right = lax.ppermute(next_right, "tensor", along_z(1))
    from_next_left = lax.ppermute(last_left, "tensor", along_z(3))
    next_left = (up.astype(jnp.float32) + next_left.astype(jnp.float32)).astype(jnp.bfloat16)
    last_right = (down.astype(jnp.float32) + last_right.astype(jnp.float32)).astype(jnp.bfloat16)
    both, next_left, last_right = lax.optimization_barrier((both, next_left, last_right))
    from_last_left = lax.ppermute(next_left, "tensor", along_z(1))
    from_next_right = lax.ppermute(last_right, "tensor", along_z(3))
    weight_grads = lax.dot_general(
        memory, both, (((0,), (0,)), ((), ())), preferred_element_type=jnp.float32
    ).astype(jnp.bfloat16)
    sent, kept = core_halves(weight_grads, c)
    sent, kept, from_last_right, from_next_left = lax.optimization_barrier(
        (sent, kept, from_last_right, from_next_left)
    )
    chip_grads = sum_on_chip(sent, kept)
    chip_grads, slot, from_last_left, from_next_right = lax.optimization_barrier(
        (chip_grads, slot, from_last_left, from_next_right)
    )
    key_part, value_part = sum_one_axis(chip_grads, x, y)
    send_rows = pack_rows(
        slot,
        (own_left, from_last_left, from_next_left, own_right, from_last_right, from_next_right),
        owners * SLOTS,
        row_width,
    )
    key_weight_grad = ring_sum(key_part, y, along_y)
    value_weight_grad = ring_sum(value_part, x, along_x)
    got_rows = lax.all_to_all(
        send_rows.reshape(owners, SLOTS, row_width),
        ("dp", "tensor"),
        split_axis=0,
        concat_axis=0,
        tiled=True,
    )
    new_table, new_first, new_second = adam_rows(
        got_ids, got_rows.reshape(-1, row_width), embed_table, first_moment, second_moment
    )
    return (key_weight_grad, value_weight_grad, new_table, new_first, new_second)


def solution(mesh):
    return jax.shard_map(
        body,
        mesh=mesh,
        in_specs=(
            P("dp", None),
            P("dp", "tensor"),
            P("dp", "tensor"),
            P("dp", "tensor"),
            P("dp", "tensor"),
            P("dp", None),
            P(("dp", "tensor"), None),
            P(("dp", "tensor"), None),
            P(("dp", "tensor"), None),
        ),
        out_specs=(
            P("dp", "tensor"),
            P("dp", "tensor"),
            P(("dp", "tensor"), None),
            P(("dp", "tensor"), None),
            P(("dp", "tensor"), None),
        ),
        check_vma=False,
    )
```

```python
import math

import jax
import jax.numpy as jnp
from jax import lax
from jax.experimental import pallas as pl
from jax.experimental.pallas import tpu as pltpu
from jax.sharding import PartitionSpec as P

D = 2560


beta_one = 0.9
beta_two = 0.999
learn_rate = 0.01
adam_eps = 1e-08
norm_eps = 1e-06
correct_one = 0.9999734386011124
correct_two = 0.0952078528863


def dp_index(x, y, c):
    return (x % 4) * 8 + (y % 4) * 2 + c


def along_x(d):
    return [
        (dp_index(x, y, c), dp_index(x + d, y, c))
        for x in range(4)
        for y in range(4)
        for c in range(2)
    ]


def along_y(d):
    return [
        (dp_index(x, y, c), dp_index(x, y + d, c))
        for x in range(4)
        for y in range(4)
        for c in range(2)
    ]


def other_core():
    return [
        (dp_index(x, y, c), dp_index(x, y, 1 - c))
        for x in range(4)
        for y in range(4)
        for c in range(2)
    ]


def along_z(d):
    return [(z, (z + d) % 4) for z in range(4)]


STEPS = (1, 2, 3)


def in_hbm(*arrays):
    return tuple(pltpu.with_memory_space_constraint(a, pltpu.HBM) for a in arrays)


def ring_gather(shard, perm_of):
    return [shard] + [lax.ppermute(shard, "dp", perm_of(d)) for d in STEPS]


def ring_pieces(tiles, here, perm_of):
    own = lax.dynamic_index_in_dim(tiles, here, 0, keepdims=False)
    return [own] + [
        lax.ppermute(
            lax.dynamic_index_in_dim(tiles, (here + d) % 4, 0, keepdims=False), "dp", perm_of(d)
        )
        for d in STEPS
    ]


def ring_sum(tiles, here, perm_of):
    return sum(p.astype(jnp.float32) for p in ring_pieces(tiles, here, perm_of))


def gather_weights(key_weight, value_weight, row_ids):
    key_x = ring_gather(key_weight, along_x)
    value_y = ring_gather(value_weight, along_y)
    key_x = jnp.stack(key_x)
    value_y = jnp.stack(value_y)
    key_x, value_y, row_ids = lax.optimization_barrier((key_x, value_y, row_ids))
    key_all = ring_gather(key_x, along_y)
    value_all = ring_gather(value_y, along_x)
    return (jnp.stack([jnp.stack(key_all), jnp.stack(value_all)]), row_ids)


def core_halves(weight_grads, c):
    tiles = weight_grads.reshape(16, 2, -1, weight_grads.shape[1])
    sent = lax.dynamic_index_in_dim(tiles, 1 - c, 1, keepdims=False)
    kept = lax.dynamic_index_in_dim(tiles, c, 1, keepdims=False)
    return (sent, kept)


def sum_on_chip(sent, kept):
    got = lax.ppermute(sent, "dp", other_core())
    both = (kept.astype(jnp.float32) + got.astype(jnp.float32)).astype(jnp.bfloat16)
    return both.reshape(4, 4, *both.shape[1:])


def sum_one_axis(both, x, y):
    half = both.shape[3] // 2
    key_part = ring_sum(both[:, :, :, :half], x, along_x).astype(jnp.bfloat16)
    value_part = ring_sum(jnp.swapaxes(both[:, :, :, half:], 0, 1), y, along_y).astype(jnp.bfloat16)
    return (key_part, value_part)


def project_kernel(
    spot_ref, mine_ref, got_ref, memory_ref, hidden_ref, grad_ref, weight_ref, key_proj_ref, sums_ref
):
    half = hidden_ref.shape[1]

    @pl.when(pl.program_id(0) == 0)
    def _():
        x, y, c = spot_ref[0], spot_ref[1], spot_ref[2]
        rows = mine_ref.shape[2]
        for one in range(4):
            for two in range(4):
                for half_index in range(2):
                    a = mine_ref[half_index, one * 4 + two].astype(jnp.float32)
                    b = got_ref[half_index, one * 4 + two].astype(jnp.float32)
                    low = jnp.where(c == 0, a, b)
                    high = jnp.where(c == 0, b, a)
                    dx, dy = (two, one) if half_index == 0 else (one, two)
                    at = ((x + 4 - dx) % 4) * 4 + (y + 4 - dy) % 4
                    both = jnp.concatenate([low, high], axis=0).astype(jnp.bfloat16)
                    weight_ref[
                        pl.ds(pl.multiple_of(at * (2 * rows), 16), 2 * rows),
                        half_index * half : (half_index + 1) * half,
                    ] = both

    memory = memory_ref[...]
    key_proj = jnp.dot(memory, weight_ref[:, :half], preferred_element_type=jnp.float32)
    value_proj = jnp.dot(memory, weight_ref[:, half:], preferred_element_type=jnp.float32)
    key_proj_ref[...] = key_proj
    hidden = hidden_ref[...].astype(jnp.float32)
    grad = grad_ref[...].astype(jnp.float32)
    square_sum = jnp.sum(key_proj * key_proj, axis=1, keepdims=True)
    cross_sum = jnp.sum(hidden * key_proj, axis=1, keepdims=True)
    output_sum = jnp.sum(grad * value_proj, axis=1, keepdims=True)
    lane = lax.broadcasted_iota(jnp.int32, (memory.shape[0], 128), 1)
    sums = jnp.where(lane == 0, square_sum, jnp.where(lane == 1, cross_sum, output_sum))
    sums_ref[...] = sums.T[:8, :]


def project(spot, mine, got, memory, hidden, grad_out):
    tokens, mem = memory.shape
    half = hidden.shape[1]
    tile = tokens // 4
    fixed = lambda i, s: (0, 0)
    return pl.pallas_call(
        project_kernel,
        out_shape=(
            jax.ShapeDtypeStruct((mem, 2 * half), jnp.bfloat16),
            pltpu.HBM((tokens, half), jnp.float32),
            jax.ShapeDtypeStruct((8, tokens), jnp.float32),
        ),
        grid_spec=pltpu.PrefetchScalarGridSpec(
            num_scalar_prefetch=1,
            grid=(4,),
            in_specs=[
                pl.BlockSpec(mine.shape, lambda i, s: (0, 0, 0, 0), pipeline_mode=pl.Buffered(1)),
                pl.BlockSpec(got.shape, lambda i, s: (0, 0, 0, 0), pipeline_mode=pl.Buffered(1)),
                pl.BlockSpec((tile, mem), lambda i, s: (i, 0)),
                pl.BlockSpec((tile, half), lambda i, s: (i, 0)),
                pl.BlockSpec((tile, half), lambda i, s: (i, 0)),
            ],
            out_specs=(
                pl.BlockSpec((mem, 2 * half), fixed, pipeline_mode=pl.Buffered(1)),
                pl.BlockSpec((tile, half), lambda i, s: (i, 0)),
                pl.BlockSpec((8, tile), lambda i, s: (0, i)),
            ),
        ),
        compiler_params=pltpu.CompilerParams(vmem_limit_bytes=30 * 1024 * 1024),
        name="project",
    )(spot, *in_hbm(mine, got, memory, hidden, grad_out))


def gates_of(sums_refs, hidden_ref, grad_ref, key_proj_ref, both_ref):
    half = hidden_ref.shape[1]
    sums = sums_refs[0][...] + sums_refs[1][...] + sums_refs[2][...] + sums_refs[3][...]
    root_width = math.sqrt(D)
    key_scale = jnp.sqrt(sums[0:1, :] / D + norm_eps)
    gate_score = sums[1:2, :] / (key_scale * root_width)
    gate_value = 1.0 / (1.0 + jnp.exp(-gate_score))
    gate_grad = gate_value * (1.0 - gate_value) * sums[2:3, :]
    by_hidden = 1.0 / (key_scale * root_width)
    by_key = gate_score / (D * key_scale * key_scale)
    row = lax.broadcasted_iota(jnp.int32, (128, sums.shape[1]), 0)
    coded = jnp.where(
        row == 0,
        gate_value,
        jnp.where(row == 1, gate_grad, jnp.where(row == 2, by_hidden, by_key)),
    ).T
    hidden = hidden_ref[...].astype(jnp.float32)
    key_grad = coded[:, 1:2] * (hidden * coded[:, 2:3] - key_proj_ref[...] * coded[:, 3:4])
    value_grad = coded[:, 0:1] * grad_ref[...].astype(jnp.float32)
    both_ref[:, :half] = key_grad.astype(jnp.bfloat16)
    both_ref[:, half:] = value_grad.astype(jnp.bfloat16)


def grads_kernel(order_ref, *refs):
    both_ref, outs = refs[8], refs[9:]
    half = outs[0].shape[1]
    gates_of(refs[:4], *refs[4:7], both_ref)

    @pl.when(pl.program_id(0) < len(outs) // 2)
    def _():
        memory_grad = lax.dot_general(
            both_ref[...],
            refs[7][...],
            (((1,), (1,)), ((), ())),
            preferred_element_type=jnp.float32,
        ).astype(jnp.bfloat16)
        for k in range(len(outs) // 2):

            @pl.when(pl.program_id(0) == k)
            def _():
                outs[2 * k][...] = memory_grad[:, :half]
                outs[2 * k + 1][...] = memory_grad[:, half:]


def grads(order, products, sums, hidden, grad_out, key_proj, weights):
    steps = order.shape[0]
    tokens, half = hidden.shape
    tile = tokens // 4
    mem = weights.shape[0]
    at = lambda i, o: (o[i], 0)
    fixed = lambda i, o: (0, 0)
    one = pl.Buffered(1)
    if steps == 1:
        both_shape, both_spec = (tile, 2 * half), pl.BlockSpec((tile, 2 * half), fixed)
    else:
        both_shape, both_spec = (tokens, 2 * half), pl.BlockSpec((tile, 2 * half), at)
    return pl.pallas_call(
        grads_kernel,
        out_shape=(
            pltpu.HBM(both_shape, jnp.bfloat16),
            *([jax.ShapeDtypeStruct((tile, mem // 2), jnp.bfloat16)] * (2 * products)),
        ),
        grid_spec=pltpu.PrefetchScalarGridSpec(
            num_scalar_prefetch=1,
            grid=(steps,),
            in_specs=[pl.BlockSpec((8, tile), lambda i, o: (0, o[i]))] * 4
            + [pl.BlockSpec((tile, half), at)] * 3
            + [pl.BlockSpec(weights.shape, fixed, pipeline_mode=one)],
            out_specs=(
                both_spec,
                *([pl.BlockSpec((tile, mem // 2), fixed, pipeline_mode=one)] * (2 * products)),
            ),
        ),
        compiler_params=pltpu.CompilerParams(vmem_limit_bytes=26 * 1024 * 1024),
        name="grads_far" if steps == 1 else "grads_near",
    )(order, *sums, *in_hbm(hidden, grad_out, key_proj), weights)


SLOTS = 48
SLOT_CAP = 45
TILE = 256


def pack_kernel(tile_ref, spot_ref, numbers_ref, l1, l2, l3, r1, r2, r3, out_ref, sum_ref, rows_ref):
    width = out_ref.shape[1]
    tokens, half = l1.shape
    entries = tile_ref.shape[1]
    lookups = 2 * half // width

    @pl.when(pl.program_id(0) == 0)
    def _():
        f32 = jnp.float32
        left = l1[...].astype(f32) + l2[...].astype(f32) + l3[...].astype(f32)
        right = r1[...].astype(f32) + r2[...].astype(f32) + r3[...].astype(f32)
        sum_ref[:, :half] = left.astype(jnp.bfloat16)
        sum_ref[:, half:] = right.astype(jnp.bfloat16)
        for l in range(lookups):
            rows_ref[l * tokens : (l + 1) * tokens, :] = sum_ref[:, l * width : (l + 1) * width]
        rows_ref[lookups * tokens :, :] = numbers_ref[...]

    steps = out_ref.shape[0] // TILE
    place = lax.broadcasted_iota(jnp.int32, (TILE, entries), 0).astype(jnp.bfloat16)
    one, zero = jnp.ones((), jnp.bfloat16), jnp.zeros((), jnp.bfloat16)
    hits = []
    for s in range(steps):
        here = pl.program_id(0) * steps + s
        spot = jnp.where(tile_ref[...] == here, spot_ref[...], -1)
        spot = jnp.broadcast_to(spot.astype(jnp.bfloat16), place.shape)
        hits.append(jnp.where(place == spot, one, zero))
    out_ref[...] = jnp.dot(
        jnp.concatenate(hits, axis=0), rows_ref[...], preferred_element_type=jnp.float32
    ).astype(jnp.bfloat16)


def pack_rows(slot, numbers, parts, total_slots, width):
    per_step = 3 * TILE
    tokens, half = parts[0].shape
    fixed = lambda i: (0, 0)
    one = pl.Buffered(1)
    return pl.pallas_call(
        pack_kernel,
        out_shape=jax.ShapeDtypeStruct((total_slots, width), jnp.bfloat16),
        grid=(total_slots // per_step,),
        in_specs=[pl.BlockSpec(slot.shape, fixed)] * 2
        + [pl.BlockSpec(numbers.shape, fixed)]
        + [pl.BlockSpec((tokens, half), fixed, pipeline_mode=one)] * 6,
        out_specs=pl.BlockSpec((per_step, width), lambda i: (i, 0)),
        scratch_shapes=[
            pltpu.VMEM((tokens, 2 * half), jnp.bfloat16),
            pltpu.VMEM((slot.shape[1], width), jnp.bfloat16),
        ],
        compiler_params=pltpu.CompilerParams(vmem_limit_bytes=26 * 1024 * 1024),
        name="pack_rows",
    )(slot // TILE, slot % TILE, numbers, *parts)


def adam_kernel(
    tile_ref, spot_ref, rows_ref, table_ref, first_ref, second_ref, new_table_ref, new_first_ref, new_second_ref
):
    steps = table_ref.shape[0] // TILE
    width = table_ref.shape[1]
    entries = rows_ref.shape[0]
    chunk = 1024
    place = lax.broadcasted_iota(jnp.int32, (TILE, chunk), 0).astype(jnp.bfloat16)
    one, zero = jnp.ones((), jnp.bfloat16), jnp.zeros((), jnp.bfloat16)
    for s in range(steps):
        here = pl.program_id(0) * steps + s
        grad = jnp.zeros((TILE, width), jnp.float32)
        for k in range(0, entries, chunk):
            spot = jnp.where(tile_ref[:, k : k + chunk] == here, spot_ref[:, k : k + chunk], -1)
            spot = jnp.broadcast_to(spot.astype(jnp.bfloat16), (TILE, chunk))
            hits = jnp.where(place == spot, one, zero)
            grad += jnp.dot(hits, rows_ref[k : k + chunk, :], preferred_element_type=jnp.float32)
        at = slice(s * TILE, (s + 1) * TILE)
        new_first = beta_one * first_ref[at, :] + (1.0 - beta_one) * grad
        new_second = beta_two * second_ref[at, :] + (1.0 - beta_two) * grad * grad
        stepped = new_first / correct_one / (jnp.sqrt(new_second / correct_two) + adam_eps)
        new_table_ref[at, :] = table_ref[at, :] - learn_rate * stepped
        new_first_ref[at, :] = new_first
        new_second_ref[at, :] = new_second


def adam_rows(got, embed_table, first_moment, second_moment):
    rows_dev, width = embed_table.shape
    per_step = 2 * TILE
    block = pl.BlockSpec((per_step, width), lambda i: (i, 0))
    tile = got[:, SLOT_CAP, :SLOTS].astype(jnp.int32).reshape(1, -1)
    spot = got[:, SLOT_CAP + 1, :SLOTS].astype(jnp.int32).reshape(1, -1)
    got_rows = got.reshape(-1, width)
    whole = pl.BlockSpec(tile.shape, lambda i: (0, 0))
    return pl.pallas_call(
        adam_kernel,
        out_shape=(jax.ShapeDtypeStruct((rows_dev, width), jnp.float32),) * 3,
        grid=(rows_dev // per_step,),
        in_specs=[
            whole,
            whole,
            pl.BlockSpec(got_rows.shape, lambda i: (0, 0)),
            block,
            block,
            block,
        ],
        out_specs=(block,) * 3,
        compiler_params=pltpu.CompilerParams(vmem_limit_bytes=26 * 1024 * 1024),
        name="adam_rows",
    )(tile, spot, got_rows, *in_hbm(embed_table, first_moment, second_moment))


def route(my_ids, owners, rows_dev, row_width):
    ids = my_ids.T
    lookups, tokens = ids.shape
    flat = ids.reshape(-1)
    entries = flat.shape[0]
    owner_of = flat // rows_dev
    local_row = flat % rows_dev
    owner_hits = (owner_of[:, None] == jnp.arange(owners, dtype=jnp.int32)[None, :]).astype(
        jnp.bfloat16
    )
    earlier = (jnp.arange(entries)[None, :] < jnp.arange(entries)[:, None]).astype(jnp.bfloat16)
    before_counts = jnp.dot(earlier, owner_hits, preferred_element_type=jnp.float32)
    slot_rank = jnp.sum(before_counts * owner_hits.astype(jnp.float32), axis=1).astype(jnp.int32)
    slot = owner_of * SLOTS + slot_rank
    rank_hits = slot_rank[:, None] == jnp.arange(SLOTS, dtype=jnp.int32)[None, :]
    low = local_row % TILE
    high = local_row // TILE
    values = jnp.concatenate(
        [
            jnp.where(rank_hits, v[:, None], 0).astype(jnp.bfloat16)
            for v in (high, low, jnp.ones_like(low))
        ],
        axis=1,
    )
    found = lax.dot_general(
        owner_hits, values, (((0,), (0,)), ((), ())), preferred_element_type=jnp.float32
    )
    got_high, got_low, filled = jnp.split(found, 3, axis=1)
    got_high = jnp.where(filled > 0, got_high, rows_dev // TILE)
    numbers = jnp.concatenate([got_high, got_low], axis=0).astype(jnp.bfloat16)
    numbers = jnp.pad(numbers, ((0, 0), (0, row_width - SLOTS)))
    owner = jnp.arange(owners, dtype=jnp.int32) * SLOTS
    number_slot = jnp.concatenate([owner + SLOT_CAP, owner + SLOT_CAP + 1])
    return (jnp.concatenate([slot.reshape(1, -1), number_slot[None, :]], axis=1), numbers)


def body(
    memory,
    hidden,
    grad_out,
    key_weight,
    value_weight,
    row_ids,
    embed_table,
    first_moment,
    second_moment,
):
    dp_count = lax.axis_size("dp")
    tensor_count = lax.axis_size("tensor")
    owners = dp_count * tensor_count
    rows_dev, row_width = embed_table.shape
    block_rows = memory.shape[0] // tensor_count
    mine, row_ids = gather_weights(key_weight, value_weight, row_ids)
    my_ids = lax.dynamic_slice_in_dim(
        row_ids, lax.axis_index("tensor") * block_rows, block_rows, 0
    )
    at = lax.axis_index("dp")
    z = lax.axis_index("tensor")
    x, y, c = at // 8, (at // 2) % 4, at % 2
    slot, numbers = route(my_ids, owners, rows_dev, row_width)
    mine, numbers, slot = lax.optimization_barrier((mine, numbers, slot))
    mine = mine.reshape(2, 16, *key_weight.shape)
    got = lax.ppermute(mine, "dp", other_core())
    spot = jnp.stack([x, y, c]).astype(jnp.int32)
    weights, key_proj, sums = project(spot, mine, got, memory, hidden, grad_out)
    sums = [sums] + [lax.ppermute(sums, "tensor", along_z(d)) for d in STEPS]
    far = ((z + 2) % 4)[None].astype(jnp.int32)
    near = jnp.stack([(z + 1) % 4, (z + 3) % 4, z, (z + 2) % 4]).astype(jnp.int32)
    _, far_left, far_right = grads(far, 1, sums, hidden, grad_out, key_proj, weights)
    up = lax.ppermute(far_left, "tensor", along_z(1))
    down = lax.ppermute(far_right, "tensor", along_z(3))
    both, next_left, next_right, last_left, last_right, own_left, own_right = grads(
        near, 3, sums, hidden, grad_out, key_proj, weights
    )
    from_last_right = lax.ppermute(next_right, "tensor", along_z(1))
    from_next_left = lax.ppermute(last_left, "tensor", along_z(3))
    next_left = (up.astype(jnp.float32) + next_left.astype(jnp.float32)).astype(jnp.bfloat16)
    last_right = (down.astype(jnp.float32) + last_right.astype(jnp.float32)).astype(jnp.bfloat16)
    both, next_left, last_right = lax.optimization_barrier((both, next_left, last_right))
    from_last_left = lax.ppermute(next_left, "tensor", along_z(1))
    from_next_right = lax.ppermute(last_right, "tensor", along_z(3))
    weight_grads = lax.dot_general(
        memory, both, (((0,), (0,)), ((), ())), preferred_element_type=jnp.float32
    ).astype(jnp.bfloat16)
    sent, kept = core_halves(weight_grads, c)
    sent, kept, from_last_right, from_next_left = lax.optimization_barrier(
        (sent, kept, from_last_right, from_next_left)
    )
    chip_grads = sum_on_chip(sent, kept)
    chip_grads, slot, from_last_left, from_next_right = lax.optimization_barrier(
        (chip_grads, slot, from_last_left, from_next_right)
    )
    key_part, value_part = sum_one_axis(chip_grads, x, y)
    send_rows = pack_rows(
        slot,
        numbers,
        (own_left, from_last_left, from_next_left, own_right, from_last_right, from_next_right),
        owners * SLOTS,
        row_width,
    )
    send_rows, key_part, value_part = lax.optimization_barrier((send_rows, key_part, value_part))
    key_pieces = ring_pieces(key_part, y, along_y)
    value_pieces = ring_pieces(value_part, x, along_x)
    got_rows = lax.all_to_all(
        send_rows.reshape(owners, SLOTS, row_width),
        ("dp", "tensor"),
        split_axis=0,
        concat_axis=0,
        tiled=True,
    )
    new_table, new_first, new_second = adam_rows(
        got_rows, embed_table, first_moment, second_moment
    )
    key_pieces, value_pieces, new_second = lax.optimization_barrier(
        (key_pieces, value_pieces, new_second)
    )
    key_weight_grad = sum(p.astype(jnp.float32) for p in key_pieces)
    value_weight_grad = sum(p.astype(jnp.float32) for p in value_pieces)
    return (key_weight_grad, value_weight_grad, new_table, new_first, new_second)


def solution(mesh):
    return jax.shard_map(
        body,
        mesh=mesh,
        in_specs=(
            P("dp", None),
            P("dp", "tensor"),
            P("dp", "tensor"),
            P("dp", "tensor"),
            P("dp", "tensor"),
            P("dp", None),
            P(("dp", "tensor"), None),
            P(("dp", "tensor"), None),
            P(("dp", "tensor"), None),
        ),
        out_specs=(
            P("dp", "tensor"),
            P("dp", "tensor"),
            P(("dp", "tensor"), None),
            P(("dp", "tensor"), None),
            P(("dp", "tensor"), None),
        ),
        check_vma=False,
    )
```

```python
import math

import jax
import jax.numpy as jnp
from jax import lax
from jax.experimental import pallas as pl
from jax.experimental.pallas import tpu as pltpu
from jax.sharding import PartitionSpec as P

D = 2560


beta_one = 0.9
beta_two = 0.999
learn_rate = 0.01
adam_eps = 1e-08
norm_eps = 1e-06
correct_one = 0.9999734386011124
correct_two = 0.0952078528863


def dp_index(x, y, c):
    return (x % 4) * 8 + (y % 4) * 2 + c


def along_x(d):
    return [
        (dp_index(x, y, c), dp_index(x + d, y, c))
        for x in range(4)
        for y in range(4)
        for c in range(2)
    ]


def along_y(d):
    return [
        (dp_index(x, y, c), dp_index(x, y + d, c))
        for x in range(4)
        for y in range(4)
        for c in range(2)
    ]


def other_core():
    return [
        (dp_index(x, y, c), dp_index(x, y, 1 - c))
        for x in range(4)
        for y in range(4)
        for c in range(2)
    ]


def along_z(d):
    return [(z, (z + d) % 4) for z in range(4)]


STEPS = (1, 2, 3)


def in_hbm(*arrays):
    return tuple(pltpu.with_memory_space_constraint(a, pltpu.HBM) for a in arrays)


def ring_gather(shard, perm_of):
    return [shard] + [lax.ppermute(shard, "dp", perm_of(d)) for d in STEPS]


def ring_pieces(tiles, here, perm_of):
    own = lax.dynamic_index_in_dim(tiles, here, 0, keepdims=False)
    return [own] + [
        lax.ppermute(
            lax.dynamic_index_in_dim(tiles, (here + d) % 4, 0, keepdims=False), "dp", perm_of(d)
        )
        for d in STEPS
    ]


def ring_sum(tiles, here, perm_of):
    return sum(p.astype(jnp.float32) for p in ring_pieces(tiles, here, perm_of))


def gather_weights(key_weight, value_weight, row_ids):
    key_x = ring_gather(key_weight, along_x)
    value_y = ring_gather(value_weight, along_y)
    key_x = jnp.stack(key_x)
    value_y = jnp.stack(value_y)
    key_x, value_y, row_ids = lax.optimization_barrier((key_x, value_y, row_ids))
    key_all = ring_gather(key_x, along_y)
    value_all = ring_gather(value_y, along_x)
    return (jnp.stack([jnp.stack(key_all), jnp.stack(value_all)]), row_ids)


def sum_on_chip(sent, kept):
    got = lax.ppermute(sent, "dp", other_core())
    both = (kept.astype(jnp.float32) + got.astype(jnp.float32)).astype(jnp.bfloat16)
    return both.reshape(4, 4, *both.shape[1:])


def project_kernel(
    spot_ref, mine_ref, got_ref, memory_ref, hidden_ref, grad_ref, weight_ref, key_proj_ref, sums_ref
):
    half = hidden_ref.shape[1]

    @pl.when(pl.program_id(0) == 0)
    def _():
        x, y, c = spot_ref[0], spot_ref[1], spot_ref[2]
        rows = mine_ref.shape[2]
        for one in range(4):
            for two in range(4):
                for half_index in range(2):
                    a = mine_ref[half_index, one * 4 + two].astype(jnp.float32)
                    b = got_ref[half_index, one * 4 + two].astype(jnp.float32)
                    low = jnp.where(c == 0, a, b)
                    high = jnp.where(c == 0, b, a)
                    dx, dy = (two, one) if half_index == 0 else (one, two)
                    at = ((x + 4 - dx) % 4) * 4 + (y + 4 - dy) % 4
                    both = jnp.concatenate([low, high], axis=0).astype(jnp.bfloat16)
                    weight_ref[
                        pl.ds(pl.multiple_of(at * (2 * rows), 16), 2 * rows),
                        half_index * half : (half_index + 1) * half,
                    ] = both

    memory = memory_ref[...]
    key_proj = jnp.dot(memory, weight_ref[:, :half], preferred_element_type=jnp.float32)
    value_proj = jnp.dot(memory, weight_ref[:, half:], preferred_element_type=jnp.float32)
    key_proj_ref[...] = key_proj
    hidden = hidden_ref[...].astype(jnp.float32)
    grad = grad_ref[...].astype(jnp.float32)
    square_sum = jnp.sum(key_proj * key_proj, axis=1, keepdims=True)
    cross_sum = jnp.sum(hidden * key_proj, axis=1, keepdims=True)
    output_sum = jnp.sum(grad * value_proj, axis=1, keepdims=True)
    lane = lax.broadcasted_iota(jnp.int32, (memory.shape[0], 128), 1)
    sums = jnp.where(lane == 0, square_sum, jnp.where(lane == 1, cross_sum, output_sum))
    sums_ref[...] = sums.T[:8, :]


def project(spot, mine, got, memory, hidden, grad_out):
    tokens, mem = memory.shape
    half = hidden.shape[1]
    tile = tokens // 2
    fixed = lambda i, s: (0, 0)
    return pl.pallas_call(
        project_kernel,
        out_shape=(
            jax.ShapeDtypeStruct((mem, 2 * half), jnp.bfloat16),
            pltpu.HBM((tokens, half), jnp.float32),
            jax.ShapeDtypeStruct((8, tokens), jnp.float32),
        ),
        grid_spec=pltpu.PrefetchScalarGridSpec(
            num_scalar_prefetch=1,
            grid=(2,),
            in_specs=[
                pl.BlockSpec(mine.shape, lambda i, s: (0, 0, 0, 0), pipeline_mode=pl.Buffered(1)),
                pl.BlockSpec(got.shape, lambda i, s: (0, 0, 0, 0), pipeline_mode=pl.Buffered(1)),
                pl.BlockSpec((tile, mem), lambda i, s: (i, 0)),
                pl.BlockSpec((tile, half), lambda i, s: (i, 0)),
                pl.BlockSpec((tile, half), lambda i, s: (i, 0)),
            ],
            out_specs=(
                pl.BlockSpec((mem, 2 * half), fixed, pipeline_mode=pl.Buffered(1)),
                pl.BlockSpec((tile, half), lambda i, s: (i, 0)),
                pl.BlockSpec((8, tile), lambda i, s: (0, i)),
            ),
        ),
        compiler_params=pltpu.CompilerParams(vmem_limit_bytes=36 * 1024 * 1024),
        name="project",
    )(spot, *in_hbm(mine, got, memory, hidden, grad_out))


def gates_of(sums_refs, hidden_ref, grad_ref, key_proj_ref, both_ref):
    half = hidden_ref.shape[1]
    sums = sums_refs[0][...] + sums_refs[1][...] + sums_refs[2][...] + sums_refs[3][...]
    root_width = math.sqrt(D)
    key_scale = jnp.sqrt(sums[0:1, :] / D + norm_eps)
    gate_score = sums[1:2, :] / (key_scale * root_width)
    gate_value = 1.0 / (1.0 + jnp.exp(-gate_score))
    gate_grad = gate_value * (1.0 - gate_value) * sums[2:3, :]
    by_hidden = 1.0 / (key_scale * root_width)
    by_key = gate_score / (D * key_scale * key_scale)
    row = lax.broadcasted_iota(jnp.int32, (128, sums.shape[1]), 0)
    coded = jnp.where(
        row == 0,
        gate_value,
        jnp.where(row == 1, gate_grad, jnp.where(row == 2, by_hidden, by_key)),
    ).T
    hidden = hidden_ref[...].astype(jnp.float32)
    key_grad = coded[:, 1:2] * (hidden * coded[:, 2:3] - key_proj_ref[...] * coded[:, 3:4])
    value_grad = coded[:, 0:1] * grad_ref[...].astype(jnp.float32)
    both_ref[:, :half] = key_grad.astype(jnp.bfloat16)
    both_ref[:, half:] = value_grad.astype(jnp.bfloat16)


def grads_kernel(order_ref, *refs):
    outs, both_ref = refs[8:-1], refs[-1]
    half = outs[0].shape[1]
    gates_of(refs[:4], *refs[4:7], both_ref)
    memory_grad = lax.dot_general(
        both_ref[...],
        refs[7][...],
        (((1,), (1,)), ((), ())),
        preferred_element_type=jnp.float32,
    ).astype(jnp.bfloat16)
    for k in range(len(outs) // 2):

        @pl.when(pl.program_id(0) == k)
        def _():
            outs[2 * k][...] = memory_grad[:, :half]
            outs[2 * k + 1][...] = memory_grad[:, half:]


def grads(order, sums, hidden, grad_out, key_proj, weights):
    steps = order.shape[0]
    tokens, half = hidden.shape
    tile = tokens // 4
    mem = weights.shape[0]
    at = lambda i, o: (o[i], 0)
    fixed = lambda i, o: (0, 0)
    one = pl.Buffered(1)
    return pl.pallas_call(
        grads_kernel,
        out_shape=(pltpu.HBM((tile, mem // 2), jnp.bfloat16),) * (2 * steps),
        grid_spec=pltpu.PrefetchScalarGridSpec(
            num_scalar_prefetch=1,
            grid=(steps,),
            in_specs=[pl.BlockSpec((8, tile), lambda i, o: (0, o[i]))] * 4
            + [pl.BlockSpec((tile, half), at)] * 3
            + [pl.BlockSpec(weights.shape, fixed, pipeline_mode=one)],
            out_specs=(pl.BlockSpec((tile, mem // 2), fixed, pipeline_mode=one),) * (2 * steps),
            scratch_shapes=[pltpu.VMEM((tile, 2 * half), jnp.bfloat16)],
        ),
        compiler_params=pltpu.CompilerParams(vmem_limit_bytes=26 * 1024 * 1024),
        name="grads_far" if steps == 1 else "grads_near",
    )(order, *sums, *in_hbm(hidden, grad_out, key_proj), weights)


def own_kernel(order_ref, *refs):
    memory_ref = refs[8]
    left_ref, right_ref, sent_ref, kept_ref, both_ref, total_ref = refs[9:]
    half = left_ref.shape[1]
    step = pl.program_id(0)
    gates_of(refs[:4], *refs[4:7], both_ref)
    product = lax.dot_general(
        memory_ref[...],
        both_ref[...],
        (((0,), (0,)), ((), ())),
        preferred_element_type=jnp.float32,
    )

    @pl.when(step == 0)
    def _():
        memory_grad = lax.dot_general(
            both_ref[...],
            refs[7][...],
            (((1,), (1,)), ((), ())),
            preferred_element_type=jnp.float32,
        ).astype(jnp.bfloat16)
        left_ref[...] = memory_grad[:, :half]
        right_ref[...] = memory_grad[:, half:]
        total_ref[...] = product

    @pl.when(step > 0)
    def _():
        total_ref[...] += product

    @pl.when(step == pl.num_programs(0) - 1)
    def _():
        first = order_ref[4] == 0
        rows = sent_ref.shape[1]
        for k in range(sent_ref.shape[0]):
            low = total_ref[2 * k * rows : (2 * k + 1) * rows, :]
            high = total_ref[(2 * k + 1) * rows : (2 * k + 2) * rows, :]
            sent_ref[k] = jnp.where(first, high, low).astype(jnp.bfloat16)
            kept_ref[k] = jnp.where(first, low, high).astype(jnp.bfloat16)


def own_grads(order, rows, sums, hidden, grad_out, key_proj, weights, memory):
    tokens, half = hidden.shape
    tile = tokens // 4
    mem = weights.shape[0]
    at = lambda i, o: (o[i], 0)
    fixed = lambda i, o: (0, 0)
    fixed_three = lambda i, o: (0, 0, 0)
    one = pl.Buffered(1)
    halves = (mem // (2 * rows), rows, 2 * half)
    return pl.pallas_call(
        own_kernel,
        out_shape=(pltpu.HBM((tile, mem // 2), jnp.bfloat16),) * 2
        + (pltpu.HBM(halves, jnp.bfloat16),) * 2,
        grid_spec=pltpu.PrefetchScalarGridSpec(
            num_scalar_prefetch=1,
            grid=(4,),
            in_specs=[pl.BlockSpec((8, tile), lambda i, o: (0, o[i]))] * 4
            + [pl.BlockSpec((tile, half), at)] * 3
            + [pl.BlockSpec(weights.shape, fixed, pipeline_mode=one)]
            + [pl.BlockSpec((tile, mem), at)],
            out_specs=(pl.BlockSpec((tile, mem // 2), fixed, pipeline_mode=one),) * 2
            + (pl.BlockSpec(halves, fixed_three, pipeline_mode=one),) * 2,
            scratch_shapes=[
                pltpu.VMEM((tile, 2 * half), jnp.bfloat16),
                pltpu.VMEM((mem, 2 * half), jnp.float32),
            ],
        ),
        compiler_params=pltpu.CompilerParams(vmem_limit_bytes=36 * 1024 * 1024),
        name="grads_own",
    )(order, *sums, *in_hbm(hidden, grad_out, key_proj), weights, *in_hbm(memory))


SLOTS = 48
SLOT_CAP = 45
TILE = 256


def pack_kernel(tile_ref, spot_ref, numbers_ref, l1, l2, l3, r1, r2, r3, out_ref, sum_ref, rows_ref):
    width = out_ref.shape[1]
    tokens, half = l1.shape
    entries = tile_ref.shape[1]
    lookups = 2 * half // width

    @pl.when(pl.program_id(0) == 0)
    def _():
        f32 = jnp.float32
        left = l1[...].astype(f32) + l2[...].astype(f32) + l3[...].astype(f32)
        right = r1[...].astype(f32) + r2[...].astype(f32) + r3[...].astype(f32)
        sum_ref[:, :half] = left.astype(jnp.bfloat16)
        sum_ref[:, half:] = right.astype(jnp.bfloat16)
        for l in range(lookups):
            rows_ref[l * tokens : (l + 1) * tokens, :] = sum_ref[:, l * width : (l + 1) * width]
        rows_ref[lookups * tokens :, :] = numbers_ref[...]

    steps = out_ref.shape[0] // TILE
    place = lax.broadcasted_iota(jnp.int32, (TILE, entries), 0).astype(jnp.bfloat16)
    one, zero = jnp.ones((), jnp.bfloat16), jnp.zeros((), jnp.bfloat16)
    hits = []
    for s in range(steps):
        here = pl.program_id(0) * steps + s
        spot = jnp.where(tile_ref[...] == here, spot_ref[...], -1)
        spot = jnp.broadcast_to(spot.astype(jnp.bfloat16), place.shape)
        hits.append(jnp.where(place == spot, one, zero))
    out_ref[...] = jnp.dot(
        jnp.concatenate(hits, axis=0), rows_ref[...], preferred_element_type=jnp.float32
    ).astype(jnp.bfloat16)


def pack_rows(slot, numbers, parts, total_slots, width):
    per_step = 3 * TILE
    tokens, half = parts[0].shape
    fixed = lambda i: (0, 0)
    one = pl.Buffered(1)
    return pl.pallas_call(
        pack_kernel,
        out_shape=pltpu.HBM((total_slots, width), jnp.bfloat16),
        grid=(total_slots // per_step,),
        in_specs=[pl.BlockSpec(slot.shape, fixed)] * 2
        + [pl.BlockSpec(numbers.shape, fixed)]
        + [pl.BlockSpec((tokens, half), fixed, pipeline_mode=one)] * 6,
        out_specs=pl.BlockSpec((per_step, width), lambda i: (i, 0)),
        scratch_shapes=[
            pltpu.VMEM((tokens, 2 * half), jnp.bfloat16),
            pltpu.VMEM((slot.shape[1], width), jnp.bfloat16),
        ],
        compiler_params=pltpu.CompilerParams(vmem_limit_bytes=26 * 1024 * 1024),
        name="pack_rows",
    )(slot // TILE, slot % TILE, numbers, *parts)


def adam_kernel(
    tile_ref, spot_ref, rows_ref, table_ref, first_ref, second_ref, new_table_ref, new_first_ref, new_second_ref
):
    steps = table_ref.shape[0] // TILE
    entries = rows_ref.shape[0]
    chunk = 2048
    place = lax.broadcasted_iota(jnp.int32, (TILE, chunk), 0).astype(jnp.bfloat16)
    one, zero = jnp.ones((), jnp.bfloat16), jnp.zeros((), jnp.bfloat16)
    grad = jnp.zeros(table_ref.shape, jnp.float32)
    for k in range(0, entries, chunk):
        hits = []
        for s in range(steps):
            here = pl.program_id(0) * steps + s
            spot = jnp.where(tile_ref[:, k : k + chunk] == here, spot_ref[:, k : k + chunk], -1)
            spot = jnp.broadcast_to(spot.astype(jnp.bfloat16), (TILE, chunk))
            hits.append(jnp.where(place == spot, one, zero))
        grad += jnp.dot(
            jnp.concatenate(hits, axis=0),
            rows_ref[k : k + chunk, :],
            preferred_element_type=jnp.float32,
        )
    new_first = beta_one * first_ref[...] + (1.0 - beta_one) * grad
    new_second = beta_two * second_ref[...] + (1.0 - beta_two) * grad * grad
    stepped = new_first / correct_one / (jnp.sqrt(new_second / correct_two) + adam_eps)
    new_table_ref[...] = table_ref[...] - learn_rate * stepped
    new_first_ref[...] = new_first
    new_second_ref[...] = new_second


def adam_rows(got, embed_table, first_moment, second_moment):
    rows_dev, width = embed_table.shape
    per_step = 2 * TILE
    block = pl.BlockSpec((per_step, width), lambda i: (i, 0))
    tile = got[:, SLOT_CAP, :SLOTS].astype(jnp.int32).reshape(1, -1)
    spot = got[:, SLOT_CAP + 1, :SLOTS].astype(jnp.int32).reshape(1, -1)
    got_rows = got.reshape(-1, width)
    whole = pl.BlockSpec(tile.shape, lambda i: (0, 0))
    return pl.pallas_call(
        adam_kernel,
        out_shape=(jax.ShapeDtypeStruct((rows_dev, width), jnp.float32),) * 3,
        grid=(rows_dev // per_step,),
        in_specs=[
            whole,
            whole,
            pl.BlockSpec(got_rows.shape, lambda i: (0, 0)),
            block,
            block,
            block,
        ],
        out_specs=(block,) * 3,
        compiler_params=pltpu.CompilerParams(vmem_limit_bytes=26 * 1024 * 1024),
        name="adam_rows",
    )(tile, spot, got_rows, *in_hbm(embed_table, first_moment, second_moment))


def route(my_ids, owners, rows_dev, row_width):
    ids = my_ids.T
    lookups, tokens = ids.shape
    flat = ids.reshape(-1)
    entries = flat.shape[0]
    owner_of = flat // rows_dev
    local_row = flat % rows_dev
    owner_hits = (owner_of[:, None] == jnp.arange(owners, dtype=jnp.int32)[None, :]).astype(
        jnp.bfloat16
    )
    earlier = (jnp.arange(entries)[None, :] < jnp.arange(entries)[:, None]).astype(jnp.bfloat16)
    before_counts = jnp.dot(earlier, owner_hits, preferred_element_type=jnp.float32)
    slot_rank = jnp.sum(before_counts * owner_hits.astype(jnp.float32), axis=1).astype(jnp.int32)
    slot = owner_of * SLOTS + slot_rank
    rank_hits = slot_rank[:, None] == jnp.arange(SLOTS, dtype=jnp.int32)[None, :]
    low = local_row % TILE
    high = local_row // TILE
    values = jnp.concatenate(
        [
            jnp.where(rank_hits, v[:, None], 0).astype(jnp.bfloat16)
            for v in (high, low, jnp.ones_like(low))
        ],
        axis=1,
    )
    found = lax.dot_general(
        owner_hits, values, (((0,), (0,)), ((), ())), preferred_element_type=jnp.float32
    )
    got_high, got_low, filled = jnp.split(found, 3, axis=1)
    got_high = jnp.where(filled > 0, got_high, rows_dev // TILE)
    numbers = jnp.concatenate([got_high, got_low], axis=0).astype(jnp.bfloat16)
    numbers = jnp.pad(numbers, ((0, 0), (0, row_width - SLOTS)))
    owner = jnp.arange(owners, dtype=jnp.int32) * SLOTS
    number_slot = jnp.concatenate([owner + SLOT_CAP, owner + SLOT_CAP + 1])
    return (jnp.concatenate([slot.reshape(1, -1), number_slot[None, :]], axis=1), numbers)


def body(
    memory,
    hidden,
    grad_out,
    key_weight,
    value_weight,
    row_ids,
    embed_table,
    first_moment,
    second_moment,
):
    dp_count = lax.axis_size("dp")
    tensor_count = lax.axis_size("tensor")
    owners = dp_count * tensor_count
    rows_dev, row_width = embed_table.shape
    block_rows = memory.shape[0] // tensor_count
    mine, row_ids = gather_weights(key_weight, value_weight, row_ids)
    my_ids = lax.dynamic_slice_in_dim(
        row_ids, lax.axis_index("tensor") * block_rows, block_rows, 0
    )
    at = lax.axis_index("dp")
    z = lax.axis_index("tensor")
    x, y, c = at // 8, (at // 2) % 4, at % 2
    slot, numbers = route(my_ids, owners, rows_dev, row_width)
    mine, numbers, slot = lax.optimization_barrier((mine, numbers, slot))
    mine = mine.reshape(2, 16, *key_weight.shape)
    got = lax.ppermute(mine, "dp", other_core())
    spot = jnp.stack([x, y, c]).astype(jnp.int32)
    weights, key_proj, sums = project(spot, mine, got, memory, hidden, grad_out)
    sums = [sums] + [lax.ppermute(sums, "tensor", along_z(d)) for d in STEPS]
    far = ((z + 2) % 4)[None].astype(jnp.int32)
    near = jnp.stack([(z + 1) % 4, (z + 3) % 4]).astype(jnp.int32)
    own = jnp.stack([z, (z + 2) % 4, (z + 1) % 4, (z + 3) % 4, c]).astype(jnp.int32)
    known = (sums, hidden, grad_out, key_proj, weights)
    far_left, far_right = grads(far, *known)
    far_left, far_right, near = lax.optimization_barrier((far_left, far_right, near))
    up = lax.ppermute(far_left, "tensor", along_z(1))
    down = lax.ppermute(far_right, "tensor", along_z(3))
    next_left, next_right, last_left, last_right = grads(near, *known)
    from_last_right = lax.ppermute(next_right, "tensor", along_z(1))
    from_next_left = lax.ppermute(last_left, "tensor", along_z(3))
    next_left = (up.astype(jnp.float32) + next_left.astype(jnp.float32)).astype(jnp.bfloat16)
    last_right = (down.astype(jnp.float32) + last_right.astype(jnp.float32)).astype(jnp.bfloat16)
    next_left, last_right, own = lax.optimization_barrier((next_left, last_right, own))
    own_left, own_right, sent, kept = own_grads(own, key_weight.shape[0], *known, memory)
    sent, kept, from_last_right, from_next_left = lax.optimization_barrier(
        (sent, kept, from_last_right, from_next_left)
    )
    from_last_left = lax.ppermute(next_left, "tensor", along_z(1))
    from_next_right = lax.ppermute(last_right, "tensor", along_z(3))
    chip_grads = sum_on_chip(sent, kept)
    half = chip_grads.shape[3] // 2
    key_chip = chip_grads[:, :, :, :half]
    value_chip = jnp.swapaxes(chip_grads[:, :, :, half:], 0, 1)
    key_part = ring_sum(key_chip, x, along_x).astype(jnp.bfloat16)
    slot, key_part, value_chip, from_last_left, from_next_right = lax.optimization_barrier(
        (slot, key_part, value_chip, from_last_left, from_next_right)
    )
    value_part = ring_sum(value_chip, y, along_y).astype(jnp.bfloat16)
    send_rows = pack_rows(
        slot,
        numbers,
        (own_left, from_last_left, from_next_left, own_right, from_last_right, from_next_right),
        owners * SLOTS,
        row_width,
    )
    send_rows, key_part, value_part = lax.optimization_barrier((send_rows, key_part, value_part))
    key_pieces = ring_pieces(key_part, y, along_y)
    value_pieces = ring_pieces(value_part, x, along_x)
    got_rows = lax.all_to_all(
        send_rows.reshape(owners, SLOTS, row_width),
        ("dp", "tensor"),
        split_axis=0,
        concat_axis=0,
        tiled=True,
    )
    new_table, new_first, new_second = adam_rows(
        got_rows, embed_table, first_moment, second_moment
    )
    key_pieces, value_pieces, new_second = lax.optimization_barrier(
        (key_pieces, value_pieces, new_second)
    )
    key_weight_grad = sum(p.astype(jnp.float32) for p in key_pieces)
    value_weight_grad = sum(p.astype(jnp.float32) for p in value_pieces)
    return (key_weight_grad, value_weight_grad, new_table, new_first, new_second)


def solution(mesh):
    return jax.shard_map(
        body,
        mesh=mesh,
        in_specs=(
            P("dp", None),
            P("dp", "tensor"),
            P("dp", "tensor"),
            P("dp", "tensor"),
            P("dp", "tensor"),
            P("dp", None),
            P(("dp", "tensor"), None),
            P(("dp", "tensor"), None),
            P(("dp", "tensor"), None),
        ),
        out_specs=(
            P("dp", "tensor"),
            P("dp", "tensor"),
            P(("dp", "tensor"), None),
            P(("dp", "tensor"), None),
            P(("dp", "tensor"), None),
        ),
        check_vma=False,
    )
```

```python
import math

import jax
import jax.numpy as jnp
from jax import lax
from jax.experimental import pallas as pl
from jax.experimental.pallas import tpu as pltpu
from jax.sharding import PartitionSpec as P

D = 2560


beta_one = 0.9
beta_two = 0.999
learn_rate = 0.01
adam_eps = 1e-08
norm_eps = 1e-06
correct_one = 0.9999734386011124
correct_two = 0.0952078528863


def dp_index(x, y, c):
    return (x % 4) * 8 + (y % 4) * 2 + c


def along_x(d):
    return [
        (dp_index(x, y, c), dp_index(x + d, y, c))
        for x in range(4)
        for y in range(4)
        for c in range(2)
    ]


def along_y(d):
    return [
        (dp_index(x, y, c), dp_index(x, y + d, c))
        for x in range(4)
        for y in range(4)
        for c in range(2)
    ]


def other_core():
    return [
        (dp_index(x, y, c), dp_index(x, y, 1 - c))
        for x in range(4)
        for y in range(4)
        for c in range(2)
    ]


def along_z(d):
    return [(z, (z + d) % 4) for z in range(4)]


STEPS = (1, 2, 3)


def in_hbm(*arrays):
    return tuple(pltpu.with_memory_space_constraint(a, pltpu.HBM) for a in arrays)


def ring_gather(shard, perm_of):
    return [shard] + [lax.ppermute(shard, "dp", perm_of(d)) for d in STEPS]


def ring_pieces(tiles, here, perm_of):
    own = lax.dynamic_index_in_dim(tiles, here, 0, keepdims=False)
    return [own] + [
        lax.ppermute(
            lax.dynamic_index_in_dim(tiles, (here + d) % 4, 0, keepdims=False), "dp", perm_of(d)
        )
        for d in STEPS
    ]


def ring_sum(tiles, here, perm_of):
    return sum(p.astype(jnp.float32) for p in ring_pieces(tiles, here, perm_of))


def gather_weights(key_weight, value_weight, row_ids):
    key_x = ring_gather(key_weight, along_x)
    value_y = ring_gather(value_weight, along_y)
    key_x = jnp.stack(key_x)
    value_y = jnp.stack(value_y)
    key_x, value_y, row_ids = lax.optimization_barrier((key_x, value_y, row_ids))
    key_all = ring_gather(key_x, along_y)
    value_all = ring_gather(value_y, along_x)
    return (jnp.stack([jnp.stack(key_all), jnp.stack(value_all)]), row_ids)


def core_halves(weight_grads, c):
    tiles = weight_grads.reshape(16, 2, -1, weight_grads.shape[1])
    sent = lax.dynamic_index_in_dim(tiles, 1 - c, 1, keepdims=False)
    kept = lax.dynamic_index_in_dim(tiles, c, 1, keepdims=False)
    return (sent, kept)


def sum_on_chip(got, kept):
    both = (kept.astype(jnp.float32) + got.astype(jnp.float32)).astype(jnp.bfloat16)
    return both.reshape(4, 4, *both.shape[1:])


def sum_one_axis(both, x, y):
    half = both.shape[3] // 2
    key_part = ring_sum(both[:, :, :, :half], x, along_x).astype(jnp.bfloat16)
    value_part = ring_sum(jnp.swapaxes(both[:, :, :, half:], 0, 1), y, along_y).astype(jnp.bfloat16)
    return (key_part, value_part)


def project_kernel(
    spot_ref, mine_ref, got_ref, memory_ref, hidden_ref, grad_ref, weight_ref, key_proj_ref, sums_ref
):
    half = hidden_ref.shape[1]

    @pl.when(pl.program_id(0) == 0)
    def _():
        x, y, c = spot_ref[0], spot_ref[1], spot_ref[2]
        rows = mine_ref.shape[2]
        for one in range(4):
            for two in range(4):
                for half_index in range(2):
                    a = mine_ref[half_index, one * 4 + two].astype(jnp.float32)
                    b = got_ref[half_index, one * 4 + two].astype(jnp.float32)
                    low = jnp.where(c == 0, a, b)
                    high = jnp.where(c == 0, b, a)
                    dx, dy = (two, one) if half_index == 0 else (one, two)
                    at = ((x + 4 - dx) % 4) * 4 + (y + 4 - dy) % 4
                    both = jnp.concatenate([low, high], axis=0).astype(jnp.bfloat16)
                    weight_ref[
                        pl.ds(pl.multiple_of(at * (2 * rows), 16), 2 * rows),
                        half_index * half : (half_index + 1) * half,
                    ] = both

    memory = memory_ref[...]
    key_proj = jnp.dot(memory, weight_ref[:, :half], preferred_element_type=jnp.float32)
    value_proj = jnp.dot(memory, weight_ref[:, half:], preferred_element_type=jnp.float32)
    key_proj_ref[...] = key_proj
    hidden = hidden_ref[...].astype(jnp.float32)
    grad = grad_ref[...].astype(jnp.float32)
    square_sum = jnp.sum(key_proj * key_proj, axis=1, keepdims=True)
    cross_sum = jnp.sum(hidden * key_proj, axis=1, keepdims=True)
    output_sum = jnp.sum(grad * value_proj, axis=1, keepdims=True)
    lane = lax.broadcasted_iota(jnp.int32, (memory.shape[0], 128), 1)
    sums = jnp.where(lane == 0, square_sum, jnp.where(lane == 1, cross_sum, output_sum))
    sums_ref[...] = sums.T[:8, :]


def project(spot, mine, got, memory, hidden, grad_out):
    tokens, mem = memory.shape
    half = hidden.shape[1]
    tile = tokens // 4
    fixed = lambda i, s: (0, 0)
    return pl.pallas_call(
        project_kernel,
        out_shape=(
            jax.ShapeDtypeStruct((mem, 2 * half), jnp.bfloat16),
            pltpu.HBM((tokens, half), jnp.float32),
            jax.ShapeDtypeStruct((8, tokens), jnp.float32),
        ),
        grid_spec=pltpu.PrefetchScalarGridSpec(
            num_scalar_prefetch=1,
            grid=(4,),
            in_specs=[
                pl.BlockSpec(mine.shape, lambda i, s: (0, 0, 0, 0), pipeline_mode=pl.Buffered(1)),
                pl.BlockSpec(got.shape, lambda i, s: (0, 0, 0, 0), pipeline_mode=pl.Buffered(1)),
                pl.BlockSpec((tile, mem), lambda i, s: (i, 0)),
                pl.BlockSpec((tile, half), lambda i, s: (i, 0)),
                pl.BlockSpec((tile, half), lambda i, s: (i, 0)),
            ],
            out_specs=(
                pl.BlockSpec((mem, 2 * half), fixed, pipeline_mode=pl.Buffered(1)),
                pl.BlockSpec((tile, half), lambda i, s: (i, 0)),
                pl.BlockSpec((8, tile), lambda i, s: (0, i)),
            ),
        ),
        compiler_params=pltpu.CompilerParams(vmem_limit_bytes=30 * 1024 * 1024),
        name="project",
    )(spot, *in_hbm(mine, got, memory, hidden, grad_out))


def gates_of(sums_refs, hidden_ref, grad_ref, key_proj_ref, both_ref):
    half = hidden_ref.shape[1]
    sums = sums_refs[0][...] + sums_refs[1][...] + sums_refs[2][...] + sums_refs[3][...]
    root_width = math.sqrt(D)
    key_scale = jnp.sqrt(sums[0:1, :] / D + norm_eps)
    gate_score = sums[1:2, :] / (key_scale * root_width)
    gate_value = 1.0 / (1.0 + jnp.exp(-gate_score))
    gate_grad = gate_value * (1.0 - gate_value) * sums[2:3, :]
    by_hidden = 1.0 / (key_scale * root_width)
    by_key = gate_score / (D * key_scale * key_scale)
    row = lax.broadcasted_iota(jnp.int32, (128, sums.shape[1]), 0)
    coded = jnp.where(
        row == 0,
        gate_value,
        jnp.where(row == 1, gate_grad, jnp.where(row == 2, by_hidden, by_key)),
    ).T
    hidden = hidden_ref[...].astype(jnp.float32)
    key_grad = coded[:, 1:2] * (hidden * coded[:, 2:3] - key_proj_ref[...] * coded[:, 3:4])
    value_grad = coded[:, 0:1] * grad_ref[...].astype(jnp.float32)
    both_ref[:, :half] = key_grad.astype(jnp.bfloat16)
    both_ref[:, half:] = value_grad.astype(jnp.bfloat16)


def grads_kernel(order_ref, *refs):
    both_ref, outs = refs[8], refs[9:]
    half = outs[0].shape[1]
    gates_of(refs[:4], *refs[4:7], both_ref)

    @pl.when(pl.program_id(0) < len(outs) // 2)
    def _():
        memory_grad = lax.dot_general(
            both_ref[...],
            refs[7][...],
            (((1,), (1,)), ((), ())),
            preferred_element_type=jnp.float32,
        ).astype(jnp.bfloat16)
        for k in range(len(outs) // 2):

            @pl.when(pl.program_id(0) == k)
            def _():
                outs[2 * k][...] = memory_grad[:, :half]
                outs[2 * k + 1][...] = memory_grad[:, half:]


def grads(order, products, sums, hidden, grad_out, key_proj, weights):
    steps = order.shape[0]
    tokens, half = hidden.shape
    tile = tokens // 4
    mem = weights.shape[0]
    at = lambda i, o: (o[i], 0)
    fixed = lambda i, o: (0, 0)
    one = pl.Buffered(1)
    if steps == 1:
        both_shape, both_spec = (tile, 2 * half), pl.BlockSpec((tile, 2 * half), fixed)
    else:
        both_shape, both_spec = (tokens, 2 * half), pl.BlockSpec((tile, 2 * half), at)
    return pl.pallas_call(
        grads_kernel,
        out_shape=(
            pltpu.HBM(both_shape, jnp.bfloat16),
            *([jax.ShapeDtypeStruct((tile, mem // 2), jnp.bfloat16)] * (2 * products)),
        ),
        grid_spec=pltpu.PrefetchScalarGridSpec(
            num_scalar_prefetch=1,
            grid=(steps,),
            in_specs=[pl.BlockSpec((8, tile), lambda i, o: (0, o[i]))] * 4
            + [pl.BlockSpec((tile, half), at)] * 3
            + [pl.BlockSpec(weights.shape, fixed, pipeline_mode=one)],
            out_specs=(
                both_spec,
                *([pl.BlockSpec((tile, mem // 2), fixed, pipeline_mode=one)] * (2 * products)),
            ),
        ),
        compiler_params=pltpu.CompilerParams(vmem_limit_bytes=26 * 1024 * 1024),
        name="grads_far" if steps == 1 else "grads_near",
    )(order, *sums, *in_hbm(hidden, grad_out, key_proj), weights)


SLOTS = 48
SLOT_CAP = 45
TILE = 256


def pack_kernel(tile_ref, spot_ref, numbers_ref, l1, l2, l3, r1, r2, r3, out_ref, sum_ref, rows_ref):
    width = out_ref.shape[1]
    tokens, half = l1.shape
    entries = tile_ref.shape[1]
    lookups = 2 * half // width

    @pl.when(pl.program_id(0) == 0)
    def _():
        f32 = jnp.float32
        left = l1[...].astype(f32) + l2[...].astype(f32) + l3[...].astype(f32)
        right = r1[...].astype(f32) + r2[...].astype(f32) + r3[...].astype(f32)
        sum_ref[:, :half] = left.astype(jnp.bfloat16)
        sum_ref[:, half:] = right.astype(jnp.bfloat16)
        for l in range(lookups):
            rows_ref[l * tokens : (l + 1) * tokens, :] = sum_ref[:, l * width : (l + 1) * width]
        rows_ref[lookups * tokens :, :] = numbers_ref[...]

    steps = out_ref.shape[0] // TILE
    place = lax.broadcasted_iota(jnp.int32, (TILE, entries), 0).astype(jnp.bfloat16)
    one, zero = jnp.ones((), jnp.bfloat16), jnp.zeros((), jnp.bfloat16)
    hits = []
    for s in range(steps):
        here = pl.program_id(0) * steps + s
        spot = jnp.where(tile_ref[...] == here, spot_ref[...], -1)
        spot = jnp.broadcast_to(spot.astype(jnp.bfloat16), place.shape)
        hits.append(jnp.where(place == spot, one, zero))
    out_ref[...] = jnp.dot(
        jnp.concatenate(hits, axis=0), rows_ref[...], preferred_element_type=jnp.float32
    ).astype(jnp.bfloat16)


def pack_rows(slot, numbers, parts, total_slots, width):
    per_step = 3 * TILE
    tokens, half = parts[0].shape
    fixed = lambda i: (0, 0)
    one = pl.Buffered(1)
    return pl.pallas_call(
        pack_kernel,
        out_shape=pltpu.HBM((total_slots, width), jnp.bfloat16),
        grid=(total_slots // per_step,),
        in_specs=[pl.BlockSpec(slot.shape, fixed)] * 2
        + [pl.BlockSpec(numbers.shape, fixed)]
        + [pl.BlockSpec((tokens, half), fixed, pipeline_mode=one)] * 6,
        out_specs=pl.BlockSpec((per_step, width), lambda i: (i, 0)),
        scratch_shapes=[
            pltpu.VMEM((tokens, 2 * half), jnp.bfloat16),
            pltpu.VMEM((slot.shape[1], width), jnp.bfloat16),
        ],
        compiler_params=pltpu.CompilerParams(vmem_limit_bytes=26 * 1024 * 1024),
        name="pack_rows",
    )(slot // TILE, slot % TILE, numbers, *parts)


def adam_kernel(
    tile_ref, spot_ref, rows_ref, table_ref, first_ref, second_ref, new_table_ref, new_first_ref, new_second_ref
):
    steps = table_ref.shape[0] // TILE
    width = table_ref.shape[1]
    entries = rows_ref.shape[0]
    chunk = 1024
    place = lax.broadcasted_iota(jnp.int32, (TILE, chunk), 0).astype(jnp.bfloat16)
    one, zero = jnp.ones((), jnp.bfloat16), jnp.zeros((), jnp.bfloat16)
    for s in range(steps):
        here = pl.program_id(0) * steps + s
        grad = jnp.zeros((TILE, width), jnp.float32)
        for k in range(0, entries, chunk):
            spot = jnp.where(tile_ref[:, k : k + chunk] == here, spot_ref[:, k : k + chunk], -1)
            spot = jnp.broadcast_to(spot.astype(jnp.bfloat16), (TILE, chunk))
            hits = jnp.where(place == spot, one, zero)
            grad += jnp.dot(hits, rows_ref[k : k + chunk, :], preferred_element_type=jnp.float32)
        at = slice(s * TILE, (s + 1) * TILE)
        new_first = beta_one * first_ref[at, :] + (1.0 - beta_one) * grad
        new_second = beta_two * second_ref[at, :] + (1.0 - beta_two) * grad * grad
        stepped = new_first / correct_one / (jnp.sqrt(new_second / correct_two) + adam_eps)
        new_table_ref[at, :] = table_ref[at, :] - learn_rate * stepped
        new_first_ref[at, :] = new_first
        new_second_ref[at, :] = new_second


def adam_rows(got, embed_table, first_moment, second_moment):
    rows_dev, width = embed_table.shape
    per_step = 2 * TILE
    block = pl.BlockSpec((per_step, width), lambda i: (i, 0))
    tile = got[:, SLOT_CAP, :SLOTS].astype(jnp.int32).reshape(1, -1)
    spot = got[:, SLOT_CAP + 1, :SLOTS].astype(jnp.int32).reshape(1, -1)
    got_rows = got.reshape(-1, width)
    whole = pl.BlockSpec(tile.shape, lambda i: (0, 0))
    return pl.pallas_call(
        adam_kernel,
        out_shape=(jax.ShapeDtypeStruct((rows_dev, width), jnp.float32),) * 3,
        grid=(rows_dev // per_step,),
        in_specs=[
            whole,
            whole,
            pl.BlockSpec(got_rows.shape, lambda i: (0, 0)),
            block,
            block,
            block,
        ],
        out_specs=(block,) * 3,
        compiler_params=pltpu.CompilerParams(vmem_limit_bytes=26 * 1024 * 1024),
        name="adam_rows",
    )(tile, spot, got_rows, *in_hbm(embed_table, first_moment, second_moment))


def route(my_ids, owners, rows_dev, row_width):
    ids = my_ids.T
    lookups, tokens = ids.shape
    flat = ids.reshape(-1)
    entries = flat.shape[0]
    owner_of = flat // rows_dev
    local_row = flat % rows_dev
    owner_hits = (owner_of[:, None] == jnp.arange(owners, dtype=jnp.int32)[None, :]).astype(
        jnp.bfloat16
    )
    earlier = (jnp.arange(entries)[None, :] < jnp.arange(entries)[:, None]).astype(jnp.bfloat16)
    before_counts = jnp.dot(earlier, owner_hits, preferred_element_type=jnp.float32)
    slot_rank = jnp.sum(before_counts * owner_hits.astype(jnp.float32), axis=1).astype(jnp.int32)
    slot = owner_of * SLOTS + slot_rank
    rank_hits = slot_rank[:, None] == jnp.arange(SLOTS, dtype=jnp.int32)[None, :]
    low = local_row % TILE
    high = local_row // TILE
    values = jnp.concatenate(
        [
            jnp.where(rank_hits, v[:, None], 0).astype(jnp.bfloat16)
            for v in (high, low, jnp.ones_like(low))
        ],
        axis=1,
    )
    found = lax.dot_general(
        owner_hits, values, (((0,), (0,)), ((), ())), preferred_element_type=jnp.float32
    )
    got_high, got_low, filled = jnp.split(found, 3, axis=1)
    got_high = jnp.where(filled > 0, got_high, rows_dev // TILE)
    numbers = jnp.concatenate([got_high, got_low], axis=0).astype(jnp.bfloat16)
    numbers = jnp.pad(numbers, ((0, 0), (0, row_width - SLOTS)))
    owner = jnp.arange(owners, dtype=jnp.int32) * SLOTS
    number_slot = jnp.concatenate([owner + SLOT_CAP, owner + SLOT_CAP + 1])
    return (jnp.concatenate([slot.reshape(1, -1), number_slot[None, :]], axis=1), numbers)


def body(
    memory,
    hidden,
    grad_out,
    key_weight,
    value_weight,
    row_ids,
    embed_table,
    first_moment,
    second_moment,
):
    dp_count = lax.axis_size("dp")
    tensor_count = lax.axis_size("tensor")
    owners = dp_count * tensor_count
    rows_dev, row_width = embed_table.shape
    block_rows = memory.shape[0] // tensor_count
    mine, row_ids = gather_weights(key_weight, value_weight, row_ids)
    my_ids = lax.dynamic_slice_in_dim(
        row_ids, lax.axis_index("tensor") * block_rows, block_rows, 0
    )
    at = lax.axis_index("dp")
    z = lax.axis_index("tensor")
    x, y, c = at // 8, (at // 2) % 4, at % 2
    slot, numbers = route(my_ids, owners, rows_dev, row_width)
    mine, numbers, slot = lax.optimization_barrier((mine, numbers, slot))
    mine = mine.reshape(2, 16, *key_weight.shape)
    got = lax.ppermute(mine, "dp", other_core())
    spot = jnp.stack([x, y, c]).astype(jnp.int32)
    weights, key_proj, sums = project(spot, mine, got, memory, hidden, grad_out)
    sums = [sums] + [lax.ppermute(sums, "tensor", along_z(d)) for d in STEPS]
    far = ((z + 2) % 4)[None].astype(jnp.int32)
    near = jnp.stack([(z + 1) % 4, (z + 3) % 4, z, (z + 2) % 4]).astype(jnp.int32)
    _, far_left, far_right = grads(far, 1, sums, hidden, grad_out, key_proj, weights)
    up = lax.ppermute(far_left, "tensor", along_z(1))
    down = lax.ppermute(far_right, "tensor", along_z(3))
    both, next_left, next_right, last_left, last_right, own_left, own_right = grads(
        near, 3, sums, hidden, grad_out, key_proj, weights
    )
    from_last_right = lax.ppermute(next_right, "tensor", along_z(1))
    from_next_left = lax.ppermute(last_left, "tensor", along_z(3))
    next_left = (up.astype(jnp.float32) + next_left.astype(jnp.float32)).astype(jnp.bfloat16)
    last_right = (down.astype(jnp.float32) + last_right.astype(jnp.float32)).astype(jnp.bfloat16)
    both, next_left, last_right = lax.optimization_barrier((both, next_left, last_right))
    from_last_left = lax.ppermute(next_left, "tensor", along_z(1))
    from_next_right = lax.ppermute(last_right, "tensor", along_z(3))
    weight_grads = lax.dot_general(
        memory, both, (((0,), (0,)), ((), ())), preferred_element_type=jnp.float32
    ).astype(jnp.bfloat16)
    sent, kept = core_halves(weight_grads, c)
    sent, kept, from_last_right, from_next_left, from_last_left, from_next_right = (
        lax.optimization_barrier(
            (sent, kept, from_last_right, from_next_left, from_last_left, from_next_right)
        )
    )
    other = lax.ppermute(sent, "dp", other_core())
    send_rows = pack_rows(
        slot,
        numbers,
        (own_left, from_last_left, from_next_left, own_right, from_last_right, from_next_right),
        owners * SLOTS,
        row_width,
    )
    send_rows, other = lax.optimization_barrier((send_rows, other))
    key_part, value_part = sum_one_axis(sum_on_chip(other, kept), x, y)
    key_pieces = ring_pieces(key_part, y, along_y)
    value_pieces = ring_pieces(value_part, x, along_x)
    got_rows = lax.all_to_all(
        send_rows.reshape(owners, SLOTS, row_width),
        ("dp", "tensor"),
        split_axis=0,
        concat_axis=0,
        tiled=True,
    )
    new_table, new_first, new_second = adam_rows(
        got_rows, embed_table, first_moment, second_moment
    )
    key_pieces, value_pieces, new_second = lax.optimization_barrier(
        (key_pieces, value_pieces, new_second)
    )
    key_weight_grad = sum(p.astype(jnp.float32) for p in key_pieces)
    value_weight_grad = sum(p.astype(jnp.float32) for p in value_pieces)
    return (key_weight_grad, value_weight_grad, new_table, new_first, new_second)


def solution(mesh):
    return jax.shard_map(
        body,
        mesh=mesh,
        in_specs=(
            P("dp", None),
            P("dp", "tensor"),
            P("dp", "tensor"),
            P("dp", "tensor"),
            P("dp", "tensor"),
            P("dp", None),
            P(("dp", "tensor"), None),
            P(("dp", "tensor"), None),
            P(("dp", "tensor"), None),
        ),
        out_specs=(
            P("dp", "tensor"),
            P("dp", "tensor"),
            P(("dp", "tensor"), None),
            P(("dp", "tensor"), None),
            P(("dp", "tensor"), None),
        ),
        check_vma=False,
    )
```

```python
import math

import jax
import jax.numpy as jnp
from jax import lax
from jax.experimental import pallas as pl
from jax.experimental.pallas import tpu as pltpu
from jax.sharding import PartitionSpec as P

D = 2560


beta_one = 0.9
beta_two = 0.999
learn_rate = 0.01
adam_eps = 1e-08
norm_eps = 1e-06
correct_one = 0.9999734386011124
correct_two = 0.0952078528863


def dp_index(x, y, c):
    return (x % 4) * 8 + (y % 4) * 2 + c


def along_first(d):
    return [
        (dp_index(x, y, c), dp_index(x, y + d, c) if c else dp_index(x + d, y, c))
        for x in range(4)
        for y in range(4)
        for c in range(2)
    ]


def along_second(d):
    return [
        (dp_index(x, y, c), dp_index(x + d, y, c) if c else dp_index(x, y + d, c))
        for x in range(4)
        for y in range(4)
        for c in range(2)
    ]


def other_core():
    return [
        (dp_index(x, y, c), dp_index(x, y, 1 - c))
        for x in range(4)
        for y in range(4)
        for c in range(2)
    ]


def along_z(d):
    return [(z, (z + d) % 4) for z in range(4)]


STEPS = (1, 2, 3)


def in_hbm(*arrays):
    return tuple(pltpu.with_memory_space_constraint(a, pltpu.HBM) for a in arrays)


def ring_gather(shard, perm_of):
    return [shard] + [lax.ppermute(shard, "dp", perm_of(d)) for d in STEPS]


def ring_pieces(tiles, here, perm_of):
    own = lax.dynamic_index_in_dim(tiles, here, 0, keepdims=False)
    return [own] + [
        lax.ppermute(
            lax.dynamic_index_in_dim(tiles, (here + d) % 4, 0, keepdims=False), "dp", perm_of(d)
        )
        for d in STEPS
    ]


def ring_sum(tiles, here, perm_of):
    return sum(p.astype(jnp.float32) for p in ring_pieces(tiles, here, perm_of))


def gather_weights(key_weight, value_weight, routed):
    both = jnp.concatenate([key_weight, value_weight], axis=1)
    line = jnp.stack(ring_gather(both, along_first))
    line, routed = lax.optimization_barrier((line, routed))
    return (jnp.stack(ring_gather(line, along_second)), *routed)


def sum_on_chip(got, kept, c):
    both = (kept.astype(jnp.float32) + got.astype(jnp.float32)).astype(jnp.bfloat16)
    both = both.reshape(4, 4, *both.shape[1:])
    return jnp.where(c == 0, both, jnp.swapaxes(both, 0, 1))


def core_halves(weight_grads, c):
    tiles = weight_grads.reshape(16, 2, -1, weight_grads.shape[1])
    sent = lax.dynamic_index_in_dim(tiles, 1 - c, 1, keepdims=False)
    kept = lax.dynamic_index_in_dim(tiles, c, 1, keepdims=False)
    return (sent, kept)


def project_kernel(
    spot_ref, mine_ref, got_ref, memory_ref, hidden_ref, grad_ref, weight_ref, key_proj_ref, sums_ref
):
    half = hidden_ref.shape[1]

    @pl.when(pl.program_id(0) == 0)
    def _():
        x, y, c = spot_ref[0], spot_ref[1], spot_ref[2]
        rows = mine_ref.shape[1]
        for dx in range(4):
            for dy in range(4):
                mine_low, mine_high = mine_ref[dy * 4 + dx], mine_ref[dx * 4 + dy]
                got_low, got_high = got_ref[dy * 4 + dx], got_ref[dx * 4 + dy]
                low = jnp.where(c == 0, mine_low.astype(jnp.float32), got_low.astype(jnp.float32))
                high = jnp.where(c == 0, got_high.astype(jnp.float32), mine_high.astype(jnp.float32))
                at = ((x + 4 - dx) % 4) * 4 + (y + 4 - dy) % 4
                both = jnp.concatenate([low, high], axis=0).astype(jnp.bfloat16)
                weight_ref[pl.ds(pl.multiple_of(at * (2 * rows), 16), 2 * rows), :] = both

    memory = memory_ref[...]
    key_proj = jnp.dot(memory, weight_ref[:, :half], preferred_element_type=jnp.float32)
    value_proj = jnp.dot(memory, weight_ref[:, half:], preferred_element_type=jnp.float32)
    key_proj_ref[...] = key_proj
    hidden = hidden_ref[...].astype(jnp.float32)
    grad = grad_ref[...].astype(jnp.float32)
    square_sum = jnp.sum(key_proj * key_proj, axis=1, keepdims=True)
    cross_sum = jnp.sum(hidden * key_proj, axis=1, keepdims=True)
    output_sum = jnp.sum(grad * value_proj, axis=1, keepdims=True)
    lane = lax.broadcasted_iota(jnp.int32, (memory.shape[0], 128), 1)
    sums = jnp.where(lane == 0, square_sum, jnp.where(lane == 1, cross_sum, output_sum))
    sums_ref[...] = sums.T[:8, :]


def project(spot, mine, got, memory, hidden, grad_out):
    tokens, mem = memory.shape
    half = hidden.shape[1]
    tile = tokens // 4
    fixed = lambda i, s: (0, 0)
    return pl.pallas_call(
        project_kernel,
        out_shape=(
            jax.ShapeDtypeStruct((mem, 2 * half), jnp.bfloat16),
            pltpu.HBM((tokens, half), jnp.float32),
            jax.ShapeDtypeStruct((8, tokens), jnp.float32),
        ),
        grid_spec=pltpu.PrefetchScalarGridSpec(
            num_scalar_prefetch=1,
            grid=(4,),
            in_specs=[
                pl.BlockSpec(mine.shape, lambda i, s: (0, 0, 0), pipeline_mode=pl.Buffered(1)),
                pl.BlockSpec(got.shape, lambda i, s: (0, 0, 0), pipeline_mode=pl.Buffered(1)),
                pl.BlockSpec((tile, mem), lambda i, s: (i, 0)),
                pl.BlockSpec((tile, half), lambda i, s: (i, 0)),
                pl.BlockSpec((tile, half), lambda i, s: (i, 0)),
            ],
            out_specs=(
                pl.BlockSpec((mem, 2 * half), fixed, pipeline_mode=pl.Buffered(1)),
                pl.BlockSpec((tile, half), lambda i, s: (i, 0)),
                pl.BlockSpec((8, tile), lambda i, s: (0, i)),
            ),
        ),
        compiler_params=pltpu.CompilerParams(vmem_limit_bytes=30 * 1024 * 1024),
        name="project",
    )(spot, *in_hbm(mine, got, memory, hidden, grad_out))


def gates_of(sums_refs, hidden_ref, grad_ref, key_proj_ref, both_ref):
    half = hidden_ref.shape[1]
    sums = sums_refs[0][...] + sums_refs[1][...] + sums_refs[2][...] + sums_refs[3][...]
    root_width = math.sqrt(D)
    key_scale = jnp.sqrt(sums[0:1, :] / D + norm_eps)
    gate_score = sums[1:2, :] / (key_scale * root_width)
    gate_value = 1.0 / (1.0 + jnp.exp(-gate_score))
    gate_grad = gate_value * (1.0 - gate_value) * sums[2:3, :]
    by_hidden = 1.0 / (key_scale * root_width)
    by_key = gate_score / (D * key_scale * key_scale)
    row = lax.broadcasted_iota(jnp.int32, (128, sums.shape[1]), 0)
    coded = jnp.where(
        row == 0,
        gate_value,
        jnp.where(row == 1, gate_grad, jnp.where(row == 2, by_hidden, by_key)),
    ).T
    hidden = hidden_ref[...].astype(jnp.float32)
    key_grad = coded[:, 1:2] * (hidden * coded[:, 2:3] - key_proj_ref[...] * coded[:, 3:4])
    value_grad = coded[:, 0:1] * grad_ref[...].astype(jnp.float32)
    both_ref[:, :half] = key_grad.astype(jnp.bfloat16)
    both_ref[:, half:] = value_grad.astype(jnp.bfloat16)


def grads_kernel(order_ref, *refs):
    both_ref, outs = refs[8], refs[9:]
    half = outs[0].shape[1]
    gates_of(refs[:4], *refs[4:7], both_ref)

    @pl.when(pl.program_id(0) < len(outs) // 2)
    def _():
        memory_grad = lax.dot_general(
            both_ref[...],
            refs[7][...],
            (((1,), (1,)), ((), ())),
            preferred_element_type=jnp.float32,
        ).astype(jnp.bfloat16)
        for k in range(len(outs) // 2):

            @pl.when(pl.program_id(0) == k)
            def _():
                outs[2 * k][...] = memory_grad[:, :half]
                outs[2 * k + 1][...] = memory_grad[:, half:]


def grads(order, products, sums, hidden, grad_out, key_proj, weights):
    steps = order.shape[0]
    tokens, half = hidden.shape
    tile = tokens // 4
    mem = weights.shape[0]
    at = lambda i, o: (o[i], 0)
    fixed = lambda i, o: (0, 0)
    one = pl.Buffered(1)
    if steps == 1:
        both_shape, both_spec = (tile, 2 * half), pl.BlockSpec((tile, 2 * half), fixed)
    else:
        both_shape, both_spec = (tokens, 2 * half), pl.BlockSpec((tile, 2 * half), at)
    return pl.pallas_call(
        grads_kernel,
        out_shape=(
            pltpu.HBM(both_shape, jnp.bfloat16),
            *([jax.ShapeDtypeStruct((tile, mem // 2), jnp.bfloat16)] * (2 * products)),
        ),
        grid_spec=pltpu.PrefetchScalarGridSpec(
            num_scalar_prefetch=1,
            grid=(steps,),
            in_specs=[pl.BlockSpec((8, tile), lambda i, o: (0, o[i]))] * 4
            + [pl.BlockSpec((tile, half), at)] * 3
            + [pl.BlockSpec(weights.shape, fixed, pipeline_mode=one)],
            out_specs=(
                both_spec,
                *([pl.BlockSpec((tile, mem // 2), fixed, pipeline_mode=one)] * (2 * products)),
            ),
        ),
        compiler_params=pltpu.CompilerParams(vmem_limit_bytes=26 * 1024 * 1024),
        name="grads_far" if steps == 1 else "grads_near",
    )(order, *sums, *in_hbm(hidden, grad_out, key_proj), weights)


SLOTS = 48
SLOT_CAP = 45
TILE = 256


def pack_kernel(tile_ref, spot_ref, numbers_ref, l1, l2, l3, r1, r2, r3, out_ref, sum_ref, rows_ref):
    width = out_ref.shape[1]
    tokens, half = l1.shape
    entries = tile_ref.shape[1]
    lookups = 2 * half // width

    @pl.when(pl.program_id(0) == 0)
    def _():
        f32 = jnp.float32
        left = l1[...].astype(f32) + l2[...].astype(f32) + l3[...].astype(f32)
        right = r1[...].astype(f32) + r2[...].astype(f32) + r3[...].astype(f32)
        sum_ref[:, :half] = left.astype(jnp.bfloat16)
        sum_ref[:, half:] = right.astype(jnp.bfloat16)
        for l in range(lookups):
            rows_ref[l * tokens : (l + 1) * tokens, :] = sum_ref[:, l * width : (l + 1) * width]
        rows_ref[lookups * tokens :, :] = numbers_ref[...]

    steps = out_ref.shape[0] // TILE
    place = lax.broadcasted_iota(jnp.int32, (TILE, entries), 0).astype(jnp.bfloat16)
    one, zero = jnp.ones((), jnp.bfloat16), jnp.zeros((), jnp.bfloat16)
    hits = []
    for s in range(steps):
        here = pl.program_id(0) * steps + s
        spot = jnp.where(tile_ref[...] == here, spot_ref[...], -1)
        spot = jnp.broadcast_to(spot.astype(jnp.bfloat16), place.shape)
        hits.append(jnp.where(place == spot, one, zero))
    out_ref[...] = jnp.dot(
        jnp.concatenate(hits, axis=0), rows_ref[...], preferred_element_type=jnp.float32
    ).astype(jnp.bfloat16)


def pack_rows(slot, numbers, parts, total_slots, width):
    per_step = 3 * TILE
    tokens, half = parts[0].shape
    fixed = lambda i: (0, 0)
    one = pl.Buffered(1)
    return pl.pallas_call(
        pack_kernel,
        out_shape=pltpu.HBM((total_slots, width), jnp.bfloat16),
        grid=(total_slots // per_step,),
        in_specs=[pl.BlockSpec(slot.shape, fixed)] * 2
        + [pl.BlockSpec(numbers.shape, fixed)]
        + [pl.BlockSpec((tokens, half), fixed, pipeline_mode=one)] * 6,
        out_specs=pl.BlockSpec((per_step, width), lambda i: (i, 0)),
        scratch_shapes=[
            pltpu.VMEM((tokens, 2 * half), jnp.bfloat16),
            pltpu.VMEM((slot.shape[1], width), jnp.bfloat16),
        ],
        compiler_params=pltpu.CompilerParams(vmem_limit_bytes=26 * 1024 * 1024),
        name="pack_rows",
    )(slot // TILE, slot % TILE, numbers, *parts)


def adam_kernel(
    tile_ref, spot_ref, rows_ref, table_ref, first_ref, second_ref, new_table_ref, new_first_ref, new_second_ref
):
    steps = table_ref.shape[0] // TILE
    width = table_ref.shape[1]
    entries = rows_ref.shape[0]
    chunk = 1024
    place = lax.broadcasted_iota(jnp.int32, (TILE, chunk), 0).astype(jnp.bfloat16)
    one, zero = jnp.ones((), jnp.bfloat16), jnp.zeros((), jnp.bfloat16)
    for s in range(steps):
        here = pl.program_id(0) * steps + s
        grad = jnp.zeros((TILE, width), jnp.float32)
        for k in range(0, entries, chunk):
            spot = jnp.where(tile_ref[:, k : k + chunk] == here, spot_ref[:, k : k + chunk], -1)
            spot = jnp.broadcast_to(spot.astype(jnp.bfloat16), (TILE, chunk))
            hits = jnp.where(place == spot, one, zero)
            grad += jnp.dot(hits, rows_ref[k : k + chunk, :], preferred_element_type=jnp.float32)
        at = slice(s * TILE, (s + 1) * TILE)
        new_first = beta_one * first_ref[at, :] + (1.0 - beta_one) * grad
        new_second = beta_two * second_ref[at, :] + (1.0 - beta_two) * grad * grad
        stepped = new_first / correct_one / (jnp.sqrt(new_second / correct_two) + adam_eps)
        new_table_ref[at, :] = table_ref[at, :] - learn_rate * stepped
        new_first_ref[at, :] = new_first
        new_second_ref[at, :] = new_second


def adam_rows(got, embed_table, first_moment, second_moment):
    rows_dev, width = embed_table.shape
    per_step = 2 * TILE
    block = pl.BlockSpec((per_step, width), lambda i: (i, 0))
    tile = got[:, SLOT_CAP, :SLOTS].astype(jnp.int32).reshape(1, -1)
    spot = got[:, SLOT_CAP + 1, :SLOTS].astype(jnp.int32).reshape(1, -1)
    got_rows = got.reshape(-1, width)
    whole = pl.BlockSpec(tile.shape, lambda i: (0, 0))
    return pl.pallas_call(
        adam_kernel,
        out_shape=(jax.ShapeDtypeStruct((rows_dev, width), jnp.float32),) * 3,
        grid=(rows_dev // per_step,),
        in_specs=[
            whole,
            whole,
            pl.BlockSpec(got_rows.shape, lambda i: (0, 0)),
            block,
            block,
            block,
        ],
        out_specs=(block,) * 3,
        compiler_params=pltpu.CompilerParams(vmem_limit_bytes=26 * 1024 * 1024),
        name="adam_rows",
    )(tile, spot, got_rows, *in_hbm(embed_table, first_moment, second_moment))


def route(my_ids, owners, rows_dev, row_width):
    ids = my_ids.T
    lookups, tokens = ids.shape
    flat = ids.reshape(-1)
    entries = flat.shape[0]
    owner_of = flat // rows_dev
    local_row = flat % rows_dev
    owner_hits = (owner_of[:, None] == jnp.arange(owners, dtype=jnp.int32)[None, :]).astype(
        jnp.bfloat16
    )
    earlier = (jnp.arange(entries)[None, :] < jnp.arange(entries)[:, None]).astype(jnp.bfloat16)
    before_counts = jnp.dot(earlier, owner_hits, preferred_element_type=jnp.float32)
    slot_rank = jnp.sum(before_counts * owner_hits.astype(jnp.float32), axis=1).astype(jnp.int32)
    slot = owner_of * SLOTS + slot_rank
    rank_hits = slot_rank[:, None] == jnp.arange(SLOTS, dtype=jnp.int32)[None, :]
    low = local_row % TILE
    high = local_row // TILE
    values = jnp.concatenate(
        [
            jnp.where(rank_hits, v[:, None], 0).astype(jnp.bfloat16)
            for v in (high, low, jnp.ones_like(low))
        ],
        axis=1,
    )
    found = lax.dot_general(
        owner_hits, values, (((0,), (0,)), ((), ())), preferred_element_type=jnp.float32
    )
    got_high, got_low, filled = jnp.split(found, 3, axis=1)
    got_high = jnp.where(filled > 0, got_high, rows_dev // TILE)
    numbers = jnp.concatenate([got_high, got_low], axis=0).astype(jnp.bfloat16)
    numbers = jnp.pad(numbers, ((0, 0), (0, row_width - SLOTS)))
    owner = jnp.arange(owners, dtype=jnp.int32) * SLOTS
    number_slot = jnp.concatenate([owner + SLOT_CAP, owner + SLOT_CAP + 1])
    return (jnp.concatenate([slot.reshape(1, -1), number_slot[None, :]], axis=1), numbers)


def body(
    memory,
    hidden,
    grad_out,
    key_weight,
    value_weight,
    row_ids,
    embed_table,
    first_moment,
    second_moment,
):
    dp_count = lax.axis_size("dp")
    tensor_count = lax.axis_size("tensor")
    owners = dp_count * tensor_count
    rows_dev, row_width = embed_table.shape
    block_rows = memory.shape[0] // tensor_count
    my_ids = lax.dynamic_slice_in_dim(
        row_ids, lax.axis_index("tensor") * block_rows, block_rows, 0
    )
    at = lax.axis_index("dp")
    z = lax.axis_index("tensor")
    x, y, c = at // 8, (at // 2) % 4, at % 2
    slot, numbers = route(my_ids, owners, rows_dev, row_width)
    mine, slot, numbers = gather_weights(key_weight, value_weight, (slot, numbers))
    mine = mine.reshape(16, *mine.shape[2:])
    got = lax.ppermute(mine, "dp", other_core())
    spot = jnp.stack([x, y, c]).astype(jnp.int32)
    weights, key_proj, sums = project(spot, mine, got, memory, hidden, grad_out)
    sums = [sums] + [lax.ppermute(sums, "tensor", along_z(d)) for d in STEPS]
    far = ((z + 2) % 4)[None].astype(jnp.int32)
    near = jnp.stack([(z + 1) % 4, (z + 3) % 4, z, (z + 2) % 4]).astype(jnp.int32)
    _, far_left, far_right = grads(far, 1, sums, hidden, grad_out, key_proj, weights)
    up = lax.ppermute(far_left, "tensor", along_z(1))
    down = lax.ppermute(far_right, "tensor", along_z(3))
    both, next_left, next_right, last_left, last_right, own_left, own_right = grads(
        near, 3, sums, hidden, grad_out, key_proj, weights
    )
    from_last_right = lax.ppermute(next_right, "tensor", along_z(1))
    from_next_left = lax.ppermute(last_left, "tensor", along_z(3))
    next_left = (up.astype(jnp.float32) + next_left.astype(jnp.float32)).astype(jnp.bfloat16)
    last_right = (down.astype(jnp.float32) + last_right.astype(jnp.float32)).astype(jnp.bfloat16)
    both, next_left, last_right = lax.optimization_barrier((both, next_left, last_right))
    from_last_left = lax.ppermute(next_left, "tensor", along_z(1))
    from_next_right = lax.ppermute(last_right, "tensor", along_z(3))
    weight_grads = lax.dot_general(
        memory, both, (((0,), (0,)), ((), ())), preferred_element_type=jnp.float32
    ).astype(jnp.bfloat16)
    sent, kept = core_halves(weight_grads, c)
    sent, kept, from_last_right, from_next_left, from_last_left, from_next_right = (
        lax.optimization_barrier(
            (sent, kept, from_last_right, from_next_left, from_last_left, from_next_right)
        )
    )
    other = lax.ppermute(sent, "dp", other_core())
    send_rows = pack_rows(
        slot,
        numbers,
        (own_left, from_last_left, from_next_left, own_right, from_last_right, from_next_right),
        owners * SLOTS,
        row_width,
    )
    send_rows, other = lax.optimization_barrier((send_rows, other))
    chip_grads = sum_on_chip(other, kept, c)
    line_grads = ring_sum(chip_grads, jnp.where(c == 0, x, y), along_first).astype(jnp.bfloat16)
    pieces = ring_pieces(line_grads, jnp.where(c == 0, y, x), along_second)
    got_rows = lax.all_to_all(
        send_rows.reshape(owners, SLOTS, row_width),
        ("dp", "tensor"),
        split_axis=0,
        concat_axis=0,
        tiled=True,
    )
    new_table, new_first, new_second = adam_rows(
        got_rows, embed_table, first_moment, second_moment
    )
    pieces, new_second = lax.optimization_barrier((pieces, new_second))
    weight_sums = sum(p.astype(jnp.float32) for p in pieces)
    half = weight_sums.shape[1] // 2
    key_weight_grad = weight_sums[:, :half]
    value_weight_grad = weight_sums[:, half:]
    return (key_weight_grad, value_weight_grad, new_table, new_first, new_second)


def solution(mesh):
    return jax.shard_map(
        body,
        mesh=mesh,
        in_specs=(
            P("dp", None),
            P("dp", "tensor"),
            P("dp", "tensor"),
            P("dp", "tensor"),
            P("dp", "tensor"),
            P("dp", None),
            P(("dp", "tensor"), None),
            P(("dp", "tensor"), None),
            P(("dp", "tensor"), None),
        ),
        out_specs=(
            P("dp", "tensor"),
            P("dp", "tensor"),
            P(("dp", "tensor"), None),
            P(("dp", "tensor"), None),
            P(("dp", "tensor"), None),
        ),
        check_vma=False,
    )
```

```python
import math

import jax
import jax.numpy as jnp
from jax import lax
from jax.experimental import pallas as pl
from jax.experimental.pallas import tpu as pltpu
from jax.sharding import PartitionSpec as P

D = 2560


beta_one = 0.9
beta_two = 0.999
learn_rate = 0.01
adam_eps = 1e-08
norm_eps = 1e-06
correct_one = 0.9999734386011124
correct_two = 0.0952078528863


def dp_index(x, y, c):
    return (x % 4) * 8 + (y % 4) * 2 + c


def along_first(d):
    return [
        (dp_index(x, y, c), dp_index(x, y + d, c) if c else dp_index(x + d, y, c))
        for x in range(4)
        for y in range(4)
        for c in range(2)
    ]


def along_second(d):
    return [
        (dp_index(x, y, c), dp_index(x + d, y, c) if c else dp_index(x, y + d, c))
        for x in range(4)
        for y in range(4)
        for c in range(2)
    ]


def other_core():
    return [
        (dp_index(x, y, c), dp_index(x, y, 1 - c))
        for x in range(4)
        for y in range(4)
        for c in range(2)
    ]


def along_z(d):
    return [(z, (z + d) % 4) for z in range(4)]


STEPS = (2, 1, 3)
POSITION = (0, 2, 1, 3)


def in_hbm(*arrays):
    return tuple(pltpu.with_memory_space_constraint(a, pltpu.HBM) for a in arrays)


def ring_gather(shard, perm_of):
    return [shard] + [lax.ppermute(shard, "dp", perm_of(d)) for d in STEPS]


def ring_pieces(tiles, here, perm_of):
    own = lax.dynamic_index_in_dim(tiles, here, 0, keepdims=False)
    return [own] + [
        lax.ppermute(
            lax.dynamic_index_in_dim(tiles, (here + d) % 4, 0, keepdims=False), "dp", perm_of(d)
        )
        for d in STEPS
    ]


def ring_sum(tiles, here, perm_of):
    return sum(p.astype(jnp.float32) for p in ring_pieces(tiles, here, perm_of))


def gather_weights(key_weight, value_weight, routed):
    both = jnp.concatenate([key_weight, value_weight], axis=1)
    line = jnp.stack(ring_gather(both, along_first))
    line, routed = lax.optimization_barrier((line, routed))
    return (jnp.stack(ring_gather(line, along_second)), *routed)


def sum_on_chip(got, kept, c):
    both = (kept.astype(jnp.float32) + got.astype(jnp.float32)).astype(jnp.bfloat16)
    both = both.reshape(4, 4, *both.shape[1:])
    return jnp.where(c == 0, both, jnp.swapaxes(both, 0, 1))


def core_halves(weight_grads, c):
    tiles = weight_grads.reshape(16, 2, -1, weight_grads.shape[1])
    sent = lax.dynamic_index_in_dim(tiles, 1 - c, 1, keepdims=False)
    kept = lax.dynamic_index_in_dim(tiles, c, 1, keepdims=False)
    return (sent, kept)


def project_kernel(
    spot_ref, mine_ref, got_ref, memory_ref, hidden_ref, grad_ref, weight_ref, key_proj_ref, sums_ref
):
    half = hidden_ref.shape[1]

    def place(core):
        x, y = spot_ref[0], spot_ref[1]
        rows = mine_ref.shape[1]
        low_ref, high_ref = (got_ref, mine_ref) if core else (mine_ref, got_ref)
        for dx in range(4):
            for dy in range(4):
                low = low_ref[POSITION[dy] * 4 + POSITION[dx]].astype(jnp.float32)
                high = high_ref[POSITION[dx] * 4 + POSITION[dy]].astype(jnp.float32)
                at = ((x + 4 - dx) % 4) * 4 + (y + 4 - dy) % 4
                both = jnp.concatenate([low, high], axis=0).astype(jnp.bfloat16)
                weight_ref[pl.ds(pl.multiple_of(at * (2 * rows), 16), 2 * rows), :] = both

    for core in range(2):

        @pl.when((pl.program_id(0) == 0) & (spot_ref[2] == core))
        def _():
            place(core)

    memory = memory_ref[...]
    key_proj = jnp.dot(memory, weight_ref[:, :half], preferred_element_type=jnp.float32)
    value_proj = jnp.dot(memory, weight_ref[:, half:], preferred_element_type=jnp.float32)
    key_proj_ref[...] = key_proj
    hidden = hidden_ref[...].astype(jnp.float32)
    grad = grad_ref[...].astype(jnp.float32)
    square_sum = jnp.sum(key_proj * key_proj, axis=1, keepdims=True)
    cross_sum = jnp.sum(hidden * key_proj, axis=1, keepdims=True)
    output_sum = jnp.sum(grad * value_proj, axis=1, keepdims=True)
    lane = lax.broadcasted_iota(jnp.int32, (memory.shape[0], 128), 1)
    sums = jnp.where(lane == 0, square_sum, jnp.where(lane == 1, cross_sum, output_sum))
    sums_ref[...] = sums.T[:8, :]


def project(spot, mine, got, memory, hidden, grad_out):
    tokens, mem = memory.shape
    half = hidden.shape[1]
    tile = tokens // 4
    fixed = lambda i, s: (0, 0)
    return pl.pallas_call(
        project_kernel,
        out_shape=(
            jax.ShapeDtypeStruct((mem, 2 * half), jnp.bfloat16),
            pltpu.HBM((tokens, half), jnp.float32),
            jax.ShapeDtypeStruct((8, tokens), jnp.float32),
        ),
        grid_spec=pltpu.PrefetchScalarGridSpec(
            num_scalar_prefetch=1,
            grid=(4,),
            in_specs=[
                pl.BlockSpec(mine.shape, lambda i, s: (0, 0, 0), pipeline_mode=pl.Buffered(1)),
                pl.BlockSpec(got.shape, lambda i, s: (0, 0, 0), pipeline_mode=pl.Buffered(1)),
                pl.BlockSpec((tile, mem), lambda i, s: (i, 0)),
                pl.BlockSpec((tile, half), lambda i, s: (i, 0)),
                pl.BlockSpec((tile, half), lambda i, s: (i, 0)),
            ],
            out_specs=(
                pl.BlockSpec((mem, 2 * half), fixed, pipeline_mode=pl.Buffered(1)),
                pl.BlockSpec((tile, half), lambda i, s: (i, 0)),
                pl.BlockSpec((8, tile), lambda i, s: (0, i)),
            ),
        ),
        compiler_params=pltpu.CompilerParams(vmem_limit_bytes=30 * 1024 * 1024),
        name="project",
    )(spot, *in_hbm(mine, got, memory, hidden, grad_out))


def gates_of(sums_refs, hidden_ref, grad_ref, key_proj_ref, both_ref):
    half = hidden_ref.shape[1]
    sums = sums_refs[0][...] + sums_refs[1][...] + sums_refs[2][...] + sums_refs[3][...]
    root_width = math.sqrt(D)
    key_scale = jnp.sqrt(sums[0:1, :] / D + norm_eps)
    gate_score = sums[1:2, :] / (key_scale * root_width)
    gate_value = 1.0 / (1.0 + jnp.exp(-gate_score))
    gate_grad = gate_value * (1.0 - gate_value) * sums[2:3, :]
    by_hidden = 1.0 / (key_scale * root_width)
    by_key = gate_score / (D * key_scale * key_scale)
    row = lax.broadcasted_iota(jnp.int32, (128, sums.shape[1]), 0)
    coded = jnp.where(
        row == 0,
        gate_value,
        jnp.where(row == 1, gate_grad, jnp.where(row == 2, by_hidden, by_key)),
    ).T
    hidden = hidden_ref[...].astype(jnp.float32)
    key_grad = coded[:, 1:2] * (hidden * coded[:, 2:3] - key_proj_ref[...] * coded[:, 3:4])
    value_grad = coded[:, 0:1] * grad_ref[...].astype(jnp.float32)
    both_ref[:, :half] = key_grad.astype(jnp.bfloat16)
    both_ref[:, half:] = value_grad.astype(jnp.bfloat16)


def grads_kernel(order_ref, *refs):
    both_ref, outs = refs[8], refs[9:]
    half = outs[0].shape[1]
    gates_of(refs[:4], *refs[4:7], both_ref)

    @pl.when(pl.program_id(0) < len(outs) // 2)
    def _():
        memory_grad = lax.dot_general(
            both_ref[...],
            refs[7][...],
            (((1,), (1,)), ((), ())),
            preferred_element_type=jnp.float32,
        ).astype(jnp.bfloat16)
        for k in range(len(outs) // 2):

            @pl.when(pl.program_id(0) == k)
            def _():
                outs[2 * k][...] = memory_grad[:, :half]
                outs[2 * k + 1][...] = memory_grad[:, half:]


def grads(order, products, sums, hidden, grad_out, key_proj, weights):
    steps = order.shape[0]
    tokens, half = hidden.shape
    tile = tokens // 4
    mem = weights.shape[0]
    at = lambda i, o: (o[i], 0)
    fixed = lambda i, o: (0, 0)
    one = pl.Buffered(1)
    if steps == 1:
        both_shape, both_spec = (tile, 2 * half), pl.BlockSpec((tile, 2 * half), fixed)
    else:
        both_shape, both_spec = (tokens, 2 * half), pl.BlockSpec((tile, 2 * half), at)
    return pl.pallas_call(
        grads_kernel,
        out_shape=(
            pltpu.HBM(both_shape, jnp.bfloat16),
            *([jax.ShapeDtypeStruct((tile, mem // 2), jnp.bfloat16)] * (2 * products)),
        ),
        grid_spec=pltpu.PrefetchScalarGridSpec(
            num_scalar_prefetch=1,
            grid=(steps,),
            in_specs=[pl.BlockSpec((8, tile), lambda i, o: (0, o[i]))] * 4
            + [pl.BlockSpec((tile, half), at)] * 3
            + [pl.BlockSpec(weights.shape, fixed, pipeline_mode=one)],
            out_specs=(
                both_spec,
                *([pl.BlockSpec((tile, mem // 2), fixed, pipeline_mode=one)] * (2 * products)),
            ),
        ),
        compiler_params=pltpu.CompilerParams(vmem_limit_bytes=26 * 1024 * 1024),
        name="grads_far" if steps == 1 else "grads_near",
    )(order, *sums, *in_hbm(hidden, grad_out, key_proj), weights)


SLOTS = 48
SLOT_CAP = 45
TILE = 256


def pack_kernel(tile_ref, spot_ref, numbers_ref, l1, l2, l3, r1, r2, r3, out_ref, sum_ref, rows_ref):
    width = out_ref.shape[1]
    tokens, half = l1.shape
    entries = tile_ref.shape[1]
    lookups = 2 * half // width

    @pl.when(pl.program_id(0) == 0)
    def _():
        f32 = jnp.float32
        left = l1[...].astype(f32) + l2[...].astype(f32) + l3[...].astype(f32)
        right = r1[...].astype(f32) + r2[...].astype(f32) + r3[...].astype(f32)
        sum_ref[:, :half] = left.astype(jnp.bfloat16)
        sum_ref[:, half:] = right.astype(jnp.bfloat16)
        for l in range(lookups):
            rows_ref[l * tokens : (l + 1) * tokens, :] = sum_ref[:, l * width : (l + 1) * width]
        rows_ref[lookups * tokens :, :] = numbers_ref[...]

    steps = out_ref.shape[0] // TILE
    place = lax.broadcasted_iota(jnp.int32, (TILE, entries), 0).astype(jnp.bfloat16)
    one, zero = jnp.ones((), jnp.bfloat16), jnp.zeros((), jnp.bfloat16)
    hits = []
    for s in range(steps):
        here = pl.program_id(0) * steps + s
        spot = jnp.where(tile_ref[...] == here, spot_ref[...], -1)
        spot = jnp.broadcast_to(spot.astype(jnp.bfloat16), place.shape)
        hits.append(jnp.where(place == spot, one, zero))
    out_ref[...] = jnp.dot(
        jnp.concatenate(hits, axis=0), rows_ref[...], preferred_element_type=jnp.float32
    ).astype(jnp.bfloat16)


def pack_rows(slot, numbers, parts, total_slots, width):
    per_step = 6 * TILE
    tokens, half = parts[0].shape
    fixed = lambda i: (0, 0)
    one = pl.Buffered(1)
    return pl.pallas_call(
        pack_kernel,
        out_shape=pltpu.HBM((total_slots, width), jnp.bfloat16),
        grid=(total_slots // per_step,),
        in_specs=[pl.BlockSpec(slot.shape, fixed)] * 2
        + [pl.BlockSpec(numbers.shape, fixed)]
        + [pl.BlockSpec((tokens, half), fixed, pipeline_mode=one)] * 6,
        out_specs=pl.BlockSpec((per_step, width), lambda i: (i, 0)),
        scratch_shapes=[
            pltpu.VMEM((tokens, 2 * half), jnp.bfloat16),
            pltpu.VMEM((slot.shape[1], width), jnp.bfloat16),
        ],
        compiler_params=pltpu.CompilerParams(vmem_limit_bytes=26 * 1024 * 1024),
        name="pack_rows",
    )(slot // TILE, slot % TILE, numbers, *parts)


def adam_kernel(
    tile_ref, spot_ref, rows_ref, table_ref, first_ref, second_ref, new_table_ref, new_first_ref, new_second_ref
):
    steps = table_ref.shape[0] // TILE
    width = table_ref.shape[1]
    entries = rows_ref.shape[0]
    chunk = 1024
    place = lax.broadcasted_iota(jnp.int32, (TILE, chunk), 0).astype(jnp.bfloat16)
    one, zero = jnp.ones((), jnp.bfloat16), jnp.zeros((), jnp.bfloat16)
    for s in range(steps):
        here = pl.program_id(0) * steps + s
        grad = jnp.zeros((TILE, width), jnp.float32)
        for k in range(0, entries, chunk):
            spot = jnp.where(tile_ref[:, k : k + chunk] == here, spot_ref[:, k : k + chunk], -1)
            spot = jnp.broadcast_to(spot.astype(jnp.bfloat16), (TILE, chunk))
            hits = jnp.where(place == spot, one, zero)
            grad += jnp.dot(hits, rows_ref[k : k + chunk, :], preferred_element_type=jnp.float32)
        at = slice(s * TILE, (s + 1) * TILE)
        new_first = beta_one * first_ref[at, :] + (1.0 - beta_one) * grad
        new_second = beta_two * second_ref[at, :] + (1.0 - beta_two) * grad * grad
        stepped = new_first / correct_one / (jnp.sqrt(new_second / correct_two) + adam_eps)
        new_table_ref[at, :] = table_ref[at, :] - learn_rate * stepped
        new_first_ref[at, :] = new_first
        new_second_ref[at, :] = new_second


def adam_rows(got, embed_table, first_moment, second_moment):
    rows_dev, width = embed_table.shape
    per_step = 2 * TILE
    block = pl.BlockSpec((per_step, width), lambda i: (i, 0))
    tile = got[:, SLOT_CAP, :SLOTS].astype(jnp.int32).reshape(1, -1)
    spot = got[:, SLOT_CAP + 1, :SLOTS].astype(jnp.int32).reshape(1, -1)
    got_rows = got.reshape(-1, width)
    whole = pl.BlockSpec(tile.shape, lambda i: (0, 0))
    return pl.pallas_call(
        adam_kernel,
        out_shape=(jax.ShapeDtypeStruct((rows_dev, width), jnp.float32),) * 3,
        grid=(rows_dev // per_step,),
        in_specs=[
            whole,
            whole,
            pl.BlockSpec(got_rows.shape, lambda i: (0, 0)),
            block,
            block,
            block,
        ],
        out_specs=(block,) * 3,
        compiler_params=pltpu.CompilerParams(vmem_limit_bytes=26 * 1024 * 1024),
        name="adam_rows",
    )(tile, spot, got_rows, *in_hbm(embed_table, first_moment, second_moment))


def route(my_ids, owners, rows_dev, row_width):
    ids = my_ids.T
    lookups, tokens = ids.shape
    flat = ids.reshape(-1)
    entries = flat.shape[0]
    owner_of = flat // rows_dev
    local_row = flat % rows_dev
    owner_hits = (owner_of[:, None] == jnp.arange(owners, dtype=jnp.int32)[None, :]).astype(
        jnp.bfloat16
    )
    earlier = (jnp.arange(entries)[None, :] < jnp.arange(entries)[:, None]).astype(jnp.bfloat16)
    before_counts = jnp.dot(earlier, owner_hits, preferred_element_type=jnp.float32)
    slot_rank = jnp.sum(before_counts * owner_hits.astype(jnp.float32), axis=1).astype(jnp.int32)
    slot = owner_of * SLOTS + slot_rank
    rank_hits = slot_rank[:, None] == jnp.arange(SLOTS, dtype=jnp.int32)[None, :]
    low = local_row % TILE
    high = local_row // TILE
    values = jnp.concatenate(
        [
            jnp.where(rank_hits, v[:, None], 0).astype(jnp.bfloat16)
            for v in (high, low, jnp.ones_like(low))
        ],
        axis=1,
    )
    found = lax.dot_general(
        owner_hits, values, (((0,), (0,)), ((), ())), preferred_element_type=jnp.float32
    )
    got_high, got_low, filled = jnp.split(found, 3, axis=1)
    got_high = jnp.where(filled > 0, got_high, rows_dev // TILE)
    numbers = jnp.concatenate([got_high, got_low], axis=0).astype(jnp.bfloat16)
    numbers = jnp.pad(numbers, ((0, 0), (0, row_width - SLOTS)))
    owner = jnp.arange(owners, dtype=jnp.int32) * SLOTS
    number_slot = jnp.concatenate([owner + SLOT_CAP, owner + SLOT_CAP + 1])
    return (jnp.concatenate([slot.reshape(1, -1), number_slot[None, :]], axis=1), numbers)


def body(
    memory,
    hidden,
    grad_out,
    key_weight,
    value_weight,
    row_ids,
    embed_table,
    first_moment,
    second_moment,
):
    dp_count = lax.axis_size("dp")
    tensor_count = lax.axis_size("tensor")
    owners = dp_count * tensor_count
    rows_dev, row_width = embed_table.shape
    block_rows = memory.shape[0] // tensor_count
    my_ids = lax.dynamic_slice_in_dim(
        row_ids, lax.axis_index("tensor") * block_rows, block_rows, 0
    )
    at = lax.axis_index("dp")
    z = lax.axis_index("tensor")
    x, y, c = at // 8, (at // 2) % 4, at % 2
    slot, numbers = route(my_ids, owners, rows_dev, row_width)
    mine, slot, numbers = gather_weights(key_weight, value_weight, (slot, numbers))
    mine = mine.reshape(16, *mine.shape[2:])
    got = lax.ppermute(mine, "dp", other_core())
    spot = jnp.stack([x, y, c]).astype(jnp.int32)
    weights, key_proj, sums = project(spot, mine, got, memory, hidden, grad_out)
    sums = [sums] + [lax.ppermute(sums, "tensor", along_z(d)) for d in STEPS]
    far = ((z + 2) % 4)[None].astype(jnp.int32)
    near = jnp.stack([(z + 1) % 4, (z + 3) % 4, z, (z + 2) % 4]).astype(jnp.int32)
    _, far_left, far_right = grads(far, 1, sums, hidden, grad_out, key_proj, weights)
    up = lax.ppermute(far_left, "tensor", along_z(1))
    down = lax.ppermute(far_right, "tensor", along_z(3))
    both, next_left, next_right, last_left, last_right, own_left, own_right = grads(
        near, 3, sums, hidden, grad_out, key_proj, weights
    )
    from_last_right = lax.ppermute(next_right, "tensor", along_z(1))
    from_next_left = lax.ppermute(last_left, "tensor", along_z(3))
    next_left = (up.astype(jnp.float32) + next_left.astype(jnp.float32)).astype(jnp.bfloat16)
    last_right = (down.astype(jnp.float32) + last_right.astype(jnp.float32)).astype(jnp.bfloat16)
    both, next_left, last_right = lax.optimization_barrier((both, next_left, last_right))
    from_last_left = lax.ppermute(next_left, "tensor", along_z(1))
    from_next_right = lax.ppermute(last_right, "tensor", along_z(3))
    weight_grads = lax.dot_general(
        memory, both, (((0,), (0,)), ((), ())), preferred_element_type=jnp.float32
    ).astype(jnp.bfloat16)
    sent, kept = core_halves(weight_grads, c)
    sent, kept, from_last_right, from_next_left, from_last_left, from_next_right = (
        lax.optimization_barrier(
            (sent, kept, from_last_right, from_next_left, from_last_left, from_next_right)
        )
    )
    other = lax.ppermute(sent, "dp", other_core())
    send_rows = pack_rows(
        slot,
        numbers,
        (own_left, from_last_left, from_next_left, own_right, from_last_right, from_next_right),
        owners * SLOTS,
        row_width,
    )
    send_rows, other = lax.optimization_barrier((send_rows, other))
    chip_grads = sum_on_chip(other, kept, c)
    line_grads = ring_sum(chip_grads, jnp.where(c == 0, x, y), along_first).astype(jnp.bfloat16)
    pieces = ring_pieces(line_grads, jnp.where(c == 0, y, x), along_second)
    got_rows = lax.all_to_all(
        send_rows.reshape(owners, SLOTS, row_width),
        ("dp", "tensor"),
        split_axis=0,
        concat_axis=0,
        tiled=True,
    )
    new_table, new_first, new_second = adam_rows(
        got_rows, embed_table, first_moment, second_moment
    )
    pieces, new_second = lax.optimization_barrier((pieces, new_second))
    weight_sums = sum(p.astype(jnp.float32) for p in pieces)
    half = weight_sums.shape[1] // 2
    key_weight_grad = weight_sums[:, :half]
    value_weight_grad = weight_sums[:, half:]
    return (key_weight_grad, value_weight_grad, new_table, new_first, new_second)


def solution(mesh):
    return jax.shard_map(
        body,
        mesh=mesh,
        in_specs=(
            P("dp", None),
            P("dp", "tensor"),
            P("dp", "tensor"),
            P("dp", "tensor"),
            P("dp", "tensor"),
            P("dp", None),
            P(("dp", "tensor"), None),
            P(("dp", "tensor"), None),
            P(("dp", "tensor"), None),
        ),
        out_specs=(
            P("dp", "tensor"),
            P("dp", "tensor"),
            P(("dp", "tensor"), None),
            P(("dp", "tensor"), None),
            P(("dp", "tensor"), None),
        ),
        check_vma=False,
    )
```

```python
import functools
import math

import jax
import jax.numpy as jnp
from jax import lax
from jax.experimental import pallas as pl
from jax.experimental.pallas import tpu as pltpu
from jax.sharding import PartitionSpec as P

D = 2560


beta_one = 0.9
beta_two = 0.999
learn_rate = 0.01
adam_eps = 1e-08
norm_eps = 1e-06
correct_one = 0.9999734386011124
correct_two = 0.0952078528863


def dp_index(x, y, c):
    return (x % 4) * 8 + (y % 4) * 2 + c


def along_first(d):
    return [
        (dp_index(x, y, c), dp_index(x, y + d, c) if c else dp_index(x + d, y, c))
        for x in range(4)
        for y in range(4)
        for c in range(2)
    ]


def along_second(d):
    return [
        (dp_index(x, y, c), dp_index(x + d, y, c) if c else dp_index(x, y + d, c))
        for x in range(4)
        for y in range(4)
        for c in range(2)
    ]


def other_core():
    return [
        (dp_index(x, y, c), dp_index(x, y, 1 - c))
        for x in range(4)
        for y in range(4)
        for c in range(2)
    ]


def along_z(d):
    return [(z, (z + d) % 4) for z in range(4)]


STEPS = (2, 1, 3)
POSITION = (0, 2, 1, 3)


def in_hbm(*arrays):
    return tuple(pltpu.with_memory_space_constraint(a, pltpu.HBM) for a in arrays)


def ring_gather(shard, perm_of):
    return [shard] + [lax.ppermute(shard, "dp", perm_of(d)) for d in STEPS]


def ring_pieces(tiles, here, perm_of):
    own = lax.dynamic_index_in_dim(tiles, here, 0, keepdims=False)
    return [own] + [
        lax.ppermute(
            lax.dynamic_index_in_dim(tiles, (here + d) % 4, 0, keepdims=False), "dp", perm_of(d)
        )
        for d in STEPS
    ]


def ring_sum(tiles, here, perm_of):
    return sum(p.astype(jnp.float32) for p in ring_pieces(tiles, here, perm_of))


def gather_weights(key_weight, value_weight, routed):
    both = jnp.concatenate([key_weight, value_weight], axis=1)
    line = jnp.stack(ring_gather(both, along_first))
    line, routed = lax.optimization_barrier((line, routed))
    return (jnp.stack(ring_gather(line, along_second)), *routed)


def sum_on_chip(got, kept, c):
    both = (kept.astype(jnp.float32) + got.astype(jnp.float32)).astype(jnp.bfloat16)
    both = both.reshape(4, 4, *both.shape[1:])
    return jnp.where(c == 0, both, jnp.swapaxes(both, 0, 1))


def core_halves(weight_grads, c):
    tiles = weight_grads.reshape(16, 2, -1, weight_grads.shape[1])
    sent = lax.dynamic_index_in_dim(tiles, 1 - c, 1, keepdims=False)
    kept = lax.dynamic_index_in_dim(tiles, c, 1, keepdims=False)
    return (sent, kept)


def project_kernel(
    spot_ref, mine_ref, got_ref, memory_ref, hidden_ref, grad_ref, weight_ref, key_proj_ref, sums_ref
):
    half = hidden_ref.shape[1]

    def place(core):
        x, y = spot_ref[0], spot_ref[1]
        rows = mine_ref.shape[1]
        low_ref, high_ref = (got_ref, mine_ref) if core else (mine_ref, got_ref)
        for dx in range(4):
            for dy in range(4):
                low = low_ref[POSITION[dy] * 4 + POSITION[dx]].astype(jnp.float32)
                high = high_ref[POSITION[dx] * 4 + POSITION[dy]].astype(jnp.float32)
                at = ((x + 4 - dx) % 4) * 4 + (y + 4 - dy) % 4
                both = jnp.concatenate([low, high], axis=0).astype(jnp.bfloat16)
                weight_ref[pl.ds(pl.multiple_of(at * (2 * rows), 16), 2 * rows), :] = both

    for core in range(2):

        @pl.when((pl.program_id(0) == 0) & (spot_ref[2] == core))
        def _():
            place(core)

    memory = memory_ref[...]
    key_proj = jnp.dot(memory, weight_ref[:, :half], preferred_element_type=jnp.float32)
    value_proj = jnp.dot(memory, weight_ref[:, half:], preferred_element_type=jnp.float32)
    key_proj_ref[...] = key_proj
    hidden = hidden_ref[...].astype(jnp.float32)
    grad = grad_ref[...].astype(jnp.float32)
    square_sum = jnp.sum(key_proj * key_proj, axis=1, keepdims=True)
    cross_sum = jnp.sum(hidden * key_proj, axis=1, keepdims=True)
    output_sum = jnp.sum(grad * value_proj, axis=1, keepdims=True)
    lane = lax.broadcasted_iota(jnp.int32, (memory.shape[0], 128), 1)
    sums = jnp.where(lane == 0, square_sum, jnp.where(lane == 1, cross_sum, output_sum))
    sums_ref[...] = sums.T[:8, :]


def project(spot, mine, got, memory, hidden, grad_out):
    tokens, mem = memory.shape
    half = hidden.shape[1]
    tile = tokens // 4
    fixed = lambda i, s: (0, 0)
    return pl.pallas_call(
        project_kernel,
        out_shape=(
            jax.ShapeDtypeStruct((mem, 2 * half), jnp.bfloat16),
            pltpu.HBM((tokens, half), jnp.float32),
            jax.ShapeDtypeStruct((8, tokens), jnp.float32),
        ),
        grid_spec=pltpu.PrefetchScalarGridSpec(
            num_scalar_prefetch=1,
            grid=(4,),
            in_specs=[
                pl.BlockSpec(mine.shape, lambda i, s: (0, 0, 0), pipeline_mode=pl.Buffered(1)),
                pl.BlockSpec(got.shape, lambda i, s: (0, 0, 0), pipeline_mode=pl.Buffered(1)),
                pl.BlockSpec((tile, mem), lambda i, s: (i, 0)),
                pl.BlockSpec((tile, half), lambda i, s: (i, 0)),
                pl.BlockSpec((tile, half), lambda i, s: (i, 0)),
            ],
            out_specs=(
                pl.BlockSpec((mem, 2 * half), fixed, pipeline_mode=pl.Buffered(1)),
                pl.BlockSpec((tile, half), lambda i, s: (i, 0)),
                pl.BlockSpec((8, tile), lambda i, s: (0, i)),
            ),
        ),
        compiler_params=pltpu.CompilerParams(vmem_limit_bytes=30 * 1024 * 1024),
        name="project",
    )(spot, *in_hbm(mine, got, memory, hidden, grad_out))


def gates_of(sums_refs, hidden_ref, grad_ref, key_proj_ref, both_ref):
    half = hidden_ref.shape[1]
    sums = sums_refs[0][...] + sums_refs[1][...] + sums_refs[2][...] + sums_refs[3][...]
    root_width = math.sqrt(D)
    key_scale = jnp.sqrt(sums[0:1, :] / D + norm_eps)
    gate_score = sums[1:2, :] / (key_scale * root_width)
    gate_value = 1.0 / (1.0 + jnp.exp(-gate_score))
    gate_grad = gate_value * (1.0 - gate_value) * sums[2:3, :]
    by_hidden = 1.0 / (key_scale * root_width)
    by_key = gate_score / (D * key_scale * key_scale)
    row = lax.broadcasted_iota(jnp.int32, (128, sums.shape[1]), 0)
    coded = jnp.where(
        row == 0,
        gate_value,
        jnp.where(row == 1, gate_grad, jnp.where(row == 2, by_hidden, by_key)),
    ).T
    hidden = hidden_ref[...].astype(jnp.float32)
    key_grad = coded[:, 1:2] * (hidden * coded[:, 2:3] - key_proj_ref[...] * coded[:, 3:4])
    value_grad = coded[:, 0:1] * grad_ref[...].astype(jnp.float32)
    both_ref[:, :half] = key_grad.astype(jnp.bfloat16)
    both_ref[:, half:] = value_grad.astype(jnp.bfloat16)


def grads_kernel(order_ref, *refs):
    both_ref, outs = refs[8], refs[9:]
    half = outs[0].shape[1]
    gates_of(refs[:4], *refs[4:7], both_ref)

    @pl.when(pl.program_id(0) < len(outs) // 2)
    def _():
        memory_grad = lax.dot_general(
            both_ref[...],
            refs[7][...],
            (((1,), (1,)), ((), ())),
            preferred_element_type=jnp.float32,
        ).astype(jnp.bfloat16)
        for k in range(len(outs) // 2):

            @pl.when(pl.program_id(0) == k)
            def _():
                outs[2 * k][...] = memory_grad[:, :half]
                outs[2 * k + 1][...] = memory_grad[:, half:]


def grads(order, products, sums, hidden, grad_out, key_proj, weights):
    steps = order.shape[0]
    tokens, half = hidden.shape
    tile = tokens // 4
    mem = weights.shape[0]
    at = lambda i, o: (o[i], 0)
    fixed = lambda i, o: (0, 0)
    one = pl.Buffered(1)
    if steps == 1:
        both_shape, both_spec = (tile, 2 * half), pl.BlockSpec((tile, 2 * half), fixed)
    else:
        both_shape, both_spec = (tokens, 2 * half), pl.BlockSpec((tile, 2 * half), at)
    return pl.pallas_call(
        grads_kernel,
        out_shape=(
            pltpu.HBM(both_shape, jnp.bfloat16),
            *([jax.ShapeDtypeStruct((tile, mem // 2), jnp.bfloat16)] * (2 * products)),
        ),
        grid_spec=pltpu.PrefetchScalarGridSpec(
            num_scalar_prefetch=1,
            grid=(steps,),
            in_specs=[pl.BlockSpec((8, tile), lambda i, o: (0, o[i]))] * 4
            + [pl.BlockSpec((tile, half), at)] * 3
            + [pl.BlockSpec(weights.shape, fixed, pipeline_mode=one)],
            out_specs=(
                both_spec,
                *([pl.BlockSpec((tile, mem // 2), fixed, pipeline_mode=one)] * (2 * products)),
            ),
        ),
        compiler_params=pltpu.CompilerParams(vmem_limit_bytes=26 * 1024 * 1024),
        name="grads_far" if steps == 1 else "grads_near",
    )(order, *sums, *in_hbm(hidden, grad_out, key_proj), weights)


SLOTS = 48
SLOT_CAP = 45
TILE = 256


def pack_kernel(tile_ref, spot_ref, numbers_ref, l1, l2, l3, r1, r2, r3, out_ref, sum_ref, rows_ref):
    width = out_ref.shape[1]
    tokens, half = l1.shape
    entries = tile_ref.shape[1]
    lookups = 2 * half // width

    @pl.when(pl.program_id(0) == 0)
    def _():
        f32 = jnp.float32
        left = l1[...].astype(f32) + l2[...].astype(f32) + l3[...].astype(f32)
        right = r1[...].astype(f32) + r2[...].astype(f32) + r3[...].astype(f32)
        sum_ref[:, :half] = left.astype(jnp.bfloat16)
        sum_ref[:, half:] = right.astype(jnp.bfloat16)
        for l in range(lookups):
            rows_ref[l * tokens : (l + 1) * tokens, :] = sum_ref[:, l * width : (l + 1) * width]
        rows_ref[lookups * tokens :, :] = numbers_ref[...]

    steps = out_ref.shape[0] // TILE
    place = lax.broadcasted_iota(jnp.int32, (TILE, entries), 0).astype(jnp.bfloat16)
    one, zero = jnp.ones((), jnp.bfloat16), jnp.zeros((), jnp.bfloat16)
    hits = []
    for s in range(steps):
        here = pl.program_id(0) * steps + s
        spot = jnp.where(tile_ref[...] == here, spot_ref[...], -1)
        spot = jnp.broadcast_to(spot.astype(jnp.bfloat16), place.shape)
        hits.append(jnp.where(place == spot, one, zero))
    out_ref[...] = jnp.dot(
        jnp.concatenate(hits, axis=0), rows_ref[...], preferred_element_type=jnp.float32
    ).astype(jnp.bfloat16)


def pack_rows(slot, numbers, parts, total_slots, width):
    per_step = 6 * TILE
    tokens, half = parts[0].shape
    fixed = lambda i: (0, 0)
    one = pl.Buffered(1)
    return pl.pallas_call(
        pack_kernel,
        out_shape=pltpu.HBM((total_slots, width), jnp.bfloat16),
        grid=(total_slots // per_step,),
        in_specs=[pl.BlockSpec(slot.shape, fixed)] * 2
        + [pl.BlockSpec(numbers.shape, fixed)]
        + [pl.BlockSpec((tokens, half), fixed, pipeline_mode=one)] * 6,
        out_specs=pl.BlockSpec((per_step, width), lambda i: (i, 0)),
        scratch_shapes=[
            pltpu.VMEM((tokens, 2 * half), jnp.bfloat16),
            pltpu.VMEM((slot.shape[1], width), jnp.bfloat16),
        ],
        compiler_params=pltpu.CompilerParams(vmem_limit_bytes=26 * 1024 * 1024),
        name="pack_rows",
    )(slot // TILE, slot % TILE, numbers, *parts)


def adam_kernel(part, tile_ref, spot_ref, rows_ref, table_ref, first_ref, second_ref, *outs):
    new_table_ref, new_first_ref, new_second_ref = outs[-3:]
    steps = table_ref.shape[0] // TILE
    width = table_ref.shape[1]
    entries = rows_ref.shape[0]
    chunk = 1024
    place = lax.broadcasted_iota(jnp.int32, (TILE, chunk), 0).astype(jnp.bfloat16)
    one, zero = jnp.ones((), jnp.bfloat16), jnp.zeros((), jnp.bfloat16)
    for s in range(steps):
        here = (pl.program_id(0) + part * pl.num_programs(0)) * steps + s
        grad = jnp.zeros((TILE, width), jnp.float32)
        for k in range(0, entries, chunk):
            spot = jnp.where(tile_ref[:, k : k + chunk] == here, spot_ref[:, k : k + chunk], -1)
            spot = jnp.broadcast_to(spot.astype(jnp.bfloat16), (TILE, chunk))
            hits = jnp.where(place == spot, one, zero)
            grad += jnp.dot(hits, rows_ref[k : k + chunk, :], preferred_element_type=jnp.float32)
        at = slice(s * TILE, (s + 1) * TILE)
        new_first = beta_one * first_ref[at, :] + (1.0 - beta_one) * grad
        new_second = beta_two * second_ref[at, :] + (1.0 - beta_two) * grad * grad
        stepped = new_first / correct_one / (jnp.sqrt(new_second / correct_two) + adam_eps)
        new_table_ref[at, :] = table_ref[at, :] - learn_rate * stepped
        new_first_ref[at, :] = new_first
        new_second_ref[at, :] = new_second


def adam_rows(part, tile, spot, got_rows, tables, done):
    rows_dev, width = tables[0].shape
    per_step = 2 * TILE
    steps = rows_dev // per_step // 2
    block = pl.BlockSpec((per_step, width), lambda i: (i + part * steps, 0))
    whole = pl.BlockSpec(tile.shape, lambda i: (0, 0))
    return pl.pallas_call(
        functools.partial(adam_kernel, part),
        out_shape=(pltpu.HBM((rows_dev, width), jnp.float32),) * 3,
        grid=(steps,),
        in_specs=[
            whole,
            whole,
            pl.BlockSpec(got_rows.shape, lambda i: (0, 0)),
            block,
            block,
            block,
        ]
        + [pl.BlockSpec(memory_space=pl.ANY)] * len(done),
        out_specs=(block,) * 3,
        input_output_aliases={6: 0, 7: 1, 8: 2} if done else {},
        compiler_params=pltpu.CompilerParams(vmem_limit_bytes=26 * 1024 * 1024),
        name="adam_first" if part == 0 else "adam_second",
    )(tile, spot, got_rows, *in_hbm(*tables), *done)


def route(my_ids, owners, rows_dev, row_width):
    ids = my_ids.T
    lookups, tokens = ids.shape
    flat = ids.reshape(-1)
    entries = flat.shape[0]
    owner_of = flat // rows_dev
    local_row = flat % rows_dev
    owner_hits = (owner_of[:, None] == jnp.arange(owners, dtype=jnp.int32)[None, :]).astype(
        jnp.bfloat16
    )
    earlier = (jnp.arange(entries)[None, :] < jnp.arange(entries)[:, None]).astype(jnp.bfloat16)
    before_counts = jnp.dot(earlier, owner_hits, preferred_element_type=jnp.float32)
    slot_rank = jnp.sum(before_counts * owner_hits.astype(jnp.float32), axis=1).astype(jnp.int32)
    slot = owner_of * SLOTS + slot_rank
    rank_hits = slot_rank[:, None] == jnp.arange(SLOTS, dtype=jnp.int32)[None, :]
    low = local_row % TILE
    high = local_row // TILE
    values = jnp.concatenate(
        [
            jnp.where(rank_hits, v[:, None], 0).astype(jnp.bfloat16)
            for v in (high, low, jnp.ones_like(low))
        ],
        axis=1,
    )
    found = lax.dot_general(
        owner_hits, values, (((0,), (0,)), ((), ())), preferred_element_type=jnp.float32
    )
    got_high, got_low, filled = jnp.split(found, 3, axis=1)
    got_high = jnp.where(filled > 0, got_high, rows_dev // TILE)
    numbers = jnp.concatenate([got_high, got_low], axis=0).astype(jnp.bfloat16)
    numbers = jnp.pad(numbers, ((0, 0), (0, row_width - SLOTS)))
    owner = jnp.arange(owners, dtype=jnp.int32) * SLOTS
    number_slot = jnp.concatenate([owner + SLOT_CAP, owner + SLOT_CAP + 1])
    return (jnp.concatenate([slot.reshape(1, -1), number_slot[None, :]], axis=1), numbers)


def body(
    memory,
    hidden,
    grad_out,
    key_weight,
    value_weight,
    row_ids,
    embed_table,
    first_moment,
    second_moment,
):
    dp_count = lax.axis_size("dp")
    tensor_count = lax.axis_size("tensor")
    owners = dp_count * tensor_count
    rows_dev, row_width = embed_table.shape
    block_rows = memory.shape[0] // tensor_count
    my_ids = lax.dynamic_slice_in_dim(
        row_ids, lax.axis_index("tensor") * block_rows, block_rows, 0
    )
    at = lax.axis_index("dp")
    z = lax.axis_index("tensor")
    x, y, c = at // 8, (at // 2) % 4, at % 2
    slot, numbers = route(my_ids, owners, rows_dev, row_width)
    mine, slot, numbers = gather_weights(key_weight, value_weight, (slot, numbers))
    mine = mine.reshape(16, *mine.shape[2:])
    got = lax.ppermute(mine, "dp", other_core())
    spot = jnp.stack([x, y, c]).astype(jnp.int32)
    weights, key_proj, sums = project(spot, mine, got, memory, hidden, grad_out)
    sums = [sums] + [lax.ppermute(sums, "tensor", along_z(d)) for d in STEPS]
    far = ((z + 2) % 4)[None].astype(jnp.int32)
    near = jnp.stack([(z + 1) % 4, (z + 3) % 4, z, (z + 2) % 4]).astype(jnp.int32)
    _, far_left, far_right = grads(far, 1, sums, hidden, grad_out, key_proj, weights)
    up = lax.ppermute(far_left, "tensor", along_z(1))
    down = lax.ppermute(far_right, "tensor", along_z(3))
    both, next_left, next_right, last_left, last_right, own_left, own_right = grads(
        near, 3, sums, hidden, grad_out, key_proj, weights
    )
    from_last_right = lax.ppermute(next_right, "tensor", along_z(1))
    from_next_left = lax.ppermute(last_left, "tensor", along_z(3))
    next_left = (up.astype(jnp.float32) + next_left.astype(jnp.float32)).astype(jnp.bfloat16)
    last_right = (down.astype(jnp.float32) + last_right.astype(jnp.float32)).astype(jnp.bfloat16)
    both, next_left, last_right = lax.optimization_barrier((both, next_left, last_right))
    from_last_left = lax.ppermute(next_left, "tensor", along_z(1))
    from_next_right = lax.ppermute(last_right, "tensor", along_z(3))
    weight_grads = lax.dot_general(
        memory, both, (((0,), (0,)), ((), ())), preferred_element_type=jnp.float32
    ).astype(jnp.bfloat16)
    sent, kept = core_halves(weight_grads, c)
    sent, kept, from_last_right, from_next_left, from_last_left, from_next_right = (
        lax.optimization_barrier(
            (sent, kept, from_last_right, from_next_left, from_last_left, from_next_right)
        )
    )
    other = lax.ppermute(sent, "dp", other_core())
    send_rows = pack_rows(
        slot,
        numbers,
        (own_left, from_last_left, from_next_left, own_right, from_last_right, from_next_right),
        owners * SLOTS,
        row_width,
    )
    send_rows, other = lax.optimization_barrier((send_rows, other))
    chip_grads = sum_on_chip(other, kept, c)
    line_pieces = ring_pieces(chip_grads, jnp.where(c == 0, x, y), along_first)
    got = lax.all_to_all(
        send_rows.reshape(owners, SLOTS, row_width),
        ("dp", "tensor"),
        split_axis=0,
        concat_axis=0,
        tiled=True,
    )
    tile = got[:, SLOT_CAP, :SLOTS].astype(jnp.int32).reshape(1, -1)
    spot_row = got[:, SLOT_CAP + 1, :SLOTS].astype(jnp.int32).reshape(1, -1)
    got_rows = got.reshape(-1, row_width)
    tables = (embed_table, first_moment, second_moment)
    done = adam_rows(0, tile, spot_row, got_rows, tables, ())
    line_pieces, done = lax.optimization_barrier((line_pieces, tuple(done)))
    line_grads = sum(p.astype(jnp.float32) for p in line_pieces).astype(jnp.bfloat16)
    line_grads, tile = lax.optimization_barrier((line_grads, tile))
    pieces = ring_pieces(line_grads, jnp.where(c == 0, y, x), along_second)
    new_table, new_first, new_second = adam_rows(1, tile, spot_row, got_rows, tables, done)
    pieces, new_second = lax.optimization_barrier((pieces, new_second))
    weight_sums = sum(p.astype(jnp.float32) for p in pieces)
    half = weight_sums.shape[1] // 2
    key_weight_grad = weight_sums[:, :half]
    value_weight_grad = weight_sums[:, half:]
    return (key_weight_grad, value_weight_grad, new_table, new_first, new_second)


def solution(mesh):
    return jax.shard_map(
        body,
        mesh=mesh,
        in_specs=(
            P("dp", None),
            P("dp", "tensor"),
            P("dp", "tensor"),
            P("dp", "tensor"),
            P("dp", "tensor"),
            P("dp", None),
            P(("dp", "tensor"), None),
            P(("dp", "tensor"), None),
            P(("dp", "tensor"), None),
        ),
        out_specs=(
            P("dp", "tensor"),
            P("dp", "tensor"),
            P(("dp", "tensor"), None),
            P(("dp", "tensor"), None),
            P(("dp", "tensor"), None),
        ),
        check_vma=False,
    )
```

```python
import functools
import math

import jax
import jax.numpy as jnp
from jax import lax
from jax.experimental import pallas as pl
from jax.experimental.pallas import tpu as pltpu
from jax.sharding import PartitionSpec as P

D = 2560


beta_one = 0.9
beta_two = 0.999
learn_rate = 0.01
adam_eps = 1e-08
norm_eps = 1e-06
correct_one = 0.9999734386011124
correct_two = 0.0952078528863


def dp_index(x, y, c):
    return (x % 4) * 8 + (y % 4) * 2 + c


def along_first(d):
    return [
        (dp_index(x, y, c), dp_index(x, y + d, c) if c else dp_index(x + d, y, c))
        for x in range(4)
        for y in range(4)
        for c in range(2)
    ]


def along_second(d):
    return [
        (dp_index(x, y, c), dp_index(x + d, y, c) if c else dp_index(x, y + d, c))
        for x in range(4)
        for y in range(4)
        for c in range(2)
    ]


def other_core():
    return [
        (dp_index(x, y, c), dp_index(x, y, 1 - c))
        for x in range(4)
        for y in range(4)
        for c in range(2)
    ]


def along_z(d):
    return [(z, (z + d) % 4) for z in range(4)]


STEPS = (2, 1, 3)
POSITION = (0, 2, 1, 3)


def in_hbm(*arrays):
    return tuple(pltpu.with_memory_space_constraint(a, pltpu.HBM) for a in arrays)


def ring_gather(shard, perm_of):
    return [shard] + [lax.ppermute(shard, "dp", perm_of(d)) for d in STEPS]


def ring_pieces(tiles, here, perm_of):
    own = lax.dynamic_index_in_dim(tiles, here, 0, keepdims=False)
    return [own] + [
        lax.ppermute(
            lax.dynamic_index_in_dim(tiles, (here + d) % 4, 0, keepdims=False), "dp", perm_of(d)
        )
        for d in STEPS
    ]


def ring_sum(tiles, here, perm_of):
    return sum(p.astype(jnp.float32) for p in ring_pieces(tiles, here, perm_of))


def gather_weights(key_weight, value_weight, routed):
    both = jnp.concatenate([key_weight, value_weight], axis=1)
    line = jnp.stack(ring_gather(both, along_first))
    line, routed = lax.optimization_barrier((line, routed))
    return (jnp.stack(ring_gather(line, along_second)), *routed)


def sum_on_chip(got, kept, c):
    both = (kept.astype(jnp.float32) + got.astype(jnp.float32)).astype(jnp.bfloat16)
    both = both.reshape(4, 4, *both.shape[1:])
    return jnp.where(c == 0, both, jnp.swapaxes(both, 0, 1))


def core_halves(weight_grads, c):
    tiles = weight_grads.reshape(16, 2, -1, weight_grads.shape[1])
    sent = lax.dynamic_index_in_dim(tiles, 1 - c, 1, keepdims=False)
    kept = lax.dynamic_index_in_dim(tiles, c, 1, keepdims=False)
    return (sent, kept)


def project_kernel(
    spot_ref, mine_ref, got_ref, memory_ref, hidden_ref, grad_ref, weight_ref, key_proj_ref, sums_ref
):
    half = hidden_ref.shape[1]

    def place(core):
        x, y = spot_ref[0], spot_ref[1]
        rows = mine_ref.shape[1]
        low_ref, high_ref = (got_ref, mine_ref) if core else (mine_ref, got_ref)
        for dx in range(4):
            for dy in range(4):
                low = low_ref[POSITION[dy] * 4 + POSITION[dx]].astype(jnp.float32)
                high = high_ref[POSITION[dx] * 4 + POSITION[dy]].astype(jnp.float32)
                at = ((x + 4 - dx) % 4) * 4 + (y + 4 - dy) % 4
                both = jnp.concatenate([low, high], axis=0).astype(jnp.bfloat16)
                weight_ref[pl.ds(pl.multiple_of(at * (2 * rows), 16), 2 * rows), :] = both

    for core in range(2):

        @pl.when((pl.program_id(0) == 0) & (spot_ref[2] == core))
        def _():
            place(core)

    memory = memory_ref[...]
    key_proj = jnp.dot(memory, weight_ref[:, :half], preferred_element_type=jnp.float32)
    value_proj = jnp.dot(memory, weight_ref[:, half:], preferred_element_type=jnp.float32)
    key_proj_ref[...] = key_proj
    hidden = hidden_ref[...].astype(jnp.float32)
    grad = grad_ref[...].astype(jnp.float32)
    square_sum = jnp.sum(key_proj * key_proj, axis=1, keepdims=True)
    cross_sum = jnp.sum(hidden * key_proj, axis=1, keepdims=True)
    output_sum = jnp.sum(grad * value_proj, axis=1, keepdims=True)
    lane = lax.broadcasted_iota(jnp.int32, (memory.shape[0], 128), 1)
    sums = jnp.where(lane == 0, square_sum, jnp.where(lane == 1, cross_sum, output_sum))
    sums_ref[...] = sums.T[:8, :]


def project(spot, mine, got, memory, hidden, grad_out):
    tokens, mem = memory.shape
    half = hidden.shape[1]
    tile = tokens // 4
    fixed = lambda i, s: (0, 0)
    return pl.pallas_call(
        project_kernel,
        out_shape=(
            jax.ShapeDtypeStruct((mem, 2 * half), jnp.bfloat16),
            pltpu.HBM((tokens, half), jnp.float32),
            jax.ShapeDtypeStruct((8, tokens), jnp.float32),
        ),
        grid_spec=pltpu.PrefetchScalarGridSpec(
            num_scalar_prefetch=1,
            grid=(4,),
            in_specs=[
                pl.BlockSpec(mine.shape, lambda i, s: (0, 0, 0), pipeline_mode=pl.Buffered(1)),
                pl.BlockSpec(got.shape, lambda i, s: (0, 0, 0), pipeline_mode=pl.Buffered(1)),
                pl.BlockSpec((tile, mem), lambda i, s: (i, 0)),
                pl.BlockSpec((tile, half), lambda i, s: (i, 0)),
                pl.BlockSpec((tile, half), lambda i, s: (i, 0)),
            ],
            out_specs=(
                pl.BlockSpec((mem, 2 * half), fixed, pipeline_mode=pl.Buffered(1)),
                pl.BlockSpec((tile, half), lambda i, s: (i, 0)),
                pl.BlockSpec((8, tile), lambda i, s: (0, i)),
            ),
        ),
        compiler_params=pltpu.CompilerParams(vmem_limit_bytes=30 * 1024 * 1024),
        name="project",
    )(spot, *in_hbm(mine, got, memory, hidden, grad_out))


def gates_of(sums_refs, hidden_ref, grad_ref, key_proj_ref, both_ref):
    half = hidden_ref.shape[1]
    sums = sums_refs[0][...] + sums_refs[1][...] + sums_refs[2][...] + sums_refs[3][...]
    root_width = math.sqrt(D)
    key_scale = jnp.sqrt(sums[0:1, :] / D + norm_eps)
    gate_score = sums[1:2, :] / (key_scale * root_width)
    gate_value = 1.0 / (1.0 + jnp.exp(-gate_score))
    gate_grad = gate_value * (1.0 - gate_value) * sums[2:3, :]
    by_hidden = 1.0 / (key_scale * root_width)
    by_key = gate_score / (D * key_scale * key_scale)
    row = lax.broadcasted_iota(jnp.int32, (128, sums.shape[1]), 0)
    coded = jnp.where(
        row == 0,
        gate_value,
        jnp.where(row == 1, gate_grad, jnp.where(row == 2, by_hidden, by_key)),
    ).T
    hidden = hidden_ref[...].astype(jnp.float32)
    key_grad = coded[:, 1:2] * (hidden * coded[:, 2:3] - key_proj_ref[...] * coded[:, 3:4])
    value_grad = coded[:, 0:1] * grad_ref[...].astype(jnp.float32)
    both_ref[:, :half] = key_grad.astype(jnp.bfloat16)
    both_ref[:, half:] = value_grad.astype(jnp.bfloat16)


def grads_kernel(order_ref, *refs):
    both_ref, outs = refs[8], refs[9:]
    half = outs[0].shape[1]
    gates_of(refs[:4], *refs[4:7], both_ref)

    @pl.when(pl.program_id(0) < len(outs) // 2)
    def _():
        memory_grad = lax.dot_general(
            both_ref[...],
            refs[7][...],
            (((1,), (1,)), ((), ())),
            preferred_element_type=jnp.float32,
        ).astype(jnp.bfloat16)
        for k in range(len(outs) // 2):

            @pl.when(pl.program_id(0) == k)
            def _():
                outs[2 * k][...] = memory_grad[:, :half]
                outs[2 * k + 1][...] = memory_grad[:, half:]


def grads(order, products, sums, hidden, grad_out, key_proj, weights):
    steps = order.shape[0]
    tokens, half = hidden.shape
    tile = tokens // 4
    mem = weights.shape[0]
    at = lambda i, o: (o[i], 0)
    fixed = lambda i, o: (0, 0)
    one = pl.Buffered(1)
    if steps == 1:
        both_shape, both_spec = (tile, 2 * half), pl.BlockSpec((tile, 2 * half), fixed)
    else:
        both_shape, both_spec = (tokens, 2 * half), pl.BlockSpec((tile, 2 * half), at)
    return pl.pallas_call(
        grads_kernel,
        out_shape=(
            pltpu.HBM(both_shape, jnp.bfloat16),
            *([jax.ShapeDtypeStruct((tile, mem // 2), jnp.bfloat16)] * (2 * products)),
        ),
        grid_spec=pltpu.PrefetchScalarGridSpec(
            num_scalar_prefetch=1,
            grid=(steps,),
            in_specs=[pl.BlockSpec((8, tile), lambda i, o: (0, o[i]))] * 4
            + [pl.BlockSpec((tile, half), at)] * 3
            + [pl.BlockSpec(weights.shape, fixed, pipeline_mode=one)],
            out_specs=(
                both_spec,
                *([pl.BlockSpec((tile, mem // 2), fixed, pipeline_mode=one)] * (2 * products)),
            ),
        ),
        compiler_params=pltpu.CompilerParams(vmem_limit_bytes=26 * 1024 * 1024),
        name="grads_far" if steps == 1 else "grads_near",
    )(order, *sums, *in_hbm(hidden, grad_out, key_proj), weights)


SLOTS = 48
SLOT_CAP = 45
TILE = 256


def pack_kernel(tile_ref, spot_ref, numbers_ref, l1, l2, l3, r1, r2, r3, out_ref, sum_ref, rows_ref):
    width = out_ref.shape[1]
    tokens, half = l1.shape
    entries = tile_ref.shape[1]
    lookups = 2 * half // width

    @pl.when(pl.program_id(0) == 0)
    def _():
        f32 = jnp.float32
        left = l1[...].astype(f32) + l2[...].astype(f32) + l3[...].astype(f32)
        right = r1[...].astype(f32) + r2[...].astype(f32) + r3[...].astype(f32)
        sum_ref[:, :half] = left.astype(jnp.bfloat16)
        sum_ref[:, half:] = right.astype(jnp.bfloat16)
        for l in range(lookups):
            rows_ref[l * tokens : (l + 1) * tokens, :] = sum_ref[:, l * width : (l + 1) * width]
        rows_ref[lookups * tokens :, :] = numbers_ref[...]

    steps = out_ref.shape[0] // TILE
    place = lax.broadcasted_iota(jnp.int32, (TILE, entries), 0).astype(jnp.bfloat16)
    one, zero = jnp.ones((), jnp.bfloat16), jnp.zeros((), jnp.bfloat16)
    hits = []
    for s in range(steps):
        here = pl.program_id(0) * steps + s
        spot = jnp.where(tile_ref[...] == here, spot_ref[...], -1)
        spot = jnp.broadcast_to(spot.astype(jnp.bfloat16), place.shape)
        hits.append(jnp.where(place == spot, one, zero))
    out_ref[...] = jnp.dot(
        jnp.concatenate(hits, axis=0), rows_ref[...], preferred_element_type=jnp.float32
    ).astype(jnp.bfloat16)


def pack_rows(slot, numbers, parts, total_slots, width):
    per_step = 6 * TILE
    tokens, half = parts[0].shape
    fixed = lambda i: (0, 0)
    one = pl.Buffered(1)
    return pl.pallas_call(
        pack_kernel,
        out_shape=pltpu.HBM((total_slots, width), jnp.bfloat16),
        grid=(total_slots // per_step,),
        in_specs=[pl.BlockSpec(slot.shape, fixed)] * 2
        + [pl.BlockSpec(numbers.shape, fixed)]
        + [pl.BlockSpec((tokens, half), fixed, pipeline_mode=one)] * 6,
        out_specs=pl.BlockSpec((per_step, width), lambda i: (i, 0)),
        scratch_shapes=[
            pltpu.VMEM((tokens, 2 * half), jnp.bfloat16),
            pltpu.VMEM((slot.shape[1], width), jnp.bfloat16),
        ],
        compiler_params=pltpu.CompilerParams(vmem_limit_bytes=26 * 1024 * 1024),
        name="pack_rows",
    )(slot // TILE, slot % TILE, numbers, *parts)


def adam_kernel(part, tile_ref, spot_ref, rows_ref, table_ref, first_ref, second_ref, *outs):
    new_table_ref, new_first_ref, new_second_ref = outs[-3:]
    steps = table_ref.shape[0] // TILE
    width = table_ref.shape[1]
    entries = rows_ref.shape[0]
    chunk = 1024
    place = lax.broadcasted_iota(jnp.int32, (TILE, chunk), 0).astype(jnp.bfloat16)
    one, zero = jnp.ones((), jnp.bfloat16), jnp.zeros((), jnp.bfloat16)
    for s in range(steps):
        here = (pl.program_id(0) + part * pl.num_programs(0)) * steps + s
        grad = jnp.zeros((TILE, width), jnp.float32)
        for k in range(0, entries, chunk):
            spot = jnp.where(tile_ref[:, k : k + chunk] == here, spot_ref[:, k : k + chunk], -1)
            spot = jnp.broadcast_to(spot.astype(jnp.bfloat16), (TILE, chunk))
            hits = jnp.where(place == spot, one, zero)
            grad += jnp.dot(hits, rows_ref[k : k + chunk, :], preferred_element_type=jnp.float32)
        at = slice(s * TILE, (s + 1) * TILE)
        new_first = beta_one * first_ref[at, :] + (1.0 - beta_one) * grad
        new_second = beta_two * second_ref[at, :] + (1.0 - beta_two) * grad * grad
        stepped = new_first / correct_one / (jnp.sqrt(new_second / correct_two) + adam_eps)
        new_table_ref[at, :] = table_ref[at, :] - learn_rate * stepped
        new_first_ref[at, :] = new_first
        new_second_ref[at, :] = new_second


def adam_rows(part, tile, spot, got_rows, tables, done):
    rows_dev, width = tables[0].shape
    per_step = 2 * TILE
    steps = rows_dev // per_step // 2
    block = pl.BlockSpec((per_step, width), lambda i: (i + part * steps, 0))
    whole = pl.BlockSpec(tile.shape, lambda i: (0, 0))
    return pl.pallas_call(
        functools.partial(adam_kernel, part),
        out_shape=(pltpu.HBM((rows_dev, width), jnp.float32),) * 3,
        grid=(steps,),
        in_specs=[
            whole,
            whole,
            pl.BlockSpec(got_rows.shape, lambda i: (0, 0)),
            block,
            block,
            block,
        ]
        + [pl.BlockSpec(memory_space=pl.ANY)] * len(done),
        out_specs=(block,) * 3,
        input_output_aliases={6: 0, 7: 1, 8: 2} if done else {},
        compiler_params=pltpu.CompilerParams(vmem_limit_bytes=26 * 1024 * 1024),
        name="adam_first" if part == 0 else "adam_second",
    )(tile, spot, got_rows, *in_hbm(*tables), *done)


def route(my_ids, owners, rows_dev, row_width):
    ids = my_ids.T
    lookups, tokens = ids.shape
    flat = ids.reshape(-1)
    entries = flat.shape[0]
    owner_of = flat // rows_dev
    local_row = flat % rows_dev
    owner_hits = (owner_of[:, None] == jnp.arange(owners, dtype=jnp.int32)[None, :]).astype(
        jnp.bfloat16
    )
    earlier = (jnp.arange(entries)[None, :] < jnp.arange(entries)[:, None]).astype(jnp.bfloat16)
    before_counts = jnp.dot(earlier, owner_hits, preferred_element_type=jnp.float32)
    slot_rank = jnp.sum(before_counts * owner_hits.astype(jnp.float32), axis=1).astype(jnp.int32)
    slot = owner_of * SLOTS + slot_rank
    rank_hits = slot_rank[:, None] == jnp.arange(SLOTS, dtype=jnp.int32)[None, :]
    low = local_row % TILE
    high = local_row // TILE
    values = jnp.concatenate(
        [
            jnp.where(rank_hits, v[:, None], 0).astype(jnp.bfloat16)
            for v in (high, low, jnp.ones_like(low))
        ],
        axis=1,
    )
    found = lax.dot_general(
        owner_hits, values, (((0,), (0,)), ((), ())), preferred_element_type=jnp.float32
    )
    got_high, got_low, filled = jnp.split(found, 3, axis=1)
    got_high = jnp.where(filled > 0, got_high, rows_dev // TILE)
    numbers = jnp.concatenate([got_high, got_low], axis=0).astype(jnp.bfloat16)
    numbers = jnp.pad(numbers, ((0, 0), (0, row_width - SLOTS)))
    owner = jnp.arange(owners, dtype=jnp.int32) * SLOTS
    number_slot = jnp.concatenate([owner + SLOT_CAP, owner + SLOT_CAP + 1])
    return (jnp.concatenate([slot.reshape(1, -1), number_slot[None, :]], axis=1), numbers)


def body(
    memory,
    hidden,
    grad_out,
    key_weight,
    value_weight,
    row_ids,
    embed_table,
    first_moment,
    second_moment,
):
    dp_count = lax.axis_size("dp")
    tensor_count = lax.axis_size("tensor")
    owners = dp_count * tensor_count
    rows_dev, row_width = embed_table.shape
    block_rows = memory.shape[0] // tensor_count
    my_ids = lax.dynamic_slice_in_dim(
        row_ids, lax.axis_index("tensor") * block_rows, block_rows, 0
    )
    at = lax.axis_index("dp")
    z = lax.axis_index("tensor")
    x, y, c = at // 8, (at // 2) % 4, at % 2
    slot, numbers = route(my_ids, owners, rows_dev, row_width)
    mine, slot, numbers = gather_weights(key_weight, value_weight, (slot, numbers))
    mine = mine.reshape(16, *mine.shape[2:])
    got = lax.ppermute(mine, "dp", other_core())
    spot = jnp.stack([x, y, c]).astype(jnp.int32)
    weights, key_proj, sums = project(spot, mine, got, memory, hidden, grad_out)
    sums = [sums] + [lax.ppermute(sums, "tensor", along_z(d)) for d in STEPS]
    far = ((z + 2) % 4)[None].astype(jnp.int32)
    near = jnp.stack([(z + 1) % 4, (z + 3) % 4, z, (z + 2) % 4]).astype(jnp.int32)
    _, far_left, far_right = grads(far, 1, sums, hidden, grad_out, key_proj, weights)
    up = lax.ppermute(far_left, "tensor", along_z(1))
    down = lax.ppermute(far_right, "tensor", along_z(3))
    both, next_left, next_right, last_left, last_right, own_left, own_right = grads(
        near, 3, sums, hidden, grad_out, key_proj, weights
    )
    from_last_right = lax.ppermute(next_right, "tensor", along_z(1))
    from_next_left = lax.ppermute(last_left, "tensor", along_z(3))
    next_left = (up.astype(jnp.float32) + next_left.astype(jnp.float32)).astype(jnp.bfloat16)
    last_right = (down.astype(jnp.float32) + last_right.astype(jnp.float32)).astype(jnp.bfloat16)
    both, next_left, last_right = lax.optimization_barrier((both, next_left, last_right))
    from_last_left = lax.ppermute(next_left, "tensor", along_z(1))
    from_next_right = lax.ppermute(last_right, "tensor", along_z(3))
    weight_grads = lax.dot_general(
        memory, both, (((0,), (0,)), ((), ())), preferred_element_type=jnp.float32
    ).astype(jnp.bfloat16)
    sent, kept = core_halves(weight_grads, c)
    sent, kept, from_last_right, from_next_left, from_last_left, from_next_right = (
        lax.optimization_barrier(
            (sent, kept, from_last_right, from_next_left, from_last_left, from_next_right)
        )
    )
    other = lax.ppermute(sent, "dp", other_core())
    send_rows = pack_rows(
        slot,
        numbers,
        (own_left, from_last_left, from_next_left, own_right, from_last_right, from_next_right),
        owners * SLOTS,
        row_width,
    )
    send_rows, other = lax.optimization_barrier((send_rows, other))
    chip_grads = sum_on_chip(other, kept, c)
    line_pieces = ring_pieces(chip_grads, jnp.where(c == 0, x, y), along_first)
    got = lax.all_to_all(
        send_rows.reshape(owners, SLOTS, row_width),
        ("dp", "tensor"),
        split_axis=0,
        concat_axis=0,
        tiled=True,
    )
    tile = got[:, SLOT_CAP, :SLOTS].astype(jnp.int32).reshape(1, -1)
    spot_row = got[:, SLOT_CAP + 1, :SLOTS].astype(jnp.int32).reshape(1, -1)
    got_rows = got.reshape(-1, row_width)
    tables = (embed_table, first_moment, second_moment)
    done = adam_rows(0, tile, spot_row, got_rows, tables, ())
    line_pieces, done = lax.optimization_barrier((line_pieces, tuple(done)))
    line_grads = sum(p.astype(jnp.float32) for p in line_pieces).astype(jnp.bfloat16)
    line_grads, tile = lax.optimization_barrier((line_grads, tile))
    pieces = ring_pieces(line_grads, jnp.where(c == 0, y, x), along_second)
    new_table, new_first, new_second = adam_rows(1, tile, spot_row, got_rows, tables, done)
    pieces, new_second = lax.optimization_barrier((pieces, new_second))
    half = pieces[0].shape[1] // 2
    key_weight_grad = sum(p[:, :half].astype(jnp.float32) for p in pieces)
    value_weight_grad = sum(p[:, half:].astype(jnp.float32) for p in pieces)
    return (key_weight_grad, value_weight_grad, new_table, new_first, new_second)


def solution(mesh):
    return jax.shard_map(
        body,
        mesh=mesh,
        in_specs=(
            P("dp", None),
            P("dp", "tensor"),
            P("dp", "tensor"),
            P("dp", "tensor"),
            P("dp", "tensor"),
            P("dp", None),
            P(("dp", "tensor"), None),
            P(("dp", "tensor"), None),
            P(("dp", "tensor"), None),
        ),
        out_specs=(
            P("dp", "tensor"),
            P("dp", "tensor"),
            P(("dp", "tensor"), None),
            P(("dp", "tensor"), None),
            P(("dp", "tensor"), None),
        ),
        check_vma=False,
    )
```
